32 devices in a mesh: dp: 8 (over z, x), tensor: 4 (over y, core).
Axes of the slice: x: 2, y: 2, z: 4, core: 2. Of those that a mesh axis runs over, the one named last changes fastest.
Arguments:
- hidden_in: bfloat16 [6144, 1536], P(('dp', 'tensor')), may hold values from -6 to 6
- attn_gain: bfloat16 [1536], P('dp'), may hold values from 0.5 to 1.5
- query_proj: bfloat16 [1536, 1536], P('dp', 'tensor'), may hold values from -0.3125 to 0.3125
- key_value_projection: bfloat16 [1536, 2, 512], P('dp', None, 'tensor'), may hold values from -0.15625 to 0.15625
- output_proj: bfloat16 [1536, 1536], P('tensor', 'dp'), may hold values from -2.5 to 2.5
- moe_gain: bfloat16 [1536], P('dp'), may hold values from 0.5 to 1.5
- router_proj: bfloat16 [1536, 8], P('dp'), may hold values from -0.106933594 to 0.106933594
- gateup_proj: bfloat16 [8, 1536, 2, 1024], P(None, 'dp', None, 'tensor'), may hold values from -0.15625 to 0.15625
- down_proj: bfloat16 [8, 1024, 1536], P(None, 'tensor', 'dp'), may hold values from -0.375 to 0.375
- segment_index_list: int32 [6144], replicated, may hold values from 0 to 11, never falling along the last dimension, each value on 1 to 1536 neighbouring positions
- expert_ids: int32 [6144, 2], P('dp'), may hold values from 0 to 7, all different within a row
- out_grad: bfloat16 [6144, 1536], P(('dp', 'tensor')), may hold values from -6 to 6
Outputs:
- hidden_out: bfloat16 [6144, 1536], P(('dp', 'tensor'))
- input_grad: float32 [6144, 1536], P(('dp', 'tensor'))
- attn_gain_grad: float32 [1536], P('dp')
- query_grad: float32 [1536, 1536], P('dp', 'tensor')
- keyval_grad: float32 [1536, 2, 512], P('dp', None, 'tensor')
- output_grad: float32 [1536, 1536], P('tensor', 'dp')
- moe_gain_grad: float32 [1536], P('dp')
- router_grad: float32 [1536, 8], P('dp')
- gateup_grad: float32 [8, 1536, 2, 1024], P(None, 'dp', None, 'tensor')
- down_grad: float32 [8, 1024, 1536], P(None, 'tensor', 'dp')
The draws below stay inside these ranges and needn't reach their ends.
Inputs may be any that keep to these rules, and one draw needn't show every extreme that they name: `segment_index_list`: segment numbers never fall along the tokens. `expert_ids`: each token names two different experts, its first choice in column 0.
All inputs are finite; a program needn't handle non-finite values.
Results may differ from the reference program's by a relative error of at most 0.03.
Values may be sent and summed in bfloat16 or wider, within the bound.
No kernel may reach another device: no remote copies, remote signals or barrier semaphores. Data moves between devices by JAX's collectives and lax.ppermute only.
A program may use at most 256 MiB of HBM per device.

```python
import math
import jax
import jax.numpy as jnp
import numpy as np
from jax import lax

MODEL_WIDTH = 1536
QUERY_HEADS_COUNT = 24
KEY_VALUE_HEADS = 8
HEAD_SIZE = 64
FF = 1024
E = 8
CH = 768
CAP = 240
SEQUENCE_LENGTH = 6144
TOKENS = 6144
N_DP = 8


def block_scale(stream_key, dims, shards, smallest, top_value):
    def one(dim, blocks):
        heights = jax.random.uniform(jax.random.fold_in(jax.random.fold_in(stream_key, 6), dim), (blocks,), jnp.float32, smallest / len(shards), top_value / len(shards))
        return jnp.repeat(jnp.exp(heights), dims[dim] // blocks).reshape((-1,) + (1,) * (len(dims) - dim - 1))

    loudness = one(*shards[0])
    for cut in shards[1:]:
        loudness = loudness * one(*cut)
    return loudness


def distinct(key, rows, count, top, lift):
    sequence = jax.random.permutation(jax.random.fold_in(key, 1), count)
    pull = sequence
    for power in range(3):
        pull = pull * pull // count
    pull = pull * lift // count
    tickets = jax.random.randint(jax.random.fold_in(key, 2), (rows, count), 0, 4096) + pull
    holders = jax.random.permutation(jax.random.fold_in(key, 3), rows)[jnp.arange(count) % rows]
    tickets = jnp.where(jnp.arange(rows)[:, None] == holders[None, :], 1 << 14, tickets)
    priority = tickets * count + jnp.arange(count)
    return lax.top_k(priority.astype(jnp.int32), top)[1].astype(jnp.int32)


def profile(number_of, total, most, skew):
    weights = [(1 << 20) // math.isqrt(rank ** skew) + 1 for rank in range(2, number_of + 1)]
    surplus, given = total - most - (number_of - 1), [1] * (number_of - 1)
    while surplus > 0:
        movable = [i for i in range(number_of - 1) if given[i] < most]
        whole, remaining = sum([weights[i] for i in movable]), surplus
        for i in movable:
            addition = min(most - given[i], max(1, remaining * weights[i] // whole), surplus)
            given[i] = given[i] + addition
            surplus = surplus - addition
    return np.array([most] + given)


def uneven(stream_key, number_of, total, bound, slope):
    if number_of == 2:
        one = jax.random.randint(stream_key, (), max(1, total - bound), min(bound, total - 1) + 1)
        return jnp.stack([one, total - one])
    sizes = jnp.asarray(profile(number_of, total, bound, slope), jnp.int32)
    couples = (number_of - 1) // 2
    giver, sink = sizes[1:1 + 2 * couples:2], sizes[2:2 + 2 * couples:2]
    margin = jnp.minimum(giver - 1, bound - sink)
    passed = jax.random.randint(jax.random.fold_in(stream_key, 1), (couples,), 0, 1 << 20) % (margin + 1)
    sizes = sizes.at[1:1 + 2 * couples:2].set(giver - passed).at[2:2 + 2 * couples:2].set(sink + passed)
    return sizes[jax.random.permutation(jax.random.fold_in(stream_key, 2), number_of)]


def normal_values(stream_key, extent, deviation, reach, split=(), kind=jnp.bfloat16):
    drawn = deviation * jax.random.normal(stream_key, extent, jnp.float32)
    if split:
        drawn = drawn * block_scale(stream_key, extent, split, -0.22, 0.18)
    return jnp.clip(drawn, -reach, reach).astype(kind)


def setup_inputs(seed: int = 0) -> dict:
    splits = jax.random.split(jax.random.key(seed), 13)
    return {
        "hidden_in": normal_values(splits[0], (TOKENS, MODEL_WIDTH), 1.0, 6.0, ((0, 32),)),
        "attn_gain": jnp.clip(1.0 + 0.1 * jax.random.normal(splits[1], (MODEL_WIDTH,), jnp.float32), 0.5, 1.5).astype(jnp.bfloat16),
        "query_proj": normal_values(splits[2], (MODEL_WIDTH, QUERY_HEADS_COUNT * HEAD_SIZE), (MODEL_WIDTH // 4) ** -0.5, 0.3125, ((0, 8), (1, 4))),
        "key_value_projection": normal_values(splits[3], (MODEL_WIDTH, 2, KEY_VALUE_HEADS * HEAD_SIZE), MODEL_WIDTH ** -0.5, 0.15625, ((0, 8), (2, 4))),
        "output_proj": normal_values(splits[4], (QUERY_HEADS_COUNT * HEAD_SIZE, MODEL_WIDTH), (max(QUERY_HEADS_COUNT * HEAD_SIZE // 256, 1)) ** -0.5, 2.5, ((0, 4), (1, 8))),
        "moe_gain": jnp.clip(1.0 + 0.1 * jax.random.normal(splits[5], (MODEL_WIDTH,), jnp.float32), 0.5, 1.5).astype(jnp.bfloat16),
        "router_proj": normal_values(splits[6], (MODEL_WIDTH, E), (0.7 / MODEL_WIDTH ** 0.5), 0.106933594, ((0, 8),)),
        "gateup_proj": normal_values(splits[7], (E, MODEL_WIDTH, 2, FF), MODEL_WIDTH ** -0.5, 0.15625, ((1, 8), (3, 4))),
        "down_proj": normal_values(splits[8], (E, FF, MODEL_WIDTH), (FF // 4) ** -0.5, 0.375, ((1, 4), (2, 8))),
        "segment_index_list": jnp.searchsorted(jnp.cumsum(uneven(splits[9], max(TOKENS // 512, 8), TOKENS, TOKENS // 4, 2)), jnp.arange(TOKENS), side="right").astype(jnp.int32),
        "expert_ids": distinct(splits[10], TOKENS, E, 2, 2048),
        "out_grad": normal_values(splits[11], (TOKENS, MODEL_WIDTH), 1.0, 6.0, ((0, 32),)),
    }


NORM_EPS = 1e-05
MASKED_SCORE = -1e+30
FULL_PREC = lax.Precision.HIGHEST

@jax.custom_vjp
def low(v):
    return lax.optimization_barrier(v.astype(jnp.bfloat16)).astype(jnp.float32)

@jax.custom_vjp
def low_back(v):
    return v

def low_keep(v):
    return (low(v), None)

def low_pass(kept, grad):
    return (grad,)

def back_keep(v):
    return (v, None)

def back_low(kept, grad):
    return (low(grad),)
low.defvjp(low_keep, low_pass)
low_back.defvjp(back_keep, back_low)

def root_norm(values, gain_vec):
    factor = lax.rsqrt(lax.optimization_barrier(jnp.mean(values * values, axis=-1, keepdims=True)) + NORM_EPS)
    return values * factor * gain_vec

def route_slots(expert_ids):
    row_count = expert_ids.shape[0]
    listed = jnp.concatenate([expert_ids[:, 0], expert_ids[:, 1]])
    onehot = (listed[:, None] == jnp.arange(E, dtype=jnp.int32)[None, :]).astype(jnp.int32)
    earlier = jnp.cumsum(onehot, axis=0) - onehot
    position = lax.optimization_barrier(jnp.sum(earlier * onehot, axis=1))
    placed = jnp.where(position < CAP, listed * CAP + position, -1)
    return placed.reshape(2, row_count).T

def attend_block(query_blk, query_pos, query_seg, key_matrix_full, value_matrix_full, key_seg):
    scores = jnp.einsum('qngd,knd->ngqk', query_blk, key_matrix_full, precision=FULL_PREC) * (1.0 / math.sqrt(HEAD_SIZE))
    scores = low_back(scores)
    key_pos = jnp.arange(key_matrix_full.shape[0], dtype=jnp.int32)
    allowed = (key_pos[None, :] <= query_pos[:, None]) & (key_seg[None, :] == query_seg[:, None])
    scores = jnp.where(allowed, scores, MASKED_SCORE)
    row_max = lax.optimization_barrier(jnp.max(scores, axis=-1, keepdims=True))
    weights = jnp.where(allowed, jnp.exp(scores - row_max), 0.0)
    row_sum = lax.optimization_barrier(jnp.sum(weights, axis=-1, keepdims=True))
    blended_rows = jnp.einsum('ngqk,knd->qngd', low(weights), value_matrix_full, precision=FULL_PREC)
    return blended_rows / jnp.transpose(row_sum, (2, 0, 1, 3))

def attend_whole_sequence(query_matrix_full, key_row_slice, value_row_slice, segment_index_list):
    length_total = query_matrix_full.shape[0]
    block_length = min(256, length_total)
    count_of_blocks = length_total // block_length
    query_block_list = query_matrix_full.reshape(count_of_blocks, block_length, KEY_VALUE_HEADS, QUERY_HEADS_COUNT // KEY_VALUE_HEADS, HEAD_SIZE)
    key_matrix_full = key_row_slice.reshape(length_total, KEY_VALUE_HEADS, HEAD_SIZE)
    value_matrix_full = value_row_slice.reshape(length_total, KEY_VALUE_HEADS, HEAD_SIZE)
    positions = jnp.arange(length_total, dtype=jnp.int32).reshape(count_of_blocks, block_length)
    seg_blocks = segment_index_list.reshape(count_of_blocks, block_length)
    checked = jax.checkpoint(attend_block)
    blended_rows = lax.map(lambda packed_documents: checked(packed_documents[0], packed_documents[1], packed_documents[2], key_matrix_full, value_matrix_full, segment_index_list), (query_block_list, positions, seg_blocks))
    return blended_rows.reshape(length_total, QUERY_HEADS_COUNT * HEAD_SIZE)

def attention(query_matrix_full, key_row_slice, value_row_slice, segment_index_list):
    sequence_count = TOKENS // SEQUENCE_LENGTH
    blended_rows = lax.map(lambda packed_documents: attend_whole_sequence(packed_documents[0], packed_documents[1], packed_documents[2], packed_documents[3]), (query_matrix_full.reshape(sequence_count, SEQUENCE_LENGTH, QUERY_HEADS_COUNT * HEAD_SIZE), key_row_slice.reshape(sequence_count, SEQUENCE_LENGTH, KEY_VALUE_HEADS * HEAD_SIZE), value_row_slice.reshape(sequence_count, SEQUENCE_LENGTH, KEY_VALUE_HEADS * HEAD_SIZE), segment_index_list.reshape(sequence_count, SEQUENCE_LENGTH)))
    return blended_rows.reshape(TOKENS, QUERY_HEADS_COUNT * HEAD_SIZE)

def expert_span(rows, ids, gateup_proj, down_proj):
    slots = route_slots(ids)
    placement = (slots[None, :, :] == jnp.arange(E * CAP, dtype=jnp.int32)[:, None, None]).astype(jnp.float32)
    dispatch = lax.optimization_barrier(jnp.sum(placement, axis=-1))
    expert_in = jnp.dot(dispatch, rows, precision=FULL_PREC).reshape(E, CAP, MODEL_WIDTH)
    gate_up = low_back(jnp.einsum('ecd,edtf->ectf', expert_in, gateup_proj, precision=FULL_PREC))
    activated = low(jax.nn.silu(gate_up[:, :, 0]) * gate_up[:, :, 1])
    expert_out = low_back(jnp.einsum('ecf,efd->ecd', activated, down_proj, precision=FULL_PREC)).reshape(E * CAP, MODEL_WIDTH)
    return jnp.einsum('sck,sd->ckd', placement, expert_out, precision=FULL_PREC)

def forward(hidden_in, attn_gain, query_proj, key_value_projection, output_proj, moe_gain, router_proj, gateup_proj, down_proj, segment_index_list, expert_ids):
    rounded_one = low(root_norm(hidden_in, attn_gain))
    queries = low(low_back(jnp.dot(rounded_one, query_proj, precision=FULL_PREC)))
    keyvals = low(low_back(jnp.einsum('cd,dtj->ctj', rounded_one, key_value_projection, precision=FULL_PREC)))
    attended = attention(queries, keyvals[:, 0], keyvals[:, 1], segment_index_list)
    attended = low(low_back(attended))
    middle = hidden_in + low_back(jnp.dot(attended, output_proj, precision=FULL_PREC))
    rounded_two = low(root_norm(middle, moe_gain))
    logits = jnp.dot(rounded_two, router_proj, precision=FULL_PREC)
    selector = (expert_ids[:, :, None] == jnp.arange(E, dtype=jnp.int32)).astype(jnp.float32)
    chosen = lax.optimization_barrier(jnp.sum(selector * logits[:, None, :], axis=-1))
    weights = jax.nn.softmax(chosen, axis=-1)
    checked = jax.checkpoint(expert_span)
    per_route = lax.map(lambda packed_documents: checked(packed_documents[0], packed_documents[1], gateup_proj, down_proj), (rounded_two.reshape(N_DP, CH, MODEL_WIDTH), expert_ids.reshape(N_DP, CH, 2))).reshape(TOKENS, 2, MODEL_WIDTH)
    mixture = lax.optimization_barrier(jnp.sum(weights[:, :, None] * per_route, axis=1))
    return middle + low_back(mixture)

def reference(hidden_in, attn_gain, query_proj, key_value_projection, output_proj, moe_gain, router_proj, gateup_proj, down_proj, segment_index_list, expert_ids, out_grad):
    floats = tuple((member.astype(jnp.float32) for member in (hidden_in, attn_gain, query_proj, key_value_projection, output_proj, moe_gain, router_proj, gateup_proj, down_proj)))

    def closed(*params):
        return forward(*params, segment_index_list, expert_ids)
    result, pullback = jax.vjp(closed, *floats)
    gradients = pullback(out_grad.astype(jnp.float32))
    return (result.astype(jnp.bfloat16), gradients[0], gradients[1], gradients[2], gradients[3], gradients[4], gradients[5], gradients[6], gradients[7], gradients[8])
```

```python
import functools

import jax
import jax.numpy as jnp
from jax import lax
from jax.experimental import pallas as pl
from jax.experimental.pallas import tpu as pltpu
from jax.sharding import PartitionSpec as P

HEAD = 64
E = 8
SEQ_SPANS = 8
CAP = 240
SLOT = 64
BLK = 256
EXTRA = 128

NORM_EPS = 1e-05
NEG = -1e30

F32 = jnp.float32
BF16 = jnp.bfloat16


def dg(a, b, ca, cb):
    return lax.dot_general(a, b, (((ca,), (cb,)), ((), ())), preferred_element_type=F32)


def sds(shape, dtype):
    return jax.ShapeDtypeStruct(shape, dtype)


def kcall(name, body, outs, smem, vmem, scratch=(), flops=0, limit=56):
    n_bytes = sum(v.size * v.dtype.itemsize for v in vmem)
    return pl.pallas_call(
        body,
        name=name,
        out_shape=list(outs),
        in_specs=[pl.BlockSpec(memory_space=pltpu.SMEM)] * len(smem)
        + [pl.BlockSpec(memory_space=pltpu.VMEM)] * len(vmem),
        out_specs=[pl.BlockSpec(memory_space=pltpu.VMEM)] * len(outs),
        scratch_shapes=list(scratch),
        compiler_params=pltpu.CompilerParams(vmem_limit_bytes=limit << 20),
        cost_estimate=pl.CostEstimate(
            flops=int(flops), bytes_accessed=int(n_bytes), transcendentals=0
        ),
    )(*smem, *vmem)


def swap(value, axis, by):
    size = lax.axis_size(axis)
    return lax.ppermute(value, axis, [(i, i ^ by) for i in range(size)])


def shifted(value, axis, by):
    size = lax.axis_size(axis)
    return lax.ppermute(value, axis, [(i, i + by) for i in range(size) if 0 <= i + by < size])


def gather_tensor(value):
    one = swap(value, "tensor", 1)
    two = swap(value, "tensor", 2)
    return [value, one, two, swap(two, "tensor", 1)]


def scatter_tensor(keep, send):
    got = swap(send, "tensor", 1)
    second = (keep[1].astype(F32) + got[1].astype(F32)).astype(BF16)
    return keep[0], got[0], swap(second, "tensor", 2)


def ring_pos(index, size):
    return jnp.where(index % 2 == 0, index // 2, size - 1 - (index - 1) // 2)


def ring_dev(pos, size):
    pos = pos % size
    return jnp.where(pos < size // 2, 2 * pos, 2 * (size - 1 - pos) + 1)


def ring_gather(value, axis):
    size = lax.axis_size(axis)
    order = list(range(0, size, 2)) + list(range(size - 1, 0, -2))
    ahead = [(order[k], order[(k + 1) % size]) for k in range(size)]
    back = [(b, a) for a, b in ahead]
    rows = value.shape[0]
    half = rows // 2
    index = lax.axis_index(axis)
    pos = ring_pos(index, size)
    pieces, offs = [value], [index * rows]
    one = two = value
    for step in range(1, size // 2):
        one = lax.ppermute(one, axis, ahead)
        two = lax.ppermute(two, axis, back)
        pieces += [one, two]
        offs += [ring_dev(pos - step, size) * rows, ring_dev(pos + step, size) * rows]
    far = ring_dev(pos + size // 2, size) * rows
    pieces += [lax.ppermute(one[:half], axis, ahead), lax.ppermute(two[half:], axis, back)]
    offs += [far, far + half]
    return pieces, jnp.stack(offs).astype(jnp.int32)


def exchange(parts):
    return [parts[0]] + [swap(parts[d], "dp", d) for d in range(1, E)]


def place_kernel(n, off_ref, *refs):
    ins, out = refs[:n], refs[n]
    for k in range(n):
        rows = ins[k].shape[0]
        out[pl.ds(pl.multiple_of(off_ref[k], 8), rows), :] = ins[k][...]


def qkv_kernel(n, own, qw, kvw, off_ref, idx_ref, *refs):
    pieces = refs[:n]
    xs = refs[n : n + 4]
    w, gt, a1, qt, kv, xb, qn = refs[n + 4 :]
    rank = idx_ref[1]
    for k in range(n):
        rows = pieces[k].shape[0]
        w[pl.ds(pl.multiple_of(off_ref[k], 8), rows), :] = pieces[k][...]
    base = 2 * qw + kvw
    gt[...] = jnp.transpose(w[:, base : base + EXTRA].astype(F32))[0:32]
    for d in range(4):
        xb[pl.ds(pl.multiple_of((rank ^ d) * own, 16), own), :] = xs[d][...]
    gain = gt[0:1, :]

    def block(j, _):
        rows = pl.ds(pl.multiple_of(j * own, 16), own)
        x = xb[rows, :].astype(F32)
        factor = lax.rsqrt(jnp.mean(x * x, axis=-1, keepdims=True) + NORM_EPS)
        a = (x * factor * gain).astype(BF16)
        a1[rows, :] = a
        y = dg(a, w[:, qw:base], 1, 0)
        qn[rows, :] = y[:, :qw] * (HEAD**-0.5)
        kv[rows, :] = y[:, qw:].astype(BF16)
        return 0

    lax.fori_loop(0, 4, block, 0)
    qt[...] = jnp.transpose(qn[...]).astype(BF16)


def tile_loop(meta_ref, qb, own_tiles, body, init):
    low, full, diag = meta_ref[0, qb], meta_ref[1, qb], own_tiles + qb
    carry = body(diag, True, init)
    carry = lax.fori_loop(low, jnp.minimum(full, diag), lambda t, c: body(t, True, c), carry)
    return lax.fori_loop(jnp.maximum(full, low), diag, lambda t, c: body(t, False, c), carry)


def allowed_mask(t, qs, own_tiles, qseg, kseg):
    key_seg = kseg[pl.ds(pl.multiple_of(t * BLK, BLK), BLK), :]
    key_pos = t * BLK + lax.broadcasted_iota(jnp.int32, (BLK, BLK), 0)
    query_pos = own_tiles * BLK + qs + lax.broadcasted_iota(jnp.int32, (BLK, BLK), 1)
    return (key_pos <= query_pos) & (key_seg == qseg)


def attend_kernel(np_, groups, own, meta_ref, idx_ref, *refs):
    qt, qseg_ref, kseg, wo = refs[:4]
    kvs = refs[4 : 4 + np_]
    att, lse, low, keep, send, kb, vt = refs[4 + np_ :]
    span = qt.shape[1]
    half = kb.shape[1]
    kv_heads = half // HEAD
    own_tiles = (np_ - 1) * (span // BLK)
    for d in range(np_):
        at = (np_ - 1 - d) * span
        kb[at : at + span, :] = kvs[d][:, :half]
        vt[:, at : at + span] = jnp.transpose(kvs[d][:, half:].astype(F32)).astype(BF16)

    def q_block(qb, _):
        start = pl.multiple_of(qb * BLK, BLK)
        qs = pl.ds(start, BLK)
        qseg = qseg_ref[:, qs]
        for n in range(kv_heads):
            heads = [n * groups + g for g in range(groups)]
            q = [qt[h * HEAD : (h + 1) * HEAD, qs] for h in heads]

            def tile(t, masked, carry):
                ks = pl.ds(pl.multiple_of(t * BLK, BLK), BLK)
                k = kb[ks, n * HEAD : (n + 1) * HEAD]
                v = vt[n * HEAD : (n + 1) * HEAD, ks]
                ok = allowed_mask(t, start, own_tiles, qseg, kseg) if masked else None
                out = []
                for g in range(groups):
                    m, l, acc = carry[g]
                    s = dg(k, q[g], 1, 0)
                    if masked:
                        s = jnp.where(ok, s, NEG)
                    m_new = jnp.maximum(m, jnp.max(s, axis=0, keepdims=True))
                    e = jnp.exp(s - m_new)
                    shrink = jnp.exp(m - m_new)
                    l = l * shrink + jnp.sum(e, axis=0, keepdims=True)
                    acc = acc * shrink + dg(v, e.astype(BF16), 1, 0)
                    out.append((m_new, l, acc))
                return tuple(out)

            init = tuple(
                (
                    jnp.full((1, BLK), NEG, F32),
                    jnp.zeros((1, BLK), F32),
                    jnp.zeros((HEAD, BLK), F32),
                )
                for _ in range(groups)
            )
            done = tile_loop(meta_ref, qb, own_tiles, tile, init)
            for g in range(groups):
                m, l, acc = done[g]
                att[heads[g] * HEAD : (heads[g] + 1) * HEAD, qs] = acc / l
                lse[heads[g] : heads[g] + 1, qs] = m + jnp.log(l)
        return 0

    lax.fori_loop(0, span // BLK, q_block, 0)
    low[...] = jnp.transpose(att[...]).astype(BF16)
    rank = idx_ref[1]
    for d in range(4):
        rows = pl.ds(pl.multiple_of((rank ^ d) * own, 16), own)
        part = dg(low[rows, :], wo[...], 1, 1).astype(BF16)
        (send if d % 2 else keep)[d // 2] = part


def middle_kernel(gain_row, x, gt, kept, got, last, middle, a2):
    mid = x[...].astype(F32) + (
        kept[...].astype(F32) + got[...].astype(F32) + last[...].astype(F32)
    )
    middle[...] = mid
    factor = lax.rsqrt(jnp.mean(mid * mid, axis=-1, keepdims=True) + NORM_EPS)
    a2[...] = (mid * factor * gt[gain_row : gain_row + 1, :]).astype(BF16)


def select_tile(d, group_index, rows_ref, k=None):
    expert = group_index ^ d
    slot = expert * SLOT + lax.broadcasted_iota(jnp.int32, (SLOT, rows_ref.shape[1]), 0)
    first, second = slot == rows_ref[0:1, :], slot == rows_ref[1:2, :]
    hit = (first | second) if k is None else (second if k else first)
    return jnp.where(hit, 1.0, 0.0).astype(BF16)


def dispatch_kernel(own, with_ids, idx_ref, rows_ref, *refs):
    xs, outs = refs[:4], refs[4 : 4 + E]
    xb, pick = refs[4 + E :]
    index, rank = idx_ref[0] % E, idx_ref[1]
    for d in range(4):
        xb[pl.ds(pl.multiple_of((rank ^ d) * own, 16), own), :] = xs[d][...]
    for d in range(E):
        pick[d * SLOT : (d + 1) * SLOT, :] = select_tile(d, index, rows_ref)
    width = 512
    for c in range(xb.shape[1] // width):
        y = dg(pick[...], xb[:, c * width : (c + 1) * width], 1, 0)
        for d in range(E):
            part = y[d * SLOT : (d + 1) * SLOT]
            if with_ids and c == 0:
                ids = rows_ref[2:4, :].astype(F32).astype(BF16)
                row = dg(ids, select_tile(d, index, rows_ref, 0), 1, 1)[0:1]
                row = row + dg(ids, select_tile(d, index, rows_ref, 1), 1, 1)[1:2]
                row = jnp.concatenate([row, jnp.zeros((1, width - SLOT), F32)], axis=1)
                at = lax.broadcasted_iota(jnp.int32, part.shape, 0)
                part = jnp.where(at == SLOT - 4, row, part)
            outs[d][:, c * width : (c + 1) * width] = part.astype(BF16)


def eye():
    shape = (SLOT, SLOT)
    return lax.broadcasted_iota(jnp.int32, shape, 0) == lax.broadcasted_iota(jnp.int32, shape, 1)


def row_to_col(row):
    return jnp.sum(jnp.where(eye(), row, 0.0), axis=1, keepdims=True)


def col_to_row(col):
    return jnp.sum(jnp.where(eye(), col, 0.0), axis=0, keepdims=True)


def split_three(value):
    one = value.astype(BF16).astype(F32)
    two = (value - one).astype(BF16).astype(F32)
    return one, two, (value - one - two).astype(BF16).astype(F32)


def expert_kernel(ff, idx_ref, *refs):
    xs, gs, ws = refs[:E], refs[E : 2 * E], refs[2 * E : 2 * E + 4]
    gt = refs[2 * E + 4]
    xo, so, ho, wo = refs[2 * E + 5 : 2 * E + 9]
    dxs = refs[2 * E + 9 : 3 * E + 9]
    (dx,) = refs[3 * E + 9 :]
    index = idx_ref[0] % E
    width = xo.shape[1]
    for d in range(E):
        xo[d * SLOT : (d + 1) * SLOT, :] = xs[d][...]
    x = xo[...]
    logits = dg(x, gt[8:16, :].astype(BF16), 1, 1)
    lane = lax.broadcasted_iota(jnp.int32, (SLOT, E), 1)
    weights = []
    for d in range(E):
        rows = slice(d * SLOT, (d + 1) * SLOT)
        part = logits[rows]
        other = row_to_col(gs[d][SLOT - 8 : SLOT, 0:SLOT].astype(F32)[4:5]).astype(jnp.int32)
        mine = jnp.sum(jnp.where(lane == index, part, 0.0), axis=1, keepdims=True)
        theirs = jnp.sum(jnp.where(lane == other, part, 0.0), axis=1, keepdims=True)
        weight = 1.0 / (1.0 + jnp.exp(theirs - mine))
        real = lax.broadcasted_iota(jnp.int32, (SLOT, 1), 0) < SLOT - 4
        weight = jnp.where(real, weight, 0.0)
        weights.append(weight)
        so[rows, :] = jnp.where(real, weight * gs[d][...].astype(F32), 0.0).astype(BF16)
    wo[...] = jnp.concatenate(weights, axis=0)
    q = jnp.zeros((E * SLOT, 1), F32)
    for f in range(4):
        gate = dg(x, ws[f][:, :ff], 1, 0)
        up = dg(x, ws[f][:, ff : 2 * ff], 1, 0)
        hidden = dg(so[...], ws[f][:, 2 * ff :], 1, 0)
        sig = 1.0 / (1.0 + jnp.exp(-gate))
        act = gate * sig * up
        q = q + jnp.sum(hidden * act, axis=1, keepdims=True)
        ho[f, :, :ff] = (hidden * up * sig * (1.0 + gate * (1.0 - sig))).astype(BF16)
        ho[f, :, ff : 2 * ff] = (hidden * gate * sig).astype(BF16)
        ho[f, :, 2 * ff :] = act.astype(BF16)
        part = dg(ho[f, :, : 2 * ff], ws[f][:, : 2 * ff], 1, 1)
        dx[...] = part if f == 0 else dx[...] + part
    for d in range(E):
        rows = slice(d * SLOT, (d + 1) * SLOT)
        dxs[d][...] = dx[rows, :].astype(BF16)
        head = dx[rows, 0:128]
        at = lax.broadcasted_iota(jnp.int32, head.shape, 0)
        row = jnp.concatenate([col_to_row(q[rows]), jnp.zeros((1, 128 - SLOT), F32)], axis=1)
        for k, term in enumerate(split_three(row)):
            head = jnp.where(at == SLOT - 4 + k, term, head)
        dxs[d][:, 0:128] = head.astype(BF16)


def expert_grad_kernel(ff, x, s, h, keep, send):
    for f in range(4):
        out = send if f % 2 else keep
        out[f // 2, :, : 2 * ff] = dg(x[...], h[f, :, : 2 * ff], 0, 0).astype(BF16)
        out[f // 2, :, 2 * ff :] = dg(s[...], h[f, :, 2 * ff :], 0, 0).astype(BF16)


def expert_out_kernel(ff, h, weight, *refs):
    ws, outs = refs[:4], refs[4 : 4 + E]
    (acc,) = refs[4 + E :]
    for f in range(4):
        part = dg(h[f, :, 2 * ff :], ws[f][:, 2 * ff :], 1, 1)
        acc[...] = part if f == 0 else acc[...] + part
    for d in range(E):
        rows = slice(d * SLOT, (d + 1) * SLOT)
        outs[d][...] = (acc[rows, :] * weight[rows, :]).astype(BF16)


def combine_kernel(own, with_q, idx_ref, cols, *refs):
    parts = refs[:E]
    keep, send, y = refs[E:]
    index, rank = idx_ref[0] % E, idx_ref[1]
    width = parts[0].shape[1]
    for d in range(E):
        rows = slice(d * SLOT, (d + 1) * SLOT)
        y[rows, :width] = parts[d][...]
        if with_q:
            tail = parts[d][SLOT - 8 : SLOT, 0:SLOT].astype(F32)
            lane = lax.broadcasted_iota(jnp.int32, (SLOT, EXTRA), 1)
            side = jnp.zeros((SLOT, EXTRA), F32)
            for k in range(3):
                side = jnp.where(
                    lane == (index ^ d) + 8 * k, row_to_col(tail[4 + k : 5 + k]), side
                )
            y[rows, width:] = side.astype(BF16)
    shape = (own, E * SLOT)
    lane = lax.broadcasted_iota(jnp.int32, shape, 1)
    slot = ((lane // SLOT) ^ index) * SLOT + lane % SLOT
    for d in range(4):
        at = pl.ds(pl.multiple_of((rank ^ d) * own, 16), own)
        hit = (cols[at, 0:1] == slot) | (cols[at, 1:2] == slot)
        part = dg(jnp.where(hit, 1.0, 0.0).astype(BF16), y[...], 1, 0)
        (send if d % 2 else keep)[d // 2] = part.astype(BF16)


def middle_back_kernel(mid_ref, a2, g, ids, gt, kept, got, last, grad_mid, branch, small):
    width = mid_ref.shape[1]
    total = kept[...].astype(F32) + got[...].astype(F32) + last[...].astype(F32)
    h2, side = total[:, :width], total[:, width:]
    own = h2.shape[0]
    logits = dg(a2[...], gt[8:16, :].astype(BF16), 1, 1)
    lane = lax.broadcasted_iota(jnp.int32, (own, E), 1)
    q = side[:, 0:8] + side[:, 8:16] + side[:, 16:24]
    hit = [lane == ids[:, k : k + 1] for k in range(2)]
    logit = [jnp.sum(jnp.where(hit[k], logits, 0.0), axis=1, keepdims=True) for k in range(2)]
    terms = [jnp.sum(jnp.where(hit[k], q, 0.0), axis=1, keepdims=True) for k in range(2)]
    both = terms[0] + terms[1]
    logit_grad = jnp.zeros((own, E), F32)
    for k in range(2):
        weight = 1.0 / (1.0 + jnp.exp(logit[1 - k] - logit[k]))
        logit_grad = jnp.where(hit[k], terms[k] - weight * both, logit_grad)
    high = logit_grad.astype(BF16)
    rest = (logit_grad - high.astype(F32)).astype(BF16)
    router = gt[8:16, :].astype(BF16)
    h2 = h2 + dg(high, router, 1, 0) + dg(rest, router, 1, 0)
    mid = mid_ref[...]
    factor = lax.rsqrt(jnp.mean(mid * mid, axis=-1, keepdims=True) + NORM_EPS)
    normed = mid * factor
    u = h2 * gt[1:2, :]
    back = g[...].astype(F32) + factor * (
        u - normed * jnp.mean(u * normed, axis=-1, keepdims=True)
    )
    grad_mid[...] = back
    branch[...] = back.astype(BF16)
    small[...] = jnp.zeros_like(small)
    small[1:2, :] = jnp.sum(h2 * normed, axis=0, keepdims=True)
    small[8:16, :] = dg(high, a2[...], 0, 0) + dg(rest, a2[...], 0, 0)


def attend_back_kernel(np_, groups, own, meta_ref, idx_ref, *refs):
    bs = refs[:4]
    qt, att, lse, qseg_ref, kseg, wo = refs[4:10]
    kvs = refs[10 : 10 + np_]
    full, dq = refs[10 + np_ : 12 + np_]
    dkvs = refs[12 + np_ : 12 + 2 * np_]
    kb, vb, kt, gt, delta, dkv = refs[12 + 2 * np_ :]
    span = qt.shape[1]
    half = kb.shape[1]
    kv_heads = half // HEAD
    own_tiles = (np_ - 1) * (span // BLK)
    rank = idx_ref[1]
    for d in range(4):
        full[pl.ds(pl.multiple_of((rank ^ d) * own, 16), own), :] = bs[d][...]
    for d in range(np_):
        at = (np_ - 1 - d) * span
        kb[at : at + span, :] = kvs[d][:, :half]
        vb[at : at + span, :] = kvs[d][:, half:]
        kt[:, at : at + span] = jnp.transpose(kvs[d][:, :half].astype(F32)).astype(BF16)
    gt[...] = dg(wo[...], full[...], 0, 1).astype(BF16)
    for h in range(kv_heads * groups):
        rows = slice(h * HEAD, (h + 1) * HEAD)
        delta[h : h + 1, :] = jnp.sum(gt[rows, :].astype(F32) * att[rows, :], axis=0, keepdims=True)
    dkv[...] = jnp.zeros_like(dkv)

    def q_block(qb, _):
        start = pl.multiple_of(qb * BLK, BLK)
        qs = pl.ds(start, BLK)
        qseg = qseg_ref[:, qs]
        for n in range(kv_heads):
            heads = [n * groups + g for g in range(groups)]
            sl = [slice(h * HEAD, (h + 1) * HEAD) for h in heads]
            q = [qt[r, qs] for r in sl]
            go = [gt[r, qs] for r in sl]
            ls = [lse[h : h + 1, qs] for h in heads]
            de = [delta[h : h + 1, qs] for h in heads]

            def tile(t, masked, carry):
                ks = pl.ds(pl.multiple_of(t * BLK, BLK), BLK)
                lanes = slice(n * HEAD, (n + 1) * HEAD)
                k, v, k_t = kb[ks, lanes], vb[ks, lanes], kt[lanes, ks]
                ok = allowed_mask(t, start, own_tiles, qseg, kseg) if masked else None
                out = []
                dk = dv = None
                for g in range(groups):
                    p = jnp.exp(dg(k, q[g], 1, 0) - ls[g])
                    if masked:
                        p = jnp.where(ok, p, 0.0)
                    ds = (p * (dg(v, go[g], 1, 0) - de[g])).astype(BF16)
                    one = dg(q[g], ds, 1, 1)
                    two = dg(go[g], p.astype(BF16), 1, 1)
                    dk = one if dk is None else dk + one
                    dv = two if dv is None else dv + two
                    out.append(carry[g] + dg(k_t, ds, 1, 0))
                dkv[n * HEAD : (n + 1) * HEAD, ks] += dk
                dkv[half + n * HEAD : half + (n + 1) * HEAD, ks] += dv
                return tuple(out)

            init = tuple(jnp.zeros((HEAD, BLK), F32) for _ in range(groups))
            done = tile_loop(meta_ref, qb, own_tiles, tile, init)
            for g in range(groups):
                dq[sl[g], qs] = (done[g] * (HEAD**-0.5)).astype(BF16)
        return 0

    lax.fori_loop(0, span // BLK, q_block, 0)
    for d in range(np_):
        at = (np_ - 1 - d) * span
        dkvs[d][...] = dkv[:, at : at + span].astype(dkvs[d].dtype)


def input_back_kernel(np_, own, idx_ref, *refs):
    dq, w, a1, gt = refs[:4]
    dkvs = refs[4 : 4 + np_]
    keep, send, nat, small = refs[4 + np_ :]
    rank = idx_ref[1]
    total = dkvs[0][...]
    for d in range(1, np_):
        total = total + dkvs[d][...].astype(F32)
    qw = dq.shape[0]
    nat[:, :qw] = jnp.transpose(dq[...].astype(F32)).astype(BF16)
    nat[:, qw:] = jnp.transpose(total).astype(BF16)
    gain = jnp.zeros((1, w.shape[0]), F32)
    for d in range(4):
        rows = pl.ds(pl.multiple_of((rank ^ d) * own, 16), own)
        part = dg(nat[rows, :], w[:, qw : qw + nat.shape[1]], 1, 1)
        gain = gain + jnp.sum(part * a1[rows, :].astype(F32), axis=0, keepdims=True)
        (send if d % 2 else keep)[d // 2] = part.astype(BF16)
    small[...] = jnp.zeros_like(small)
    small[0:1, :] = gain / gt[0:1, :]


def weight_grad_kernel(n, rows, idx_ref, left, right, small, *refs):
    outs, full = refs[:n], refs[n]
    width = right.shape[1]
    full[:, :width] = dg(left[...], right[...], 0, 0)
    pad = jnp.zeros((EXTRA - small.shape[0], small.shape[1]), F32)
    full[:, width:] = jnp.transpose(jnp.concatenate([small[...], pad], axis=0))
    for d in range(n):
        at = pl.ds(pl.multiple_of((idx_ref[0] ^ d) * rows, 8), rows)
        outs[d][...] = full[at, :].astype(BF16)


def input_grad_kernel(x, gt, grad_mid, kept, got, last, out):
    h1 = kept[...].astype(F32) + got[...].astype(F32) + last[...].astype(F32)
    v = x[...].astype(F32)
    factor = lax.rsqrt(jnp.mean(v * v, axis=-1, keepdims=True) + NORM_EPS)
    normed = v * factor
    u = h1 * gt[0:1, :]
    out[...] = grad_mid[...] + factor * (
        u - normed * jnp.mean(u * normed, axis=-1, keepdims=True)
    )


def expert_unpack_kernel(ff, idx_ref, *refs):
    parts = refs[:E]
    gateup, down = refs[E:]
    index = idx_ref[0] % E
    for d in range(E):
        e = index ^ d
        gateup[e] = parts[d][:, : 2 * ff].astype(F32)
        down[e] = jnp.transpose(parts[d][:, 2 * ff :].astype(F32))


def route_slots(expert_ids):
    listed = jnp.concatenate([expert_ids[:, 0], expert_ids[:, 1]])
    onehot = (listed[:, None] == jnp.arange(E, dtype=jnp.int32)[None, :]).astype(jnp.int32)
    earlier = jnp.cumsum(onehot, axis=0) - onehot
    return jnp.sum(earlier * onehot, axis=1).reshape(2, -1)


def per_device(
    hidden_in,
    attn_gain,
    query_proj,
    key_value_projection,
    output_proj,
    moe_gain,
    router_proj,
    gateup_proj,
    down_proj,
    segment_index_list,
    expert_ids,
    out_grad,
):
    n_dp, n_tensor = lax.axis_size("dp"), lax.axis_size("tensor")
    own, width = hidden_in.shape
    span = own * n_tensor
    rows = query_proj.shape[0]
    qw = query_proj.shape[1]
    kvw = 2 * key_value_projection.shape[2]
    groups = 2 * qw // kvw
    ff = gateup_proj.shape[3]
    n_groups = n_dp // E
    dp, rank = lax.axis_index("dp"), lax.axis_index("tensor")
    idx = jnp.stack([dp, rank]).astype(jnp.int32)
    base = 2 * qw + kvw

    mine = jnp.concatenate(
        [
            output_proj.T,
            query_proj,
            key_value_projection.reshape(rows, kvw),
            attn_gain[:, None],
            moe_gain[:, None],
            jnp.zeros((rows, 6), BF16),
            router_proj,
            jnp.zeros((rows, EXTRA - 16), BF16),
        ],
        axis=1,
    )
    x_parts = gather_tensor(hidden_in)
    pieces, offs = ring_gather(mine, "dp")
    w_attn, gt, a1, qt, kv = kcall(
        "qkv",
        functools.partial(qkv_kernel, len(pieces), own, qw, kvw),
        [
            sds((width, base + EXTRA), BF16),
            sds((32, width), F32),
            sds((span, width), BF16),
            sds((qw, span), BF16),
            sds((span, kvw), BF16),
        ],
        [offs, idx],
        pieces + x_parts,
        [pltpu.VMEM((span, width), BF16), pltpu.VMEM((span, qw), F32)],
        flops=2 * span * width * (qw + kvw),
    )
    wo = w_attn[:, :qw]

    longest = segment_index_list.shape[0] // 4
    reach = min(SEQ_SPANS - 1, -(-(longest - 1) // span))
    n_pieces = reach + 1
    tiles = span // BLK
    padded = jnp.concatenate([jnp.full((reach * span,), -1, jnp.int32), segment_index_list])
    window = lax.dynamic_slice_in_dim(padded, dp * span, n_pieces * span, 0)
    seg_mine = window[reach * span :]
    valid = jnp.minimum(dp % SEQ_SPANS, reach)
    first_seg, last_seg = seg_mine[::BLK], seg_mine[BLK - 1 :: BLK]
    low_tile = jnp.sum(window[None, :] < first_seg[:, None], axis=1) // BLK
    low_tile = jnp.maximum(low_tile, (reach - valid) * tiles)
    full_tile = -(-jnp.sum(window[None, :] < last_seg[:, None], axis=1) // BLK)
    meta = jnp.stack([low_tile, full_tile]).astype(jnp.int32)
    kseg, qseg = window[:, None], seg_mine[None, :]

    position = route_slots(expert_ids)
    per_rank = CAP // n_tensor
    local = position - rank * per_rank
    ids_t = expert_ids.T
    slots = jnp.where(
        (local >= 0) & (local < per_rank) & (position < CAP), ids_t * SLOT + local, -1
    ).astype(jnp.int32)
    slot_rows = jnp.concatenate([slots, ids_t[::-1], jnp.zeros((4, span), jnp.int32)], axis=0)
    slot_cols = slots.T
    ids_own = lax.dynamic_slice_in_dim(expert_ids, rank * own, own, 0)

    kvs = [kv] + [shifted(kv, "dp", d) for d in range(1, n_pieces)]

    packed = jnp.concatenate(
        [gateup_proj[:, :, 0], gateup_proj[:, :, 1], jnp.transpose(down_proj, (0, 2, 1))], axis=2
    )
    group_index = dp % E
    sent = [
        lax.dynamic_index_in_dim(packed, group_index ^ d, 0, keepdims=False) for d in range(E)
    ]
    parts = exchange(sent)
    group_base = (dp - group_index) * rows
    part_offs = jnp.stack([group_base + (group_index ^ d) * rows for d in range(E)])
    if n_groups > 1:
        near = jnp.concatenate(parts, axis=0)
        parts, part_offs = list(parts), list(part_offs)
        for h in range(1, n_groups):
            far = swap(near, "dp", h * E)
            other = dp ^ (h * E)
            for d in range(E):
                parts.append(far[d * rows : (d + 1) * rows])
                part_offs.append((other - group_index + ((group_index) ^ d)) * rows)
        part_offs = jnp.stack(part_offs)
    (w_expert,) = kcall(
        "place",
        functools.partial(place_kernel, len(parts)),
        [sds((width, 3 * ff), BF16)],
        [part_offs.astype(jnp.int32)],
        list(parts),
        limit=24,
    )
    w_parts = gather_tensor(w_expert)

    def dispatch(pieces_, with_ids):
        outs = kcall(
            "dispatch",
            functools.partial(dispatch_kernel, own, with_ids),
            [sds((SLOT, width), BF16)] * E,
            [idx],
            [slot_rows] + pieces_,
            [pltpu.VMEM((span, width), BF16), pltpu.VMEM((E * SLOT, span), BF16)],
            flops=2 * E * SLOT * span * width,
            limit=32,
        )
        return exchange(outs)

    g_parts = dispatch(gather_tensor(out_grad), True)

    att, lse, low, keep, send = kcall(
        "attend",
        functools.partial(attend_kernel, n_pieces, groups, own),
        [
            sds((qw, span), F32),
            sds((8, span), F32),
            sds((span, qw), BF16),
            sds((2, own, width), BF16),
            sds((2, own, width), BF16),
        ],
        [meta, idx],
        [qt, qseg, kseg, wo] + kvs,
        [
            pltpu.VMEM((n_pieces * span, kvw // 2), BF16),
            pltpu.VMEM((kvw // 2, n_pieces * span), BF16),
        ],
        flops=2 * span * span * 2 * qw * 2,
    )
    middle, a2 = kcall(
        "middle",
        functools.partial(middle_kernel, 1),
        [sds((own, width), F32), sds((own, width), BF16)],
        [],
        [hidden_in, gt] + list(scatter_tensor(keep, send)),
        limit=24,
    )

    in_parts = dispatch(gather_tensor(a2), False)
    outs = kcall(
        "expert",
        functools.partial(expert_kernel, ff),
        [
            sds((E * SLOT, width), BF16),
            sds((E * SLOT, width), BF16),
            sds((4, E * SLOT, 3 * ff), BF16),
            sds((E * SLOT, 1), F32),
        ]
        + [sds((SLOT, width), BF16)] * E,
        [idx],
        in_parts + g_parts + w_parts + [gt],
        [pltpu.VMEM((E * SLOT, width), F32)],
        flops=2 * E * SLOT * width * 4 * 5 * ff,
    )
    x_slots, s_slots, hid, slot_weight = outs[:4]
    dx_parts = exchange(outs[4:])
    keep_w, send_w = kcall(
        "expert_grad",
        functools.partial(expert_grad_kernel, ff),
        [sds((2, width, 3 * ff), BF16)] * 2,
        [],
        [x_slots, s_slots, hid],
        flops=2 * E * SLOT * width * 4 * 3 * ff,
    )
    grad_terms = scatter_tensor(keep_w, send_w)
    out_parts = exchange(
        kcall(
            "expert_out",
            functools.partial(expert_out_kernel, ff),
            [sds((SLOT, width), BF16)] * E,
            [],
            [hid, slot_weight] + w_parts,
            [pltpu.VMEM((E * SLOT, width), F32)],
            flops=2 * E * SLOT * width * 4 * ff,
        )
    )

    def combine(parts_, with_q):
        wide = width + (EXTRA if with_q else 0)
        return scatter_tensor(
            *kcall(
                "combine",
                functools.partial(combine_kernel, own, with_q),
                [sds((2, own, wide), BF16)] * 2,
                [idx],
                [slot_cols] + list(parts_),
                [pltpu.VMEM((E * SLOT, wide), BF16)],
                flops=2 * E * SLOT * span * width,
                limit=32,
            )
        )

    back_terms = combine(dx_parts, True)
    grad_middle, branch, small_two = kcall(
        "middle_back",
        middle_back_kernel,
        [sds((own, width), F32), sds((own, width), BF16), sds((16, width), F32)],
        [],
        [middle, a2, out_grad, ids_own, gt] + list(back_terms),
        limit=32,
    )
    out_terms = combine(out_parts, False)
    hidden_out = (middle + sum(t.astype(F32) for t in out_terms)).astype(BF16)

    outs = kcall(
        "attend_back",
        functools.partial(attend_back_kernel, n_pieces, groups, own),
        [sds((span, width), BF16), sds((qw, span), BF16), sds((kvw, span), F32)]
        + [sds((kvw, span), BF16)] * reach,
        [meta, idx],
        gather_tensor(branch) + [qt, att, lse, qseg, kseg, wo] + kvs,
        [
            pltpu.VMEM((n_pieces * span, kvw // 2), BF16),
            pltpu.VMEM((n_pieces * span, kvw // 2), BF16),
            pltpu.VMEM((kvw // 2, n_pieces * span), BF16),
            pltpu.VMEM((qw, span), BF16),
            pltpu.VMEM((8, span), F32),
            pltpu.VMEM((kvw, n_pieces * span), F32),
        ],
        flops=5 * span * span * 2 * qw * 2,
    )
    branch_full, dq = outs[:2]
    dkvs = [outs[2]] + [shifted(outs[2 + d], "dp", -d) for d in range(1, n_pieces)]

    def spread(left, right, small):
        full = right.shape[1] + EXTRA
        got = kcall(
            "weight_grad",
            functools.partial(weight_grad_kernel, n_dp, rows),
            [sds((rows, full), BF16)] * n_dp,
            [idx],
            [left, right, small],
            [pltpu.VMEM((width, full), F32)],
            flops=2 * span * width * right.shape[1],
            limit=40,
        )
        return sum(
            (got[d] if d == 0 else swap(got[d], "dp", d)).astype(F32) for d in range(n_dp)
        )

    out_sum = spread(branch_full, low, small_two)
    keep_h, send_h, nat, small_one = kcall(
        "input_back",
        functools.partial(input_back_kernel, n_pieces, own),
        [
            sds((2, own, width), BF16),
            sds((2, own, width), BF16),
            sds((span, qw + kvw), BF16),
            sds((16, width), F32),
        ],
        [idx],
        [dq, w_attn, a1, gt] + dkvs,
        flops=2 * span * width * (qw + kvw),
        limit=40,
    )
    in_terms = scatter_tensor(keep_h, send_h)
    in_sum = spread(a1, nat, small_one)
    (input_grad,) = kcall(
        "input_grad",
        input_grad_kernel,
        [sds((own, width), F32)],
        [],
        [hidden_in, gt, grad_middle] + list(in_terms),
        limit=24,
    )

    side = out_sum[:, qw : qw + 16] + in_sum[:, qw + kvw : qw + kvw + 16]
    side = side + swap(side, "tensor", 1)
    side = side + swap(side, "tensor", 2)
    grad_w = sum(t.astype(F32) for t in grad_terms)
    if n_groups > 1:
        group = dp // E
        blocks = grad_w.astype(BF16).reshape(n_groups, E * rows, 3 * ff)
        grad_w = lax.dynamic_index_in_dim(blocks, group, 0, keepdims=False).astype(F32)
        for h in range(1, n_groups):
            there = lax.dynamic_index_in_dim(blocks, group ^ h, 0, keepdims=False)
            grad_w = grad_w + swap(there, "dp", h * E).astype(F32)
    blocks = grad_w.astype(BF16).reshape(E, rows, 3 * ff)
    back = exchange(
        [lax.dynamic_index_in_dim(blocks, group_index ^ d, 0, keepdims=False) for d in range(E)]
    )
    gateup_grad, down_grad = kcall(
        "expert_unpack",
        functools.partial(expert_unpack_kernel, ff),
        [sds((E, rows, 2 * ff), F32), sds((E, ff, rows), F32)],
        [idx],
        back,
        limit=32,
    )
    return (
        hidden_out,
        input_grad,
        side[:, 0],
        in_sum[:, :qw],
        in_sum[:, qw : qw + kvw].reshape(rows, 2, kvw // 2),
        out_sum[:, :qw].T,
        side[:, 1],
        side[:, 8:16],
        gateup_grad.reshape(E, rows, 2, ff),
        down_grad,
    )


def solution(mesh):
    return jax.shard_map(
        per_device,
        mesh=mesh,
        in_specs=(
            P(("dp", "tensor"), None),
            P("dp"),
            P("dp", "tensor"),
            P("dp", None, "tensor"),
            P("tensor", "dp"),
            P("dp"),
            P("dp", None),
            P(None, "dp", None, "tensor"),
            P(None, "tensor", "dp"),
            P(),
            P("dp", None),
            P(("dp", "tensor"), None),
        ),
        out_specs=(
            P(("dp", "tensor"), None),
            P(("dp", "tensor"), None),
            P("dp"),
            P("dp", "tensor"),
            P("dp", None, "tensor"),
            P("tensor", "dp"),
            P("dp"),
            P("dp", None),
            P(None, "dp", None, "tensor"),
            P(None, "tensor", "dp"),
        ),
        check_vma=False,
    )
```

```python
import functools

import jax
import jax.numpy as jnp
from jax import lax
from jax.experimental import pallas as pl
from jax.experimental.pallas import tpu as pltpu
from jax.sharding import PartitionSpec as P

HEAD = 64
E = 8
SEQ_SPANS = 8
CAP = 240
SLOT = 64
BLK = 256
EXTRA = 128

NORM_EPS = 1e-05
NEG = -1e30

F32 = jnp.float32
BF16 = jnp.bfloat16


def dg(a, b, ca, cb):
    return lax.dot_general(a, b, (((ca,), (cb,)), ((), ())), preferred_element_type=F32)


def sds(shape, dtype):
    return jax.ShapeDtypeStruct(shape, dtype)


def kcall(name, body, outs, smem, vmem, scratch=(), flops=0, limit=60):
    n_bytes = sum(v.size * v.dtype.itemsize for v in vmem)
    return pl.pallas_call(
        body,
        name=name,
        out_shape=list(outs),
        in_specs=[pl.BlockSpec(memory_space=pltpu.SMEM)] * len(smem)
        + [pl.BlockSpec(memory_space=pltpu.VMEM)] * len(vmem),
        out_specs=[pl.BlockSpec(memory_space=pltpu.VMEM)] * len(outs),
        scratch_shapes=list(scratch),
        compiler_params=pltpu.CompilerParams(vmem_limit_bytes=limit << 20),
        cost_estimate=pl.CostEstimate(
            flops=int(flops), bytes_accessed=int(n_bytes), transcendentals=0
        ),
    )(*smem, *vmem)


def swap(value, axis, by):
    size = lax.axis_size(axis)
    return lax.ppermute(value, axis, [(i, i ^ by) for i in range(size)])


def shifted(value, axis, by):
    size = lax.axis_size(axis)
    return lax.ppermute(value, axis, [(i, i + by) for i in range(size) if 0 <= i + by < size])


def gather_tensor(value):
    one = swap(value, "tensor", 1)
    two = swap(value, "tensor", 2)
    return [value, one, two, swap(two, "tensor", 1)]


def scatter_tensor(keep, send):
    got = swap(send, "tensor", 1)
    second = (keep[1].astype(F32) + got[1].astype(F32)).astype(BF16)
    return keep[0], got[0], swap(second, "tensor", 2)


def ring_pos(index, size):
    return jnp.where(index % 2 == 0, index // 2, size - 1 - (index - 1) // 2)


def ring_dev(pos, size):
    pos = pos % size
    return jnp.where(pos < size // 2, 2 * pos, 2 * (size - 1 - pos) + 1)


def ring_gather(value, axis, between):
    size = lax.axis_size(axis)
    order = list(range(0, size, 2)) + list(range(size - 1, 0, -2))
    ahead = [(order[k], order[(k + 1) % size]) for k in range(size)]
    back = [(b, a) for a, b in ahead]
    half = value.shape[0] // 16 * 8
    index = lax.axis_index(axis)
    pos = ring_pos(index, size)
    pieces, source = [value], [index]
    one = two = value
    for step in range(1, size // 2):
        between(step, one)
        one = lax.ppermute(one, axis, ahead)
        two = lax.ppermute(two, axis, back)
        pieces += [one, two]
        source += [ring_dev(pos - step, size), ring_dev(pos + step, size)]
    between(size // 2, one)
    far = ring_dev(pos + size // 2, size)
    pieces += [lax.ppermute(one[:half], axis, ahead), lax.ppermute(two[half:], axis, back)]
    source += [far, far]
    return pieces, jnp.stack(source).astype(jnp.int32)


def exchange(value, groups=None):
    return lax.all_to_all(
        value, "dp", split_axis=0, concat_axis=0, axis_index_groups=groups, tiled=True
    )


def after(value, *others):
    return lax.optimization_barrier((value,) + others)[0]


def qkv_kernel(n, own, rows, qw, src_ref, idx_ref, *refs):
    pieces = refs[:n]
    xs = refs[n : n + 4]
    w, gain, a1, qt, kv, xb, qn, gs = refs[n + 4 :]
    rank = idx_ref[1]
    for k in range(n):
        piece = pieces[k]
        first = pieces[n - 2].shape[0] if k == n - 1 else 0
        last = min(first + piece.shape[0], rows)
        at = pl.multiple_of(src_ref[k] * rows + first, 8)
        w[pl.ds(at, last - first), :] = piece[: last - first, :]
        if first + piece.shape[0] > rows:
            gs[pl.ds(src_ref[k], 1), :] = piece[last - first :, :rows].astype(F32)[0:1]
    for d in range(4):
        xb[pl.ds(pl.multiple_of((rank ^ d) * own, 16), own), :] = xs[d][...]
    gain[...] = jnp.concatenate([gs[j : j + 1, :] for j in range(gs.shape[0])], axis=1)

    def block(j, _):
        at = pl.ds(pl.multiple_of(j * own, 16), own)
        x = xb[at, :].astype(F32)
        factor = lax.rsqrt(jnp.mean(x * x, axis=-1, keepdims=True) + NORM_EPS)
        a = (x * factor * gain[...]).astype(BF16)
        a1[at, :] = a
        y = dg(a, w[...], 1, 0)
        qn[at, :] = y[:, :qw] * (HEAD**-0.5)
        kv[at, :] = y[:, qw:].astype(BF16)
        return 0

    lax.fori_loop(0, 4, block, 0)
    qt[...] = jnp.transpose(qn[...]).astype(BF16)


def tile_loop(meta_ref, qb, own_tiles, body, init):
    low, full, diag = meta_ref[0, qb], meta_ref[1, qb], own_tiles + qb
    carry = body(diag, True, init)
    carry = lax.fori_loop(low, jnp.minimum(full, diag), lambda t, c: body(t, True, c), carry)
    return lax.fori_loop(jnp.maximum(full, low), diag, lambda t, c: body(t, False, c), carry)


def allowed_mask(t, qs, own_tiles, qseg, kseg):
    key_seg = kseg[pl.ds(pl.multiple_of(t * BLK, BLK), BLK), :]
    key_pos = t * BLK + lax.broadcasted_iota(jnp.int32, (BLK, BLK), 0)
    query_pos = own_tiles * BLK + qs + lax.broadcasted_iota(jnp.int32, (BLK, BLK), 1)
    return (key_pos <= query_pos) & (key_seg == qseg)


def attend_kernel(np_, groups, meta_ref, *refs):
    qt, qseg_ref, kseg = refs[:3]
    kvs = refs[3 : 3 + np_]
    att, lse, low, kb, vt = refs[3 + np_ :]
    span = qt.shape[1]
    half = kb.shape[1]
    kv_heads = half // HEAD
    own_tiles = (np_ - 1) * (span // BLK)
    for d in range(np_):
        at = (np_ - 1 - d) * span
        kb[at : at + span, :] = kvs[d][:, :half]
        vt[:, at : at + span] = jnp.transpose(kvs[d][:, half:].astype(F32)).astype(BF16)

    def q_block(qb, _):
        start = pl.multiple_of(qb * BLK, BLK)
        qs = pl.ds(start, BLK)
        qseg = qseg_ref[:, qs]
        for n in range(kv_heads):
            heads = [n * groups + g for g in range(groups)]
            q = [qt[h * HEAD : (h + 1) * HEAD, qs] for h in heads]

            def tile(t, masked, carry):
                ks = pl.ds(pl.multiple_of(t * BLK, BLK), BLK)
                k = kb[ks, n * HEAD : (n + 1) * HEAD]
                v = vt[n * HEAD : (n + 1) * HEAD, ks]
                ok = allowed_mask(t, start, own_tiles, qseg, kseg) if masked else None
                out = []
                for g in range(groups):
                    m, l, acc = carry[g]
                    s = dg(k, q[g], 1, 0)
                    if masked:
                        s = jnp.where(ok, s, NEG)
                    m_new = jnp.maximum(m, jnp.max(s, axis=0, keepdims=True))
                    e = jnp.exp(s - m_new)
                    shrink = jnp.exp(m - m_new)
                    l = l * shrink + jnp.sum(e, axis=0, keepdims=True)
                    acc = acc * shrink + dg(v, e.astype(BF16), 1, 0)
                    out.append((m_new, l, acc))
                return tuple(out)

            init = tuple(
                (
                    jnp.full((1, BLK), NEG, F32),
                    jnp.zeros((1, BLK), F32),
                    jnp.zeros((HEAD, BLK), F32),
                )
                for _ in range(groups)
            )
            done = tile_loop(meta_ref, qb, own_tiles, tile, init)
            for g in range(groups):
                m, l, acc = done[g]
                att[heads[g] * HEAD : (heads[g] + 1) * HEAD, qs] = acc / l
                lse[heads[g] : heads[g] + 1, qs] = m + jnp.log(l)
        return 0

    lax.fori_loop(0, span // BLK, q_block, 0)
    low[...] = jnp.transpose(att[...]).astype(BF16)


def project_kernel(own, qw, idx_ref, low, w_late, keep, send, gt):
    rank = idx_ref[1]
    gt[...] = jnp.transpose(w_late[:, qw:].astype(F32))[0:16]
    for d in range(4):
        rows = pl.ds(pl.multiple_of((rank ^ d) * own, 16), own)
        part = dg(low[rows, :], w_late[:, :qw], 1, 1).astype(BF16)
        (send if d % 2 else keep)[d // 2] = part


def middle_kernel(x, gt, kept, got, last, middle, a2):
    mid = x[...].astype(F32) + (
        kept[...].astype(F32) + got[...].astype(F32) + last[...].astype(F32)
    )
    middle[...] = mid
    factor = lax.rsqrt(jnp.mean(mid * mid, axis=-1, keepdims=True) + NORM_EPS)
    a2[...] = (mid * factor * gt[0:1, :]).astype(BF16)


def select_tile(e, rows_ref, k=None):
    slot = e * SLOT + lax.broadcasted_iota(jnp.int32, (SLOT, rows_ref.shape[1]), 0)
    first, second = slot == rows_ref[0:1, :], slot == rows_ref[1:2, :]
    hit = (first | second) if k is None else (second if k else first)
    return jnp.where(hit, 1.0, 0.0).astype(BF16)


def dispatch_kernel(own, with_ids, idx_ref, rows_ref, *refs):
    xs, out = refs[:4], refs[4]
    xb, pick = refs[5:]
    rank = idx_ref[1]
    for d in range(4):
        xb[pl.ds(pl.multiple_of((rank ^ d) * own, 16), own), :] = xs[d][...]
    for e in range(E):
        pick[e * SLOT : (e + 1) * SLOT, :] = select_tile(e, rows_ref)
    width = 512
    for c in range(xb.shape[1] // width):
        lanes = slice(c * width, (c + 1) * width)
        y = dg(pick[...], xb[:, lanes], 1, 0)
        if not (with_ids and c == 0):
            out[:, lanes] = y.astype(BF16)
            continue
        ids = rows_ref[2:4, :].astype(F32).astype(BF16)
        for e in range(E):
            rows = slice(e * SLOT, (e + 1) * SLOT)
            row = dg(ids, select_tile(e, rows_ref, 0), 1, 1)[0:1]
            row = row + dg(ids, select_tile(e, rows_ref, 1), 1, 1)[1:2]
            row = jnp.concatenate([row, jnp.zeros((1, width - SLOT), F32)], axis=1)
            at = lax.broadcasted_iota(jnp.int32, (SLOT, width), 0)
            out[rows, lanes] = jnp.where(at == SLOT - 4, row, y[rows]).astype(BF16)


def eye():
    shape = (SLOT, SLOT)
    return lax.broadcasted_iota(jnp.int32, shape, 0) == lax.broadcasted_iota(jnp.int32, shape, 1)


def row_to_col(row):
    return jnp.sum(jnp.where(eye(), row, 0.0), axis=1, keepdims=True)


def col_to_row(col):
    return jnp.sum(jnp.where(eye(), col, 0.0), axis=0, keepdims=True)


def split_three(value):
    one = value.astype(BF16).astype(F32)
    two = (value - one).astype(BF16).astype(F32)
    return one, two, (value - one - two).astype(BF16).astype(F32)


def expert_slices(ff, x, so, ws, ho, dx, q, fresh):
    for f in range(2):
        gate = dg(x, ws[f][:, :ff], 1, 0)
        up = dg(x, ws[f][:, ff : 2 * ff], 1, 0)
        hidden = dg(so[...], ws[f][:, 2 * ff :], 1, 0)
        sig = 1.0 / (1.0 + jnp.exp(-gate))
        act = gate * sig * up
        q = q + jnp.sum(hidden * act, axis=1, keepdims=True)
        ho[f, :, :ff] = (hidden * up * sig * (1.0 + gate * (1.0 - sig))).astype(BF16)
        ho[f, :, ff : 2 * ff] = (hidden * gate * sig).astype(BF16)
        ho[f, :, 2 * ff :] = act.astype(BF16)
        part = dg(ho[f, :, : 2 * ff], ws[f][:, : 2 * ff], 1, 1)
        dx[...] = part if fresh and f == 0 else dx[...] + part
    return q


def expert_near_kernel(ff, idx_ref, x, gs, w0, w1, gt, so, ho, wo, qo, dx):
    index = idx_ref[0] % E
    logits = dg(x[...], gt[8:16, :].astype(BF16), 1, 1)
    lane = lax.broadcasted_iota(jnp.int32, (SLOT, E), 1)
    weights = []
    for d in range(E):
        rows = slice(d * SLOT, (d + 1) * SLOT)
        part = logits[rows]
        side = gs[(d + 1) * SLOT - 8 : (d + 1) * SLOT, 0:SLOT].astype(F32)
        other = row_to_col(side[4:5]).astype(jnp.int32)
        mine = jnp.sum(jnp.where(lane == index, part, 0.0), axis=1, keepdims=True)
        theirs = jnp.sum(jnp.where(lane == other, part, 0.0), axis=1, keepdims=True)
        weight = 1.0 / (1.0 + jnp.exp(theirs - mine))
        real = lax.broadcasted_iota(jnp.int32, (SLOT, 1), 0) < SLOT - 4
        weight = jnp.where(real, weight, 0.0)
        weights.append(weight)
        so[rows, :] = jnp.where(real, weight * gs[rows, :].astype(F32), 0.0).astype(BF16)
    wo[...] = jnp.concatenate(weights, axis=0)
    qo[...] = expert_slices(ff, x[...], so, (w0, w1), ho, dx, jnp.zeros((E * SLOT, 1), F32), True)


def expert_far_kernel(ff, x, so, w0, w1, q_near, dx_near, ho, dxo, dx):
    dx[...] = dx_near[...]
    q = expert_slices(ff, x[...], so, (w0, w1), ho, dx, q_near[...], False)
    dxo[...] = dx[...].astype(BF16)
    for d in range(E):
        rows = slice(d * SLOT, (d + 1) * SLOT)
        head = dx[rows, 0:128]
        at = lax.broadcasted_iota(jnp.int32, head.shape, 0)
        row = jnp.concatenate([col_to_row(q[rows]), jnp.zeros((1, 128 - SLOT), F32)], axis=1)
        for k, term in enumerate(split_three(row)):
            head = jnp.where(at == SLOT - 4 + k, term, head)
        dxo[rows, 0:128] = head.astype(BF16)


def expert_grad_kernel(ff, x, s, near, far, keep_a, send_a, keep_b, send_b):
    for part, h in ((0, near), (1, far)):
        for f, first, rest in ((0, keep_a, keep_b), (1, send_a, send_b)):
            first[part] = dg(x[...], h[f, :, :ff], 0, 0).astype(BF16)
            rest[part, :, :ff] = dg(x[...], h[f, :, ff : 2 * ff], 0, 0).astype(BF16)
            rest[part, :, ff:] = dg(s[...], h[f, :, 2 * ff :], 0, 0).astype(BF16)


def expert_out_kernel(ff, near, far, weight, w0, w1, w2, w3, out, acc):
    for k, (h, f, w) in enumerate(((near, 0, w0), (near, 1, w1), (far, 0, w2), (far, 1, w3))):
        part = dg(h[f, :, 2 * ff :], w[:, 2 * ff :], 1, 1)
        acc[...] = part if k == 0 else acc[...] + part
    out[...] = (acc[...] * weight[...]).astype(BF16)


def combine_kernel(own, with_q, idx_ref, cols, parts, keep, send, y):
    rank = idx_ref[1]
    width = parts.shape[1]
    y[:, :width] = parts[...]
    if with_q:
        for e in range(E):
            rows = slice(e * SLOT, (e + 1) * SLOT)
            tail = parts[(e + 1) * SLOT - 8 : (e + 1) * SLOT, 0:SLOT].astype(F32)
            lane = lax.broadcasted_iota(jnp.int32, (SLOT, EXTRA), 1)
            side = jnp.zeros((SLOT, EXTRA), F32)
            for k in range(3):
                side = jnp.where(lane == e + 8 * k, row_to_col(tail[4 + k : 5 + k]), side)
            y[rows, width:] = side.astype(BF16)
    slot = lax.broadcasted_iota(jnp.int32, (own, E * SLOT), 1)
    for d in range(4):
        at = pl.ds(pl.multiple_of((rank ^ d) * own, 16), own)
        hit = (cols[at, 0:1] == slot) | (cols[at, 1:2] == slot)
        part = dg(jnp.where(hit, 1.0, 0.0).astype(BF16), y[...], 1, 0)
        (send if d % 2 else keep)[d // 2] = part.astype(BF16)


def middle_back_kernel(mid_ref, a2, g, ids, gt, kept, got, last, grad_mid, branch, small):
    width = mid_ref.shape[1]
    total = kept[...].astype(F32) + got[...].astype(F32) + last[...].astype(F32)
    h2, side = total[:, :width], total[:, width:]
    own = h2.shape[0]
    logits = dg(a2[...], gt[8:16, :].astype(BF16), 1, 1)
    lane = lax.broadcasted_iota(jnp.int32, (own, E), 1)
    q = side[:, 0:8] + side[:, 8:16] + side[:, 16:24]
    hit = [lane == ids[:, k : k + 1] for k in range(2)]
    logit = [jnp.sum(jnp.where(hit[k], logits, 0.0), axis=1, keepdims=True) for k in range(2)]
    terms = [jnp.sum(jnp.where(hit[k], q, 0.0), axis=1, keepdims=True) for k in range(2)]
    both = terms[0] + terms[1]
    logit_grad = jnp.zeros((own, E), F32)
    for k in range(2):
        weight = 1.0 / (1.0 + jnp.exp(logit[1 - k] - logit[k]))
        logit_grad = jnp.where(hit[k], terms[k] - weight * both, logit_grad)
    high = logit_grad.astype(BF16)
    rest = (logit_grad - high.astype(F32)).astype(BF16)
    router = gt[8:16, :].astype(BF16)
    h2 = h2 + dg(high, router, 1, 0) + dg(rest, router, 1, 0)
    mid = mid_ref[...]
    factor = lax.rsqrt(jnp.mean(mid * mid, axis=-1, keepdims=True) + NORM_EPS)
    normed = mid * factor
    u = h2 * gt[0:1, :]
    back = g[...].astype(F32) + factor * (
        u - normed * jnp.mean(u * normed, axis=-1, keepdims=True)
    )
    grad_mid[...] = back
    branch[...] = back.astype(BF16)
    small[...] = jnp.zeros_like(small)
    small[1:2, :] = jnp.sum(h2 * normed, axis=0, keepdims=True)
    small[8:16, :] = dg(high, a2[...], 0, 0) + dg(rest, a2[...], 0, 0)


def weight_grad_kernel(left, right, small, out):
    width = right.shape[1]
    out[:, :width] = dg(left[...], right[...], 0, 0).astype(BF16)
    pad = jnp.zeros((EXTRA - small.shape[0], small.shape[1]), F32)
    side = jnp.transpose(jnp.concatenate([small[...], pad], axis=0))
    out[:, width:] = side.astype(BF16)


def branch_kernel(own, qw, heads, idx_ref, *refs):
    bs = refs[:4]
    att, low, w_late, small = refs[4:8]
    gt, delta, grad, full = refs[8:]
    rank = idx_ref[1]
    for d in range(4):
        full[pl.ds(pl.multiple_of((rank ^ d) * own, 16), own), :] = bs[d][...]
    gt[...] = dg(w_late[:, :qw], full[...], 0, 1).astype(BF16)
    for h in range(heads):
        rows = slice(h * HEAD, (h + 1) * HEAD)
        delta[h : h + 1, :] = jnp.sum(gt[rows, :].astype(F32) * att[rows, :], axis=0, keepdims=True)
    weight_grad_kernel(full, low, small, grad)


def attend_back_kernel(np_, groups, meta_ref, *refs):
    qt, gt, lse, delta, qseg_ref, kseg = refs[:6]
    kvs = refs[6 : 6 + np_]
    dq = refs[6 + np_]
    dkvs = refs[7 + np_ : 7 + 2 * np_]
    kb, vb, kt, dkv = refs[7 + 2 * np_ :]
    span = qt.shape[1]
    half = kb.shape[1]
    kv_heads = half // HEAD
    own_tiles = (np_ - 1) * (span // BLK)
    for d in range(np_):
        at = (np_ - 1 - d) * span
        kb[at : at + span, :] = kvs[d][:, :half]
        vb[at : at + span, :] = kvs[d][:, half:]
        kt[:, at : at + span] = jnp.transpose(kvs[d][:, :half].astype(F32)).astype(BF16)
    dkv[...] = jnp.zeros_like(dkv)

    def q_block(qb, _):
        start = pl.multiple_of(qb * BLK, BLK)
        qs = pl.ds(start, BLK)
        qseg = qseg_ref[:, qs]
        for n in range(kv_heads):
            heads = [n * groups + g for g in range(groups)]
            sl = [slice(h * HEAD, (h + 1) * HEAD) for h in heads]
            q = [qt[r, qs] for r in sl]
            go = [gt[r, qs] for r in sl]
            ls = [lse[h : h + 1, qs] for h in heads]
            de = [delta[h : h + 1, qs] for h in heads]

            def tile(t, masked, carry):
                ks = pl.ds(pl.multiple_of(t * BLK, BLK), BLK)
                lanes = slice(n * HEAD, (n + 1) * HEAD)
                k, v, k_t = kb[ks, lanes], vb[ks, lanes], kt[lanes, ks]
                ok = allowed_mask(t, start, own_tiles, qseg, kseg) if masked else None
                out = []
                dk = dv = None
                for g in range(groups):
                    p = jnp.exp(dg(k, q[g], 1, 0) - ls[g])
                    if masked:
                        p = jnp.where(ok, p, 0.0)
                    ds = (p * (dg(v, go[g], 1, 0) - de[g])).astype(BF16)
                    one = dg(q[g], ds, 1, 1)
                    two = dg(go[g], p.astype(BF16), 1, 1)
                    dk = one if dk is None else dk + one
                    dv = two if dv is None else dv + two
                    out.append(carry[g] + dg(k_t, ds, 1, 0))
                dkv[n * HEAD : (n + 1) * HEAD, ks] += dk
                dkv[half + n * HEAD : half + (n + 1) * HEAD, ks] += dv
                return tuple(out)

            init = tuple(jnp.zeros((HEAD, BLK), F32) for _ in range(groups))
            done = tile_loop(meta_ref, qb, own_tiles, tile, init)
            for g in range(groups):
                dq[sl[g], qs] = (done[g] * (HEAD**-0.5)).astype(BF16)
        return 0

    lax.fori_loop(0, span // BLK, q_block, 0)
    for d in range(np_):
        at = (np_ - 1 - d) * span
        dkvs[d][...] = dkv[:, at : at + span].astype(dkvs[d].dtype)


def input_back_kernel(np_, own, idx_ref, *refs):
    dq, w, a1, gain_ref = refs[:4]
    dkvs = refs[4 : 4 + np_]
    keep, send, nat, small = refs[4 + np_ :]
    rank = idx_ref[1]
    total = dkvs[0][...]
    for d in range(1, np_):
        total = total + dkvs[d][...].astype(F32)
    qw = dq.shape[0]
    nat[:, :qw] = jnp.transpose(dq[...].astype(F32)).astype(BF16)
    nat[:, qw:] = jnp.transpose(total).astype(BF16)
    gain = jnp.zeros((1, w.shape[0]), F32)
    for d in range(4):
        rows = pl.ds(pl.multiple_of((rank ^ d) * own, 16), own)
        part = dg(nat[rows, :], w[...], 1, 1)
        gain = gain + jnp.sum(part * a1[rows, :].astype(F32), axis=0, keepdims=True)
        (send if d % 2 else keep)[d // 2] = part.astype(BF16)
    small[...] = jnp.zeros_like(small)
    small[0:1, :] = gain / gain_ref[...]


def input_grad_kernel(x, gain, grad_mid, kept, got, last, out):
    h1 = kept[...].astype(F32) + got[...].astype(F32) + last[...].astype(F32)
    v = x[...].astype(F32)
    factor = lax.rsqrt(jnp.mean(v * v, axis=-1, keepdims=True) + NORM_EPS)
    normed = v * factor
    u = h1 * gain[...]
    out[...] = grad_mid[...] + factor * (
        u - normed * jnp.mean(u * normed, axis=-1, keepdims=True)
    )


def expert_unpack_kernel(ff, first, rest, gateup, down):
    for e in range(E):
        gateup[e, :, 0, :] = first[e].astype(F32)
        gateup[e, :, 1, :] = rest[e, :, :ff].astype(F32)
        down[e] = rest[e, :, ff:].astype(F32)


def route_slots(expert_ids):
    listed = jnp.concatenate([expert_ids[:, 0], expert_ids[:, 1]])
    onehot = (listed[:, None] == jnp.arange(E, dtype=jnp.int32)[None, :]).astype(jnp.int32)
    earlier = jnp.cumsum(onehot, axis=0) - onehot
    return jnp.sum(earlier * onehot, axis=1).reshape(2, -1)


def per_device(
    hidden_in,
    attn_gain,
    query_proj,
    key_value_projection,
    output_proj,
    moe_gain,
    router_proj,
    gateup_proj,
    down_proj,
    segment_index_list,
    expert_ids,
    out_grad,
):
    n_dp, n_tensor = lax.axis_size("dp"), lax.axis_size("tensor")
    own, width = hidden_in.shape
    span = own * n_tensor
    rows = query_proj.shape[0]
    qw = query_proj.shape[1]
    kvw = 2 * key_value_projection.shape[2]
    groups = 2 * qw // kvw
    ff = gateup_proj.shape[3]
    n_groups = n_dp // E
    dp_groups = None
    if n_groups > 1:
        dp_groups = [list(range(g * E, (g + 1) * E)) for g in range(n_groups)]
    dp, rank = lax.axis_index("dp"), lax.axis_index("tensor")
    idx = jnp.stack([dp, rank]).astype(jnp.int32)

    pad = jnp.zeros((8, qw + kvw - rows), BF16)
    first_gain = jnp.concatenate([jnp.broadcast_to(attn_gain[None, :], (8, rows)), pad], axis=1)
    early = jnp.concatenate([query_proj, key_value_projection.reshape(rows, kvw)], axis=1)
    early = jnp.concatenate([early, first_gain], axis=0)
    x_parts, g_parts = [hidden_in, swap(hidden_in, "tensor", 1)], [out_grad]

    def between(step, piece):
        if step == 3:
            two = after(x_parts.pop(), piece)
            x_parts.extend([two, swap(two, "tensor", 1)])
            g_parts.append(swap(after(out_grad, piece), "tensor", 1))
            g_parts.append(swap(after(out_grad, piece), "tensor", 2))

    x_parts.append(swap(hidden_in, "tensor", 2))
    pieces, source = ring_gather(early, "dp", between)
    g_parts.append(swap(after(g_parts[2], pieces[-1]), "tensor", 1))
    w_early, gain_one, a1, qt, kv = kcall(
        "qkv",
        functools.partial(qkv_kernel, len(pieces), own, rows, qw),
        [
            sds((width, qw + kvw), BF16),
            sds((1, width), F32),
            sds((span, width), BF16),
            sds((qw, span), BF16),
            sds((span, kvw), BF16),
        ],
        [source, idx],
        pieces + x_parts,
        [
            pltpu.VMEM((span, width), BF16),
            pltpu.VMEM((span, qw), F32),
            pltpu.VMEM((n_dp, rows), F32),
        ],
        flops=2 * span * width * (qw + kvw),
    )
    late = jnp.concatenate(
        [
            output_proj.T,
            moe_gain[:, None],
            jnp.zeros((rows, 7), BF16),
            router_proj,
            jnp.zeros((rows, EXTRA - 16), BF16),
        ],
        axis=1,
    )
    w_late = lax.all_gather(after(late, pieces[-1]), "dp", axis=0, tiled=True)

    position = route_slots(expert_ids)
    per_rank = CAP // n_tensor
    local = position - rank * per_rank
    ids_t = expert_ids.T
    slots = jnp.where(
        (local >= 0) & (local < per_rank) & (position < CAP), ids_t * SLOT + local, -1
    ).astype(jnp.int32)
    slot_rows = jnp.concatenate([slots, ids_t[::-1], jnp.zeros((4, span), jnp.int32)], axis=0)
    slot_cols = slots.T
    ids_own = lax.dynamic_slice_in_dim(expert_ids, rank * own, own, 0)

    def dispatch(parts, with_ids):
        (tiles_,) = kcall(
            "dispatch",
            functools.partial(dispatch_kernel, own, with_ids),
            [sds((E * SLOT, width), BF16)],
            [idx],
            [slot_rows] + parts,
            [pltpu.VMEM((span, width), BF16), pltpu.VMEM((E * SLOT, span), BF16)],
            flops=2 * E * SLOT * span * width,
        )
        return tiles_

    g_tiles = dispatch(g_parts, True)

    longest = segment_index_list.shape[0] // 4
    reach = min(SEQ_SPANS - 1, -(-(longest - 1) // span))
    n_pieces = reach + 1
    tiles = span // BLK
    padded = jnp.concatenate([jnp.full((reach * span,), -1, jnp.int32), segment_index_list])
    window = lax.dynamic_slice_in_dim(padded, dp * span, n_pieces * span, 0)
    seg_mine = window[reach * span :]
    valid = jnp.minimum(dp % SEQ_SPANS, reach)
    first_seg, last_seg = seg_mine[::BLK], seg_mine[BLK - 1 :: BLK]
    low_tile = jnp.sum(window[None, :] < first_seg[:, None], axis=1) // BLK
    low_tile = jnp.maximum(low_tile, (reach - valid) * tiles)
    full_tile = -(-jnp.sum(window[None, :] < last_seg[:, None], axis=1) // BLK)
    meta = jnp.stack([low_tile, full_tile]).astype(jnp.int32)
    kseg, qseg = window[:, None], seg_mine[None, :]

    kvs = [kv] + [shifted(kv, "dp", d) for d in range(1, n_pieces)]

    packed = jnp.concatenate(
        [gateup_proj[:, :, 0], gateup_proj[:, :, 1], jnp.transpose(down_proj, (0, 2, 1))], axis=2
    )
    near = exchange(after(packed, *kvs[1:]), dp_groups)
    w_expert = near.reshape(E * rows, 3 * ff)
    if n_groups > 1:
        shape = (n_groups, E * rows, 3 * ff)
        whole = jnp.zeros(shape, BF16)
        for h in range(n_groups):
            part = w_expert if h == 0 else swap(near.reshape(E * rows, 3 * ff), "dp", h * E)
            whole = lax.dynamic_update_index_in_dim(whole, part, (dp // E) ^ h, 0)
        w_expert = whole.reshape(width, 3 * ff)
    w_core = swap(w_expert, "tensor", 1)
    g_slots = exchange(after(g_tiles, w_expert), dp_groups)

    att, lse, low = kcall(
        "attend",
        functools.partial(attend_kernel, n_pieces, groups),
        [sds((qw, span), F32), sds((8, span), F32), sds((span, qw), BF16)],
        [meta],
        [qt, qseg, kseg] + kvs,
        [
            pltpu.VMEM((n_pieces * span, kvw // 2), BF16),
            pltpu.VMEM((kvw // 2, n_pieces * span), BF16),
        ],
        flops=2 * span * span * 2 * qw * 2,
    )
    keep, send, gt = kcall(
        "project",
        functools.partial(project_kernel, own, qw),
        [
            sds((2, own, width), BF16),
            sds((2, own, width), BF16),
            sds((16, width), F32),
        ],
        [idx],
        [low, w_late],
        flops=2 * span * width * qw,
    )
    middle, a2 = kcall(
        "middle",
        middle_kernel,
        [sds((own, width), F32), sds((own, width), BF16)],
        [],
        [hidden_in, gt] + list(scatter_tensor(keep, send)),
    )

    a2_parts = gather_tensor(a2)
    w_across = swap(after(w_expert, a2_parts[2]), "tensor", 2)
    w_across_core = swap(w_across, "tensor", 1)
    x_slots = exchange(after(dispatch(a2_parts, False), g_slots), dp_groups)
    n_slots = E * SLOT
    s_slots, h_near, slot_weight, q_near, dx_near = kcall(
        "expert_near",
        functools.partial(expert_near_kernel, ff),
        [
            sds((n_slots, width), BF16),
            sds((2, n_slots, 3 * ff), BF16),
            sds((n_slots, 1), F32),
            sds((n_slots, 1), F32),
            sds((n_slots, width), F32),
        ],
        [idx],
        [x_slots, g_slots, w_expert, w_core, gt],
        flops=2 * n_slots * width * 2 * 5 * ff,
    )
    h_far, dx = kcall(
        "expert_far",
        functools.partial(expert_far_kernel, ff),
        [sds((2, n_slots, 3 * ff), BF16), sds((n_slots, width), BF16)],
        [],
        [x_slots, s_slots, w_across, w_across_core, q_near, dx_near],
        [pltpu.VMEM((n_slots, width), F32)],
        flops=2 * n_slots * width * 2 * 5 * ff,
    )
    dx_back = exchange(dx, dp_groups)
    keep_a, send_a, keep_b, send_b = kcall(
        "expert_grad",
        functools.partial(expert_grad_kernel, ff),
        [sds((2, width, ff), BF16)] * 2 + [sds((2, width, 2 * ff), BF16)] * 2,
        [],
        [x_slots, s_slots, h_near, h_far],
        flops=2 * n_slots * width * 4 * 3 * ff,
    )
    got_a, got_b = swap(send_a, "tensor", 1), swap(send_b, "tensor", 1)
    second_a = (keep_a[1].astype(F32) + got_a[1].astype(F32)).astype(BF16)
    second_b = (keep_b[1].astype(F32) + got_b[1].astype(F32)).astype(BF16)
    last_a = swap(second_a, "tensor", 2)
    (out_slots,) = kcall(
        "expert_out",
        functools.partial(expert_out_kernel, ff),
        [sds((n_slots, width), BF16)],
        [],
        [h_near, h_far, slot_weight, w_expert, w_core, w_across, w_across_core],
        [pltpu.VMEM((n_slots, width), F32)],
        flops=2 * n_slots * width * 4 * ff,
    )
    dx_back = after(dx_back, second_a, out_slots)
    out_back = exchange(after(out_slots, dx_back), dp_groups)

    def combine(parts_, with_q):
        wide = width + (EXTRA if with_q else 0)
        return scatter_tensor(
            *kcall(
                "combine",
                functools.partial(combine_kernel, own, with_q),
                [sds((2, own, wide), BF16)] * 2,
                [idx],
                [slot_cols, parts_],
                [pltpu.VMEM((E * SLOT, wide), BF16)],
                flops=2 * E * SLOT * span * width,
            )
        )

    back_terms = list(combine(dx_back, True))
    back_terms[0] = after(back_terms[0], second_b, last_a)
    grad_middle, branch, small_two = kcall(
        "middle_back",
        middle_back_kernel,
        [sds((own, width), F32), sds((own, width), BF16), sds((16, width), F32)],
        [],
        [middle, a2, out_grad, ids_own, gt] + list(back_terms),
    )
    def own_grad(kept, got, last, *others):
        total = (kept.astype(F32) + got.astype(F32) + last.astype(F32)).astype(BF16)
        if n_groups > 1:
            group = dp // E
            blocks = total.reshape(n_groups, E * rows, -1)
            total = lax.dynamic_index_in_dim(blocks, group, 0, keepdims=False).astype(F32)
            for h in range(1, n_groups):
                there = lax.dynamic_index_in_dim(blocks, group ^ h, 0, keepdims=False)
                total = total + swap(there, "dp", h * E).astype(F32)
            total = total.astype(BF16)
        return exchange(after(total.reshape(E, rows, -1), *others), dp_groups)

    branch_parts = gather_tensor(branch)
    own_a = own_grad(keep_a[0], got_a[0], last_a, out_back)
    last_b = swap(after(second_b, branch_parts[2]), "tensor", 2)

    heads = qw // HEAD
    g_heads, delta, out_part = kcall(
        "branch",
        functools.partial(branch_kernel, own, qw, heads),
        [sds((qw, span), BF16), sds((8, span), F32), sds((width, qw + EXTRA), BF16)],
        [idx],
        branch_parts + [att, low, w_late, small_two],
        [pltpu.VMEM((span, width), BF16)],
        flops=4 * span * width * qw,
    )
    out_sum = lax.psum_scatter(out_part, "dp", scatter_dimension=0, tiled=True).astype(F32)
    outs = kcall(
        "attend_back",
        functools.partial(attend_back_kernel, n_pieces, groups),
        [sds((qw, span), BF16), sds((kvw, span), F32)] + [sds((kvw, span), BF16)] * reach,
        [meta],
        [qt, g_heads, lse, delta, qseg, kseg] + kvs,
        [
            pltpu.VMEM((n_pieces * span, kvw // 2), BF16),
            pltpu.VMEM((n_pieces * span, kvw // 2), BF16),
            pltpu.VMEM((kvw // 2, n_pieces * span), BF16),
            pltpu.VMEM((kvw, n_pieces * span), F32),
        ],
        flops=5 * span * span * 2 * qw * 2,
    )
    dq = outs[0]
    dkvs = [outs[1]] + [shifted(outs[1 + d], "dp", -d) for d in range(1, n_pieces)]
    dkvs[-1] = after(dkvs[-1], own_a, last_b)
    own_b = own_grad(keep_b[0], got_b[0], last_b, own_a)

    keep_h, send_h, nat, small_one = kcall(
        "input_back",
        functools.partial(input_back_kernel, n_pieces, own),
        [
            sds((2, own, width), BF16),
            sds((2, own, width), BF16),
            sds((span, qw + kvw), BF16),
            sds((16, width), F32),
        ],
        [idx],
        [dq, w_early, a1, gain_one] + dkvs,
        flops=2 * span * width * (qw + kvw),
    )
    in_terms = scatter_tensor(keep_h, send_h)
    (in_part,) = kcall(
        "weight_grad",
        weight_grad_kernel,
        [sds((width, qw + kvw + EXTRA), BF16)],
        [],
        [a1, nat, small_one],
        flops=2 * span * width * (qw + kvw),
    )
    in_parts = exchange(after(in_part, out_sum, own_b))
    in_sum = jnp.sum(in_parts.reshape(n_dp, rows, -1).astype(F32), axis=0)
    (input_grad,) = kcall(
        "input_grad",
        input_grad_kernel,
        [sds((own, width), F32)],
        [],
        [hidden_in, gain_one, grad_middle] + list(in_terms),
    )

    side = out_sum[:, qw : qw + 16] + in_sum[:, qw + kvw : qw + kvw + 16]
    side = side + swap(side, "tensor", 1)
    side = side + swap(side, "tensor", 2)
    out_terms = combine(after(out_back, dq), False)
    hidden_out = (middle + sum(t.astype(F32) for t in out_terms)).astype(BF16)
    gateup_grad, down_grad = kcall(
        "expert_unpack",
        functools.partial(expert_unpack_kernel, ff),
        [sds((E, rows, 2, ff), F32), sds((E, rows, ff), F32)],
        [],
        [own_a, own_b],
    )
    return (
        hidden_out,
        input_grad,
        side[:, 0],
        in_sum[:, :qw],
        in_sum[:, qw : qw + kvw].reshape(rows, 2, kvw // 2),
        out_sum[:, :qw].T,
        side[:, 1],
        side[:, 8:16],
        gateup_grad,
        jnp.transpose(down_grad, (0, 2, 1)),
    )


def solution(mesh):
    return jax.shard_map(
        per_device,
        mesh=mesh,
        in_specs=(
            P(("dp", "tensor"), None),
            P("dp"),
            P("dp", "tensor"),
            P("dp", None, "tensor"),
            P("tensor", "dp"),
            P("dp"),
            P("dp", None),
            P(None, "dp", None, "tensor"),
            P(None, "tensor", "dp"),
            P(),
            P("dp", None),
            P(("dp", "tensor"), None),
        ),
        out_specs=(
            P(("dp", "tensor"), None),
            P(("dp", "tensor"), None),
            P("dp"),
            P("dp", "tensor"),
            P("dp", None, "tensor"),
            P("tensor", "dp"),
            P("dp"),
            P("dp", None),
            P(None, "dp", None, "tensor"),
            P(None, "tensor", "dp"),
        ),
        check_vma=False,
    )
```

```python
import functools

import jax
import jax.numpy as jnp
from jax import lax
from jax.experimental import pallas as pl
from jax.experimental.pallas import tpu as pltpu
from jax.sharding import PartitionSpec as P

HEAD = 64
E = 8
SEQ_SPANS = 8
CAP = 240
SLOT = 64
BLK = 256
EXTRA = 128

NORM_EPS = 1e-05
NEG = -1e30

F32 = jnp.float32
BF16 = jnp.bfloat16


def dg(a, b, ca, cb):
    return lax.dot_general(a, b, (((ca,), (cb,)), ((), ())), preferred_element_type=F32)


def sds(shape, dtype):
    return jax.ShapeDtypeStruct(shape, dtype)


TIMES = {
    "qkv": 7,
    "attend_own": 14,
    "attend_far": 20,
    "project": 4,
    "middle": 3,
    "dispatch": 4,
    "expert": 17,
    "expert_grad": 3,
    "expert_out": 3,
    "combine": 12,
    "middle_back": 5,
    "branch": 6,
    "attend_back_far": 20,
    "attend_back_own": 14,
    "query_grad": 4,
    "input_back": 7,
    "keyval_grad": 4,
    "input_grad": 4,
    "expert_unpack": 5,
}


def kcall(name, body, outs, smem, vmem, scratch=(), limit=60):
    return pl.pallas_call(
        body,
        name=name,
        out_shape=list(outs),
        in_specs=[pl.BlockSpec(memory_space=pltpu.SMEM)] * len(smem)
        + [pl.BlockSpec(memory_space=pltpu.VMEM)] * len(vmem),
        out_specs=[pl.BlockSpec(memory_space=pltpu.VMEM)] * len(outs),
        scratch_shapes=list(scratch),
        compiler_params=pltpu.CompilerParams(vmem_limit_bytes=limit << 20),
        cost_estimate=pl.CostEstimate(
            flops=TIMES[name] * 10**9, bytes_accessed=10**6, transcendentals=0
        ),
    )(*smem, *vmem)


def swap(value, axis, by):
    size = lax.axis_size(axis)
    return lax.ppermute(value, axis, [(i, i ^ by) for i in range(size)])


def shifted(value, axis, by):
    size = lax.axis_size(axis)
    return lax.ppermute(value, axis, [(i, i + by) for i in range(size) if 0 <= i + by < size])


def gather_tensor(value):
    one = swap(value, "tensor", 1)
    two = swap(value, "tensor", 2)
    return [value, one, two, swap(two, "tensor", 1)]


def scatter_tensor(keep, other, send):
    got = swap(send, "tensor", 1)
    second = (other.astype(F32) + got[1].astype(F32)).astype(BF16)
    return [keep, got, swap(second, "tensor", 2)]


def three(kept, got, last):
    return kept[...].astype(F32) + got[0].astype(F32) + last[...].astype(F32)


def ring_pos(index, size):
    return jnp.where(index % 2 == 0, index // 2, size - 1 - (index - 1) // 2)


def ring_dev(pos, size):
    pos = pos % size
    return jnp.where(pos < size // 2, 2 * pos, 2 * (size - 1 - pos) + 1)


def ring_gather(value, axis, meanwhile):
    size = lax.axis_size(axis)
    order = list(range(0, size, 2)) + list(range(size - 1, 0, -2))
    ahead = [(order[k], order[(k + 1) % size]) for k in range(size)]
    back = [(b, a) for a, b in ahead]
    half = value.shape[0] // 16 * 8
    index = lax.axis_index(axis)
    pos = ring_pos(index, size)
    pieces, source = [value], [index]
    one = two = value
    for step in range(1, size // 2 + 1):
        last = step == size // 2
        got_one = lax.ppermute(one[:half] if last else one, axis, ahead)
        got_two = lax.ppermute(two[half:] if last else two, axis, back)
        done = meanwhile(step, one)
        one, two = (after(got_one, *done), got_two) if done else (got_one, got_two)
        pieces += [one, two]
        source += [ring_dev(pos - step, size), ring_dev(pos + step, size)]
    return pieces, jnp.stack(source).astype(jnp.int32)


def exchange(value, groups=None):
    return lax.all_to_all(
        value, "dp", split_axis=0, concat_axis=0, axis_index_groups=groups, tiled=True
    )


def after(value, *others):
    return lax.optimization_barrier((value,) + others)[0]


def qkv_kernel(n, own, rows, qw, cols, src_ref, idx_ref, *refs):
    pieces = refs[:n]
    xs = refs[n : n + 4]
    w, wo, gt, a1, qt, kv, xb, qn, gs = refs[n + 4 :]
    rank = idx_ref[1]
    for k in range(n):
        piece = pieces[k]
        first = pieces[n - 2].shape[0] if k == n - 1 else 0
        last = min(first + piece.shape[0], rows)
        at = pl.ds(pl.multiple_of(src_ref[k] * rows + first, 8), last - first)
        w[at, :] = piece[: last - first, :cols]
        wo[at, :] = piece[: last - first, cols:]
        if first + piece.shape[0] > rows:
            gs[pl.ds(src_ref[k], 1)] = piece[last - first :, :rows].astype(F32)[None]
    for d in range(4):
        xb[pl.ds(pl.multiple_of((rank ^ d) * own, 16), own), :] = xs[d][...]
    gt[...] = jnp.concatenate([gs[j] for j in range(gs.shape[0])], axis=1)

    def block(j, _):
        at = pl.ds(pl.multiple_of(j * own, 16), own)
        x = xb[at, :].astype(F32)
        factor = lax.rsqrt(jnp.mean(x * x, axis=-1, keepdims=True) + NORM_EPS)
        a = (x * factor * gt[0:1, :]).astype(BF16)
        a1[at, :] = a
        y = dg(a, w[...], 1, 0)
        qn[at, :] = y[:, :qw] * (HEAD**-0.5)
        kv[at, :] = y[:, qw:].astype(BF16)
        return 0

    lax.fori_loop(0, 4, block, 0)
    qt[...] = jnp.transpose(qn[...]).astype(BF16)


def tile_loop(meta_ref, qb, end, body, carry):
    low, full = meta_ref[0, qb], meta_ref[1, qb]
    carry = lax.fori_loop(low, jnp.minimum(full, end), lambda t, c: body(t, True, c), carry)
    return lax.fori_loop(jnp.maximum(full, low), end, lambda t, c: body(t, False, c), carry)


def allowed_mask(t, start, diag, qseg, kseg):
    ok = kseg[pl.ds(pl.multiple_of(t * BLK, BLK), BLK), :] == qseg
    if diag:
        keys = lax.broadcasted_iota(jnp.int32, (BLK, BLK), 0)
        ok = ok & (keys <= lax.broadcasted_iota(jnp.int32, (BLK, BLK), 1))
    return ok


def attend_kernel(np_, groups, local, meta_ref, *refs):
    qt, qseg_ref, kseg = refs[:3]
    kvs = refs[3 : 3 + np_]
    if local:
        acc_ref, m_ref, l_ref, kb, vt = refs[3 + np_ :]
    else:
        acc_in, m_in, l_in, att, lse, low, kb, vt = refs[3 + np_ :]
    span = qt.shape[1]
    half = kb.shape[1]
    kv_heads = half // HEAD
    for d in range(np_):
        at = (np_ - 1 - d) * span
        kb[at : at + span, :] = kvs[d][:, :half]
        vt[:, at : at + span] = jnp.transpose(kvs[d][:, half:].astype(F32)).astype(BF16)

    def q_block(qb, _):
        start = pl.multiple_of(qb * BLK, BLK)
        qs = pl.ds(start, BLK)
        qseg = qseg_ref[:, qs]
        for n in range(kv_heads):
            heads = [n * groups + g for g in range(groups)]
            sl = [slice(h * HEAD, (h + 1) * HEAD) for h in heads]
            q = [qt[r, qs] for r in sl]

            def tile(t, masked, carry, diag=False):
                ks = pl.ds(pl.multiple_of(t * BLK, BLK), BLK)
                k = kb[ks, n * HEAD : (n + 1) * HEAD]
                v = vt[n * HEAD : (n + 1) * HEAD, ks]
                ok = allowed_mask(t, start, diag, qseg, kseg) if masked else None
                out = []
                for g in range(groups):
                    m, l, acc = carry[g]
                    s = dg(k, q[g], 1, 0)
                    if masked:
                        s = jnp.where(ok, s, NEG)
                    m_new = jnp.maximum(m, jnp.max(s, axis=0, keepdims=True))
                    e = jnp.exp(s - m_new)
                    shrink = jnp.exp(m - m_new)
                    l = l * shrink + jnp.sum(e, axis=0, keepdims=True)
                    acc = acc * shrink + dg(v, e.astype(BF16), 1, 0)
                    out.append((m_new, l, acc))
                return tuple(out)

            if local:
                none = jnp.full((1, BLK), NEG, F32)
                init = (none, jnp.zeros((1, BLK), F32), jnp.zeros((HEAD, BLK), F32))
                state = tile(qb, True, (init,) * groups, True)
                state = tile_loop(meta_ref, qb, qb, tile, state)
                for g in range(groups):
                    h = heads[g]
                    m_ref[h : h + 1, qs], l_ref[h : h + 1, qs], acc_ref[sl[g], qs] = state[g]
            else:
                state = tuple(
                    (m_in[h : h + 1, qs], l_in[h : h + 1, qs], acc_in[r, qs])
                    for h, r in zip(heads, sl)
                )
                state = tile_loop(meta_ref, qb, np_ * (span // BLK), tile, state)
                for g in range(groups):
                    m, l, acc = state[g]
                    att[sl[g], qs] = acc / l
                    lse[heads[g] : heads[g] + 1, qs] = m + jnp.log(l)
        return 0

    lax.fori_loop(0, span // BLK, q_block, 0)
    if not local:
        low[...] = jnp.transpose(att[...]).astype(BF16)


def put_quarter(d, part, keep, other, send):
    if d % 2:
        send[d // 2] = part.astype(BF16)
    else:
        (other if d else keep)[...] = part.astype(BF16)


def project_kernel(own, idx_ref, low, wo, keep, other, send):
    rank = idx_ref[1]
    for d in range(4):
        rows = pl.ds(pl.multiple_of((rank ^ d) * own, 16), own)
        put_quarter(d, dg(low[rows, :], wo[...], 1, 1), keep, other, send)


def middle_kernel(x, gt, kept, got, last, middle, a2):
    mid = x[...].astype(F32) + three(kept, got, last)
    middle[...] = mid
    factor = lax.rsqrt(jnp.mean(mid * mid, axis=-1, keepdims=True) + NORM_EPS)
    a2[...] = (mid * factor * gt[1:2, :]).astype(BF16)


def select_tile(e, rows_ref, k=None):
    slot = e * SLOT + lax.broadcasted_iota(jnp.int32, (SLOT, rows_ref.shape[1]), 0)
    first, second = slot == rows_ref[0:1, :], slot == rows_ref[1:2, :]
    hit = (first | second) if k is None else (second if k else first)
    return jnp.where(hit, 1.0, 0.0).astype(BF16)


def dispatch_kernel(own, with_ids, idx_ref, rows_ref, *refs):
    xs, out = refs[:4], refs[4]
    xb, pick = refs[5:]
    rank = idx_ref[1]
    for d in range(4):
        xb[pl.ds(pl.multiple_of((rank ^ d) * own, 16), own), :] = xs[d][...]
    for e in range(E):
        pick[e * SLOT : (e + 1) * SLOT, :] = select_tile(e, rows_ref)
    width = 512
    for c in range(xb.shape[1] // width):
        lanes = slice(c * width, (c + 1) * width)
        y = dg(pick[...], xb[:, lanes], 1, 0)
        if not (with_ids and c == 0):
            out[:, lanes] = y.astype(BF16)
            continue
        ids = rows_ref[2:4, :].astype(F32).astype(BF16)
        for e in range(E):
            rows = slice(e * SLOT, (e + 1) * SLOT)
            row = dg(ids, select_tile(e, rows_ref, 0), 1, 1)[0:1]
            row = row + dg(ids, select_tile(e, rows_ref, 1), 1, 1)[1:2]
            row = jnp.concatenate([row, jnp.zeros((1, width - SLOT), F32)], axis=1)
            at = lax.broadcasted_iota(jnp.int32, (SLOT, width), 0)
            out[rows, lanes] = jnp.where(at == SLOT - 4, row, y[rows]).astype(BF16)


def eye():
    shape = (SLOT, SLOT)
    return lax.broadcasted_iota(jnp.int32, shape, 0) == lax.broadcasted_iota(jnp.int32, shape, 1)


def row_to_col(row):
    return jnp.sum(jnp.where(eye(), row, 0.0), axis=1, keepdims=True)


def col_to_row(col):
    return jnp.sum(jnp.where(eye(), col, 0.0), axis=0, keepdims=True)


def split_three(value):
    one = value.astype(BF16).astype(F32)
    two = (value - one).astype(BF16).astype(F32)
    return one, two, (value - one - two).astype(BF16).astype(F32)


def expert_kernel(ff, idx_ref, x_ref, gs, w0, w1, w2, w3, gt, so, ho, wo, dxo, dx):
    index = idx_ref[0] % E
    x = x_ref[...]
    logits = dg(x, gt[8:16, :].astype(BF16), 1, 1)
    lane = lax.broadcasted_iota(jnp.int32, (SLOT, E), 1)
    weights = []
    for d in range(E):
        rows = slice(d * SLOT, (d + 1) * SLOT)
        part = logits[rows]
        side = gs[(d + 1) * SLOT - 8 : (d + 1) * SLOT, 0:SLOT].astype(F32)
        other = row_to_col(side[4:5]).astype(jnp.int32)
        mine = jnp.sum(jnp.where(lane == index, part, 0.0), axis=1, keepdims=True)
        theirs = jnp.sum(jnp.where(lane == other, part, 0.0), axis=1, keepdims=True)
        weight = 1.0 / (1.0 + jnp.exp(theirs - mine))
        real = lax.broadcasted_iota(jnp.int32, (SLOT, 1), 0) < SLOT - 4
        weight = jnp.where(real, weight, 0.0)
        weights.append(weight)
        so[rows, :] = jnp.where(real, weight * gs[rows, :].astype(F32), 0.0).astype(BF16)
    wo[...] = jnp.concatenate(weights, axis=0)
    q = jnp.zeros((E * SLOT, 1), F32)
    for f, w in enumerate((w0, w1, w2, w3)):
        gate = dg(x, w[:, :ff], 1, 0)
        up = dg(x, w[:, ff : 2 * ff], 1, 0)
        hidden = dg(so[...], w[:, 2 * ff :], 1, 0)
        sig = 1.0 / (1.0 + jnp.exp(-gate))
        act = gate * sig * up
        q = q + jnp.sum(hidden * act, axis=1, keepdims=True)
        ho[f, :, :ff] = (hidden * up * sig * (1.0 + gate * (1.0 - sig))).astype(BF16)
        ho[f, :, ff : 2 * ff] = (hidden * gate * sig).astype(BF16)
        ho[f, :, 2 * ff :] = act.astype(BF16)
        part = dg(ho[f, :, : 2 * ff], w[:, : 2 * ff], 1, 1)
        dx[...] = part if f == 0 else dx[...] + part
    dxo[...] = dx[...].astype(BF16)
    for d in range(E):
        rows = slice(d * SLOT, (d + 1) * SLOT)
        head = dx[rows, 0:128]
        at = lax.broadcasted_iota(jnp.int32, head.shape, 0)
        row = jnp.concatenate([col_to_row(q[rows]), jnp.zeros((1, 128 - SLOT), F32)], axis=1)
        for k, term in enumerate(split_three(row)):
            head = jnp.where(at == SLOT - 4 + k, term, head)
        dxo[rows, 0:128] = head.astype(BF16)


def expert_grad_kernel(ff, cut, first, x, s, h, *outs):
    for f in range(4):
        out = outs[f]
        if first:
            out[...] = dg(x[...], h[f, :, :cut], 0, 0).astype(BF16)
        else:
            out[:, : 2 * ff - cut] = dg(x[...], h[f, :, cut : 2 * ff], 0, 0).astype(BF16)
            out[:, 2 * ff - cut :] = dg(s[...], h[f, :, 2 * ff :], 0, 0).astype(BF16)


def expert_out_kernel(ff, h, weight, w0, w1, w2, w3, out, acc):
    for f, w in enumerate((w0, w1, w2, w3)):
        part = dg(h[f, :, 2 * ff :], w[:, 2 * ff :], 1, 1)
        acc[...] = part if f == 0 else acc[...] + part
    out[...] = (acc[...] * weight[...]).astype(BF16)


def combine_kernel(own, with_q, idx_ref, cols, parts, keep, other, send, y):
    rank = idx_ref[1]
    width = parts.shape[1]
    y[:, :width] = parts[...]
    if with_q:
        for e in range(E):
            rows = slice(e * SLOT, (e + 1) * SLOT)
            tail = parts[(e + 1) * SLOT - 8 : (e + 1) * SLOT, 0:SLOT].astype(F32)
            lane = lax.broadcasted_iota(jnp.int32, (SLOT, EXTRA), 1)
            side = jnp.zeros((SLOT, EXTRA), F32)
            for k in range(3):
                side = jnp.where(lane == e + 8 * k, row_to_col(tail[4 + k : 5 + k]), side)
            y[rows, width:] = side.astype(BF16)
    slot = lax.broadcasted_iota(jnp.int32, (own, E * SLOT), 1)
    for d in range(4):
        at = pl.ds(pl.multiple_of((rank ^ d) * own, 16), own)
        hit = (cols[at, 0:1] == slot) | (cols[at, 1:2] == slot)
        part = dg(jnp.where(hit, 1.0, 0.0).astype(BF16), y[...], 1, 0)
        put_quarter(d, part, keep, other, send)


def middle_back_kernel(mid_ref, a2, g, ids, gt, kept, got, last, grad_mid, branch, small):
    width = mid_ref.shape[1]
    total = three(kept, got, last)
    h2, side = total[:, :width], total[:, width:]
    own = h2.shape[0]
    logits = dg(a2[...], gt[8:16, :].astype(BF16), 1, 1)
    lane = lax.broadcasted_iota(jnp.int32, (own, E), 1)
    q = side[:, 0:8] + side[:, 8:16] + side[:, 16:24]
    hit = [lane == ids[:, k : k + 1] for k in range(2)]
    logit = [jnp.sum(jnp.where(hit[k], logits, 0.0), axis=1, keepdims=True) for k in range(2)]
    terms = [jnp.sum(jnp.where(hit[k], q, 0.0), axis=1, keepdims=True) for k in range(2)]
    both = terms[0] + terms[1]
    logit_grad = jnp.zeros((own, E), F32)
    for k in range(2):
        weight = 1.0 / (1.0 + jnp.exp(logit[1 - k] - logit[k]))
        logit_grad = jnp.where(hit[k], terms[k] - weight * both, logit_grad)
    high = logit_grad.astype(BF16)
    rest = (logit_grad - high.astype(F32)).astype(BF16)
    router = gt[8:16, :].astype(BF16)
    h2 = h2 + dg(high, router, 1, 0) + dg(rest, router, 1, 0)
    mid = mid_ref[...]
    factor = lax.rsqrt(jnp.mean(mid * mid, axis=-1, keepdims=True) + NORM_EPS)
    normed = mid * factor
    u = h2 * gt[1:2, :]
    back = g[...].astype(F32) + factor * (
        u - normed * jnp.mean(u * normed, axis=-1, keepdims=True)
    )
    grad_mid[...] = back
    branch[...] = back.astype(BF16)
    small[...] = jnp.zeros_like(small)
    small[1:2, :] = jnp.sum(h2 * normed, axis=0, keepdims=True)
    small[8:16, :] = dg(high, a2[...], 0, 0) + dg(rest, a2[...], 0, 0)


def branch_kernel(own, rows, heads, idx_ref, *refs):
    bs = refs[:4]
    att, low, wo, small = refs[4:8]
    gt, delta, mine, theirs, full, grad = refs[8:]
    rank = idx_ref[1]
    qw = wo.shape[1]
    for d in range(4):
        full[pl.ds(pl.multiple_of((rank ^ d) * own, 16), own), :] = bs[d][...]
    gt[...] = dg(wo[...], full[...], 0, 1).astype(BF16)
    for h in range(heads):
        at = slice(h * HEAD, (h + 1) * HEAD)
        delta[h : h + 1, :] = jnp.sum(gt[at, :].astype(F32) * att[at, :], axis=0, keepdims=True)
    grad[:, :qw] = dg(full[...], low[...], 0, 0).astype(BF16)
    grad[:, qw:] = rows_as_columns(small)
    by_parity(rows, idx_ref[0] % 2, grad, mine, theirs)


def by_parity(rows, parity, grad, mine, theirs):
    for k in range(mine.shape[0] // rows):
        for out, p in ((mine, parity), (theirs, 1 - parity)):
            at = pl.ds(pl.multiple_of((2 * k + p) * rows, 8), rows)
            out[k * rows : (k + 1) * rows, :] = grad[at, :]


def rows_as_columns(small):
    pad = jnp.zeros((EXTRA - small.shape[0], small.shape[1]), F32)
    return jnp.transpose(jnp.concatenate([small[...], pad], axis=0)).astype(BF16)


def attend_back_kernel(np_, groups, local, meta_ref, *refs):
    qt, gt, lse, delta, qseg_ref, kseg = refs[:6]
    kvs = refs[6 : 6 + np_]
    refs = refs[6 + np_ :]
    if local:
        dq_in, dq, dkv, kb, vb, kt = refs
    else:
        dq = refs[0]
        dkvs = refs[1 : 1 + np_]
        kb, vb, kt, dkv = refs[1 + np_ :]
    span = qt.shape[1]
    half = kb.shape[1]
    kv_heads = half // HEAD
    for d in range(np_):
        at = (np_ - 1 - d) * span
        kb[at : at + span, :] = kvs[d][:, :half]
        vb[at : at + span, :] = kvs[d][:, half:]
        kt[:, at : at + span] = jnp.transpose(kvs[d][:, :half].astype(F32)).astype(BF16)
    dkv[...] = jnp.zeros_like(dkv)

    def q_block(qb, _):
        start = pl.multiple_of(qb * BLK, BLK)
        qs = pl.ds(start, BLK)
        qseg = qseg_ref[:, qs]
        for n in range(kv_heads):
            heads = [n * groups + g for g in range(groups)]
            sl = [slice(h * HEAD, (h + 1) * HEAD) for h in heads]
            q = [qt[r, qs] for r in sl]
            go = [gt[r, qs] for r in sl]
            ls = [lse[h : h + 1, qs] for h in heads]
            de = [delta[h : h + 1, qs] for h in heads]

            def tile(t, masked, carry, diag=False):
                ks = pl.ds(pl.multiple_of(t * BLK, BLK), BLK)
                lanes = slice(n * HEAD, (n + 1) * HEAD)
                k, v, k_t = kb[ks, lanes], vb[ks, lanes], kt[lanes, ks]
                ok = allowed_mask(t, start, diag, qseg, kseg) if masked else None
                out = []
                dk = dv = None
                for g in range(groups):
                    p = jnp.exp(dg(k, q[g], 1, 0) - ls[g])
                    if masked:
                        p = jnp.where(ok, p, 0.0)
                    ds = (p * (dg(v, go[g], 1, 0) - de[g])).astype(BF16)
                    one = dg(q[g], ds, 1, 1)
                    two = dg(go[g], p.astype(BF16), 1, 1)
                    dk = one if dk is None else dk + one
                    dv = two if dv is None else dv + two
                    out.append(carry[g] + dg(k_t, ds, 1, 0))
                dkv[n * HEAD : (n + 1) * HEAD, ks] += dk
                dkv[half + n * HEAD : half + (n + 1) * HEAD, ks] += dv
                return tuple(out)

            if local:
                state = tile(qb, True, tuple(dq_in[r, qs] for r in sl), True)
                state = tile_loop(meta_ref, qb, qb, tile, state)
                for g in range(groups):
                    dq[sl[g], qs] = (state[g] * (HEAD**-0.5)).astype(BF16)
            else:
                state = tuple(jnp.zeros((HEAD, BLK), F32) for _ in range(groups))
                state = tile_loop(meta_ref, qb, np_ * (span // BLK), tile, state)
                for g in range(groups):
                    dq[sl[g], qs] = state[g]
        return 0

    lax.fori_loop(0, span // BLK, q_block, 0)
    if not local:
        for d in range(np_):
            at = (np_ - 1 - d) * span
            dkvs[d][...] = dkv[:, at : at + span].astype(BF16)


def query_grad_kernel(rows, idx_ref, dq, a1, nat, mine, theirs, grad):
    nat[...] = jnp.transpose(dq[...].astype(F32)).astype(BF16)
    grad[...] = dg(a1[...], nat[...], 0, 0).astype(BF16)
    by_parity(rows, idx_ref[0] % 2, grad, mine, theirs)


def input_back_kernel(np_, own, idx_ref, *refs):
    nat_q, w, a1, gt = refs[:4]
    dkvs = refs[4 : 4 + np_]
    keep, other, send, nat, small = refs[4 + np_ :]
    rank = idx_ref[1]
    total = dkvs[0][...]
    for d in range(1, np_):
        total = total + dkvs[d][...].astype(F32)
    qw = nat_q.shape[1]
    nat[...] = jnp.transpose(total).astype(BF16)
    gain = jnp.zeros((1, w.shape[0]), F32)
    for d in range(4):
        rows = pl.ds(pl.multiple_of((rank ^ d) * own, 16), own)
        part = dg(nat_q[rows, :], w[:, :qw], 1, 1) + dg(nat[rows, :], w[:, qw:], 1, 1)
        gain = gain + jnp.sum(part * a1[rows, :].astype(F32), axis=0, keepdims=True)
        put_quarter(d, part, keep, other, send)
    small[...] = jnp.zeros_like(small)
    small[0:1, :] = gain / gt[0:1, :]


def keyval_grad_kernel(a1, nat, small, grad):
    width = nat.shape[1]
    grad[:, :width] = dg(a1[...], nat[...], 0, 0).astype(BF16)
    grad[:, width:] = rows_as_columns(small)


def input_grad_kernel(x, gt, grad_mid, kept, got, last, out):
    h1 = three(kept, got, last)
    v = x[...].astype(F32)
    factor = lax.rsqrt(jnp.mean(v * v, axis=-1, keepdims=True) + NORM_EPS)
    normed = v * factor
    u = h1 * gt[0:1, :]
    out[...] = grad_mid[...] + factor * (
        u - normed * jnp.mean(u * normed, axis=-1, keepdims=True)
    )


def expert_unpack_kernel(ff, cut, first, rest, gateup, down):
    for e in range(E):
        gateup[e, :, 0, :] = first[e, :, :ff].astype(F32)
        gateup[e, :, 1, : cut - ff] = first[e, :, ff:].astype(F32)
        gateup[e, :, 1, cut - ff :] = rest[e, :, : 2 * ff - cut].astype(F32)
        down[e] = rest[e, :, 2 * ff - cut :].astype(F32)


def route_slots(expert_ids):
    listed = jnp.concatenate([expert_ids[:, 0], expert_ids[:, 1]])
    onehot = (listed[:, None] == jnp.arange(E, dtype=jnp.int32)[None, :]).astype(jnp.int32)
    earlier = jnp.cumsum(onehot, axis=0) - onehot
    return jnp.sum(earlier * onehot, axis=1).reshape(2, -1)


def per_device(
    hidden_in,
    attn_gain,
    query_proj,
    key_value_projection,
    output_proj,
    moe_gain,
    router_proj,
    gateup_proj,
    down_proj,
    segment_index_list,
    expert_ids,
    out_grad,
):
    n_dp, n_tensor = lax.axis_size("dp"), lax.axis_size("tensor")
    own, width = hidden_in.shape
    span = own * n_tensor
    rows = query_proj.shape[0]
    qw = query_proj.shape[1]
    kvw = 2 * key_value_projection.shape[2]
    groups = 2 * qw // kvw
    ff = gateup_proj.shape[3]
    n_groups = n_dp // E
    dp_groups = None
    if n_groups > 1:
        dp_groups = [list(range(g * E, (g + 1) * E)) for g in range(n_groups)]
    dp, rank = lax.axis_index("dp"), lax.axis_index("tensor")
    idx = jnp.stack([dp, rank]).astype(jnp.int32)

    cols = qw + kvw
    early = jnp.concatenate(
        [query_proj, key_value_projection.reshape(rows, kvw), output_proj.T], axis=1
    )
    side = [attn_gain[None, :], moe_gain[None, :], jnp.zeros((6, rows), BF16), router_proj.T]
    side = jnp.pad(jnp.concatenate(side, axis=0), ((0, 0), (0, cols + qw - rows)))
    early = jnp.concatenate([early, side], axis=0)
    x_parts = [hidden_in, swap(hidden_in, "tensor", 1)]

    def slots_of(ids):
        position = route_slots(ids)
        per_rank = CAP // n_tensor
        local = position - rank * per_rank
        ids_t = ids.T
        slots = jnp.where(
            (local >= 0) & (local < per_rank) & (position < CAP), ids_t * SLOT + local, -1
        ).astype(jnp.int32)
        pad = jnp.zeros((4, span), jnp.int32)
        slot_rows = jnp.concatenate([slots, ids_t[::-1], pad], axis=0)
        return slot_rows, slots.T, lax.dynamic_slice_in_dim(ids, rank * own, own, 0)

    longest = segment_index_list.shape[0] // 4
    reach = min(SEQ_SPANS - 1, -(-(longest - 1) // span))
    n_pieces = reach + 1
    tiles = span // BLK

    def keys_of(segments):
        padded = jnp.concatenate([jnp.full((reach * span,), -1, jnp.int32), segments])
        window = lax.dynamic_slice_in_dim(padded, dp * span, n_pieces * span, 0)
        seg_mine = window[reach * span :]
        valid = jnp.minimum(dp % SEQ_SPANS, reach)
        first_seg, last_seg = seg_mine[::BLK], seg_mine[BLK - 1 :: BLK]
        low_tile = jnp.sum(window[None, :] < first_seg[:, None], axis=1) // BLK
        low_tile = jnp.maximum(low_tile, (reach - valid) * tiles)
        full_tile = -(-jnp.sum(window[None, :] < last_seg[:, None], axis=1) // BLK)
        meta = jnp.stack([low_tile, full_tile]).astype(jnp.int32)
        meta_own, meta = jnp.maximum(meta - reach * tiles, 0), jnp.minimum(meta, reach * tiles)
        return meta, meta_own, seg_mine[None, :], seg_mine[:, None], window[: reach * span, None]

    def packed_of(gateup, down):
        return jnp.concatenate(
            [gateup[:, :, 0], gateup[:, :, 1], jnp.transpose(down, (0, 2, 1))], axis=2
        )

    made = {}

    def meanwhile(step, piece):
        if step == 1:
            made["slots"] = slots_of(expert_ids)
            return made["slots"]
        if step == 2:
            made["packed"] = packed_of(after(gateup_proj, piece), down_proj)
            return (made["packed"],)
        if step == 3:
            two = after(x_parts.pop(), piece)
            x_parts.extend([two, swap(two, "tensor", 1)])
            made["keys"] = keys_of(after(segment_index_list, piece))
            return made["keys"]
        return ()

    x_parts.append(swap(hidden_in, "tensor", 2))
    pieces, source = ring_gather(early, "dp", meanwhile)
    slot_rows, slot_cols, ids_own = made["slots"]
    meta, meta_own, qseg, kseg_own, kseg = made["keys"]
    packed = made["packed"]
    w_early, wo, gt, a1, qt, kv = kcall(
        "qkv",
        functools.partial(qkv_kernel, len(pieces), own, rows, qw, cols),
        [
            sds((width, cols), BF16),
            sds((width, qw), BF16),
            sds((16, width), F32),
            sds((span, width), BF16),
            sds((qw, span), BF16),
            sds((span, kvw), BF16),
        ],
        [source, idx],
        pieces + x_parts,
        [
            pltpu.VMEM((span, width), BF16),
            pltpu.VMEM((span, qw), F32),
            pltpu.VMEM((n_dp, 16, rows), F32),
        ],
    )

    def dispatch(parts, with_ids):
        (tiles_,) = kcall(
            "dispatch",
            functools.partial(dispatch_kernel, own, with_ids),
            [sds((E * SLOT, width), BF16)],
            [idx],
            [slot_rows] + parts,
            [pltpu.VMEM((span, width), BF16), pltpu.VMEM((E * SLOT, span), BF16)],
        )
        return tiles_

    half = kvw // 2
    far = [shifted(kv, "dp", d) for d in range(1, n_pieces)]
    acc, top, total = kcall(
        "attend_own",
        functools.partial(attend_kernel, 1, groups, True),
        [sds((qw, span), F32), sds((8, span), F32), sds((8, span), F32)],
        [meta_own],
        [qt, qseg, kseg_own, kv],
        [pltpu.VMEM((span, half), BF16), pltpu.VMEM((half, span), BF16)],
    )

    g_in = after(out_grad, qt)
    g_parts = [out_grad, swap(g_in, "tensor", 1), after(swap(g_in, "tensor", 2), acc, *far)]
    g_parts.append(swap(g_parts[2], "tensor", 1))
    g_tiles = dispatch(g_parts, True)

    near = exchange(after(packed, acc, *far), dp_groups)
    w_expert = near.reshape(E * rows, 3 * ff)
    if n_groups > 1:
        shape = (n_groups, E * rows, 3 * ff)
        whole = jnp.zeros(shape, BF16)
        for h in range(n_groups):
            part = w_expert if h == 0 else swap(near.reshape(E * rows, 3 * ff), "dp", h * E)
            whole = lax.dynamic_update_index_in_dim(whole, part, (dp // E) ^ h, 0)
        w_expert = whole.reshape(width, 3 * ff)
    w_core = swap(w_expert, "tensor", 1)

    far[-1] = after(far[-1], g_tiles)
    att, lse, low = kcall(
        "attend_far",
        functools.partial(attend_kernel, reach, groups, False),
        [sds((qw, span), F32), sds((8, span), F32), sds((span, qw), BF16)],
        [meta],
        [qt, qseg, kseg] + far + [acc, top, total],
        [pltpu.VMEM((reach * span, half), BF16), pltpu.VMEM((half, reach * span), BF16)],
    )
    def quarters(wide):
        return [sds((own, wide), BF16), sds((own, wide), BF16), sds((2, own, wide), BF16)]

    keep, other, send = kcall(
        "project",
        functools.partial(project_kernel, own),
        quarters(width),
        [idx],
        [low, wo],
    )
    middle, a2 = kcall(
        "middle",
        middle_kernel,
        [sds((own, width), F32), sds((own, width), BF16)],
        [],
        [hidden_in, gt] + scatter_tensor(keep, other, send),
    )

    g_slots = exchange(after(g_tiles, w_expert, a2), dp_groups)
    a2_parts = gather_tensor(a2)
    w_across = swap(after(w_expert, a2_parts[2]), "tensor", 2)
    w_parts = [w_expert, w_core, w_across, swap(w_across, "tensor", 1)]
    x_slots = exchange(after(dispatch(a2_parts, False), g_slots), dp_groups)
    n_slots = E * SLOT
    s_slots, hid, slot_weight, dx = kcall(
        "expert",
        functools.partial(expert_kernel, ff),
        [
            sds((n_slots, width), BF16),
            sds((4, n_slots, 3 * ff), BF16),
            sds((n_slots, 1), F32),
            sds((n_slots, width), BF16),
        ],
        [idx],
        [x_slots, g_slots] + w_parts + [gt],
        [pltpu.VMEM((n_slots, width), F32)],
    )
    cut = 3 * ff // 2

    def expert_grad(first):
        return kcall(
            "expert_grad",
            functools.partial(expert_grad_kernel, ff, cut, first),
            [sds((width, cut), BF16)] * 4,
            [],
            [x_slots, s_slots, hid],
        )

    dx_back = exchange(dx, dp_groups)
    keep_a, near_a, other_a, far_a = expert_grad(True)
    keep_b, near_b, other_b, far_b = expert_grad(False)
    (out_slots,) = kcall(
        "expert_out",
        functools.partial(expert_out_kernel, ff),
        [sds((n_slots, width), BF16)],
        [],
        [hid, slot_weight] + w_parts,
        [pltpu.VMEM((n_slots, width), F32)],
    )
    second_a = (other_a.astype(F32) + swap(far_a, "tensor", 1).astype(F32)).astype(BF16)
    second_b = (other_b.astype(F32) + swap(far_b, "tensor", 1).astype(F32)).astype(BF16)
    got_a, got_b = swap(near_a, "tensor", 1), swap(near_b, "tensor", 1)
    last_a = swap(second_a, "tensor", 2)
    dx_back = after(dx_back, keep_a, keep_b, out_slots)
    out_back = exchange(after(out_slots, dx_back), dp_groups)

    def combine(parts_, with_q, *others):
        wide = width + (EXTRA if with_q else 0)
        keep, other, send = kcall(
            "combine",
            functools.partial(combine_kernel, own, with_q),
            quarters(wide),
            [idx],
            [slot_cols, parts_],
            [pltpu.VMEM((E * SLOT, wide), BF16)],
        )
        return scatter_tensor(keep, other, after(send, *others) if others else send)

    back_terms = combine(dx_back, True, last_a)
    grad_middle, branch, small_two = kcall(
        "middle_back",
        middle_back_kernel,
        [sds((own, width), F32), sds((own, width), BF16), sds((16, width), F32)],
        [],
        [middle, a2, out_grad, ids_own, gt] + back_terms,
    )
    def own_grad(kept, got, last, *others):
        total = (kept.astype(F32) + got.astype(F32) + last.astype(F32)).astype(BF16)
        if n_groups > 1:
            group = dp // E
            blocks = total.reshape(n_groups, E * rows, -1)
            total = lax.dynamic_index_in_dim(blocks, group, 0, keepdims=False).astype(F32)
            for h in range(1, n_groups):
                there = lax.dynamic_index_in_dim(blocks, group ^ h, 0, keepdims=False)
                total = total + swap(there, "dp", h * E).astype(F32)
            total = total.astype(BF16)
        return exchange(after(total.reshape(E, rows, -1), *others), dp_groups)

    branch_parts = gather_tensor(branch)
    own_a = own_grad(keep_a, got_a, last_a, out_back)
    last_b = swap(after(second_b, branch_parts[2]), "tensor", 2)

    heads = qw // HEAD
    g_heads, delta, mine, theirs = kcall(
        "branch",
        functools.partial(branch_kernel, own, rows, heads),
        [
            sds((qw, span), BF16),
            sds((8, span), F32),
            sds((width // 2, qw + EXTRA), BF16),
            sds((width // 2, qw + EXTRA), BF16),
        ],
        [idx],
        branch_parts + [att, low, wo, small_two],
        [pltpu.VMEM((span, width), BF16), pltpu.VMEM((width, qw + EXTRA), BF16)],
    )
    pairs = [list(range(p, n_dp, 2)) for p in range(2)]

    def pair_sum(mine, theirs):
        return (mine.astype(F32) + swap(theirs, "dp", 1).astype(F32)).astype(BF16)

    def owner_sum(value, *others):
        parts = exchange(after(value, *others), pairs)
        return jnp.sum(parts.reshape(n_dp // 2, rows, -1).astype(F32), axis=0)

    out_sum = owner_sum(pair_sum(mine, theirs), own_a)
    outs = kcall(
        "attend_back_far",
        functools.partial(attend_back_kernel, reach, groups, False),
        [sds((qw, span), F32)] + [sds((kvw, span), BF16)] * reach,
        [meta],
        [qt, g_heads, lse, delta, qseg, kseg] + far,
        [
            pltpu.VMEM((reach * span, half), BF16),
            pltpu.VMEM((reach * span, half), BF16),
            pltpu.VMEM((half, reach * span), BF16),
            pltpu.VMEM((kvw, reach * span), F32),
        ],
    )
    dkv_far = [shifted(outs[d], "dp", -d) for d in range(1, n_pieces)]
    dq, dkv_own = kcall(
        "attend_back_own",
        functools.partial(attend_back_kernel, 1, groups, True),
        [sds((qw, span), BF16), sds((kvw, span), F32)],
        [meta_own],
        [qt, g_heads, lse, delta, qseg, kseg_own, kv, outs[0]],
        [
            pltpu.VMEM((span, half), BF16),
            pltpu.VMEM((span, half), BF16),
            pltpu.VMEM((half, span), BF16),
        ],
    )
    own_b = own_grad(keep_b, got_b, after(last_b, outs[0]), out_sum)

    nat_q, mine, theirs = kcall(
        "query_grad",
        functools.partial(query_grad_kernel, rows),
        [
            sds((span, qw), BF16),
            sds((width // 2, qw), BF16),
            sds((width // 2, qw), BF16),
        ],
        [idx],
        [after(dq, *dkv_far), a1],
        [pltpu.VMEM((width, qw), BF16)],
    )
    q_sum = owner_sum(pair_sum(mine, theirs), own_b)
    keep_h, other_h, send_h, nat_kv, small_one = kcall(
        "input_back",
        functools.partial(input_back_kernel, n_pieces, own),
        quarters(width) + [sds((span, kvw), BF16), sds((16, width), F32)],
        [idx],
        [nat_q, w_early, a1, gt, dkv_own] + dkv_far,
    )
    in_terms = scatter_tensor(keep_h, other_h, send_h)
    gain_sum = small_one + swap(small_one, "tensor", 1)
    gain_sum = gain_sum + swap(gain_sum, "tensor", 2)
    (kv_part,) = kcall(
        "keyval_grad",
        keyval_grad_kernel,
        [sds((width, kvw + EXTRA), BF16)],
        [],
        [a1, nat_kv, gain_sum],
    )
    kv_parts = exchange(after(kv_part, q_sum))
    (input_grad,) = kcall(
        "input_grad",
        input_grad_kernel,
        [sds((own, width), F32)],
        [],
        [hidden_in, gt, grad_middle] + in_terms,
    )

    out_terms = combine(after(out_back, nat_q), False)
    hidden_out = (
        middle + out_terms[0].astype(F32) + out_terms[1][0].astype(F32) + out_terms[2].astype(F32)
    ).astype(BF16)
    gateup_grad, down_grad = kcall(
        "expert_unpack",
        functools.partial(expert_unpack_kernel, ff, cut),
        [sds((E, rows, 2, ff), F32), sds((E, rows, ff), F32)],
        [],
        [own_a, own_b],
    )
    o_sum = out_sum[:, :qw].T
    side = out_sum[:, qw : qw + 16]
    side = side + swap(side, "tensor", 1)
    side = side + swap(side, "tensor", 2)
    ready = (input_grad, hidden_out, gateup_grad, down_grad, q_sum, o_sum, side)
    kv_parts = after(kv_parts, *ready)
    kv_sum = jnp.sum(kv_parts.reshape(n_dp, rows, -1).astype(F32), axis=0)
    return (
        hidden_out,
        input_grad,
        kv_sum[:, kvw],
        q_sum,
        kv_sum[:, :kvw].reshape(rows, 2, kvw // 2),
        o_sum,
        side[:, 1],
        side[:, 8:16],
        gateup_grad,
        jnp.transpose(down_grad, (0, 2, 1)),
    )


def solution(mesh):
    return jax.shard_map(
        per_device,
        mesh=mesh,
        in_specs=(
            P(("dp", "tensor"), None),
            P("dp"),
            P("dp", "tensor"),
            P("dp", None, "tensor"),
            P("tensor", "dp"),
            P("dp"),
            P("dp", None),
            P(None, "dp", None, "tensor"),
            P(None, "tensor", "dp"),
            P(),
            P("dp", None),
            P(("dp", "tensor"), None),
        ),
        out_specs=(
            P(("dp", "tensor"), None),
            P(("dp", "tensor"), None),
            P("dp"),
            P("dp", "tensor"),
            P("dp", None, "tensor"),
            P("tensor", "dp"),
            P("dp"),
            P("dp", None),
            P(None, "dp", None, "tensor"),
            P(None, "tensor", "dp"),
        ),
        check_vma=False,
    )
```

```python
import functools

import jax
import jax.numpy as jnp
from jax import lax
from jax.experimental import pallas as pl
from jax.experimental.pallas import tpu as pltpu
from jax.sharding import PartitionSpec as P

HEAD = 64
E = 8
SEQ_SPANS = 8
CAP = 240
SLOT = 64
BLK = 256
EXTRA = 128

NORM_EPS = 1e-05
NEG = -1e30

F32 = jnp.float32
BF16 = jnp.bfloat16


def dg(a, b, ca, cb):
    return lax.dot_general(a, b, (((ca,), (cb,)), ((), ())), preferred_element_type=F32)


def sds(shape, dtype):
    return jax.ShapeDtypeStruct(shape, dtype)


TIMES = {
    "qkv": 7,
    "attend_own": 14,
    "attend_far": 20,
    "project": 4,
    "middle": 3,
    "dispatch": 4,
    "expert": 17,
    "expert_grad": 3,
    "expert_out": 3,
    "combine": 12,
    "combine_out": 1,
    "middle_back": 5,
    "branch": 6,
    "attend_back_far": 20,
    "attend_back_own": 14,
    "query_grad": 1,
    "input_back": 1,
    "keyval_grad": 1,
    "input_grad": 1,
    "expert_unpack": 1,
}


def kcall(name, body, outs, smem, vmem, scratch=(), limit=60):
    return pl.pallas_call(
        body,
        name=name,
        out_shape=list(outs),
        in_specs=[pl.BlockSpec(memory_space=pltpu.SMEM)] * len(smem)
        + [pl.BlockSpec(memory_space=pltpu.VMEM)] * len(vmem),
        out_specs=[pl.BlockSpec(memory_space=pltpu.VMEM)] * len(outs),
        scratch_shapes=list(scratch),
        compiler_params=pltpu.CompilerParams(vmem_limit_bytes=limit << 20),
        cost_estimate=pl.CostEstimate(
            flops=TIMES[name] * 10**9, bytes_accessed=10**6, transcendentals=0
        ),
    )(*smem, *vmem)


def swap(value, axis, by):
    size = lax.axis_size(axis)
    return lax.ppermute(value, axis, [(i, i ^ by) for i in range(size)])


def shifted(value, axis, by):
    size = lax.axis_size(axis)
    return lax.ppermute(value, axis, [(i, i + by) for i in range(size) if 0 <= i + by < size])


def gather_tensor(value):
    one = swap(value, "tensor", 1)
    two = swap(value, "tensor", 2)
    return [value, one, two, swap(two, "tensor", 1)]


def scatter_tensor(keep, other, send):
    got = swap(send, "tensor", 1)
    second = (other.astype(F32) + got[1].astype(F32)).astype(BF16)
    return [keep, got, swap(second, "tensor", 2)], second


def three(kept, got, last):
    return kept[...].astype(F32) + got[0].astype(F32) + last[...].astype(F32)


def ring_pos(index, size):
    return jnp.where(index % 2 == 0, index // 2, size - 1 - (index - 1) // 2)


def ring_dev(pos, size):
    pos = pos % size
    return jnp.where(pos < size // 2, 2 * pos, 2 * (size - 1 - pos) + 1)


def ring_gather(value, axis, meanwhile):
    size = lax.axis_size(axis)
    order = list(range(0, size, 2)) + list(range(size - 1, 0, -2))
    ahead = [(order[k], order[(k + 1) % size]) for k in range(size)]
    back = [(b, a) for a, b in ahead]
    half = value.shape[0] // 16 * 8
    index = lax.axis_index(axis)
    pos = ring_pos(index, size)
    pieces, source = [value], [index]
    one = two = value
    for step in range(1, size // 2 + 1):
        last = step == size // 2
        got_one = lax.ppermute(one[:half] if last else one, axis, ahead)
        got_two = lax.ppermute(two[half:] if last else two, axis, back)
        done = meanwhile(step, one)
        one, two = (after(got_one, *done), got_two) if done else (got_one, got_two)
        pieces += [one, two]
        source += [ring_dev(pos - step, size), ring_dev(pos + step, size)]
    return pieces, jnp.stack(source).astype(jnp.int32)


def exchange(value, groups=None):
    return lax.all_to_all(
        value, "dp", split_axis=0, concat_axis=0, axis_index_groups=groups, tiled=True
    )


def after(value, *others):
    return lax.optimization_barrier((value,) + others)[0]


def qkv_kernel(n, own, rows, qw, cols, src_ref, idx_ref, *refs):
    pieces = refs[:n]
    xs = refs[n : n + 4]
    w, wo, gt, a1, qt, kv, xb, qn, gs = refs[n + 4 :]
    rank = idx_ref[1]
    for k in range(n):
        piece = pieces[k]
        first = pieces[n - 2].shape[0] if k == n - 1 else 0
        last = min(first + piece.shape[0], rows)
        at = pl.ds(pl.multiple_of(src_ref[k] * rows + first, 8), last - first)
        w[at, :] = piece[: last - first, :cols]
        wo[at, :] = piece[: last - first, cols:]
        if first + piece.shape[0] > rows:
            gs[pl.ds(src_ref[k], 1)] = piece[last - first :, :rows].astype(F32)[None]
    for d in range(4):
        xb[pl.ds(pl.multiple_of((rank ^ d) * own, 16), own), :] = xs[d][...]
    gt[...] = jnp.concatenate([gs[j] for j in range(gs.shape[0])], axis=1)

    def block(j, _):
        at = pl.ds(pl.multiple_of(j * own, 16), own)
        x = xb[at, :].astype(F32)
        factor = lax.rsqrt(jnp.mean(x * x, axis=-1, keepdims=True) + NORM_EPS)
        a = (x * factor * gt[0:1, :]).astype(BF16)
        a1[at, :] = a
        y = dg(a, w[...], 1, 0)
        qn[at, :] = y[:, :qw] * (HEAD**-0.5)
        kv[at, :] = y[:, qw:].astype(BF16)
        return 0

    lax.fori_loop(0, 4, block, 0)
    qt[...] = jnp.transpose(qn[...]).astype(BF16)


def tile_loop(meta_ref, qb, end, body, carry):
    low, full = meta_ref[0, qb], meta_ref[1, qb]
    carry = lax.fori_loop(low, jnp.minimum(full, end), lambda t, c: body(t, True, c), carry)
    return lax.fori_loop(jnp.maximum(full, low), end, lambda t, c: body(t, False, c), carry)


def allowed_mask(t, start, diag, qseg, kseg):
    ok = kseg[pl.ds(pl.multiple_of(t * BLK, BLK), BLK), :] == qseg
    if diag:
        keys = lax.broadcasted_iota(jnp.int32, (BLK, BLK), 0)
        ok = ok & (keys <= lax.broadcasted_iota(jnp.int32, (BLK, BLK), 1))
    return ok


def attend_kernel(np_, groups, local, meta_ref, *refs):
    qt, qseg_ref, kseg = refs[:3]
    kvs = refs[3 : 3 + np_]
    if local:
        acc_ref, m_ref, l_ref, kb, vt = refs[3 + np_ :]
    else:
        acc_in, m_in, l_in, att, lse, low, kb, vt = refs[3 + np_ :]
    span = qt.shape[1]
    half = kb.shape[1]
    kv_heads = half // HEAD
    for d in range(np_):
        at = (np_ - 1 - d) * span
        kb[at : at + span, :] = kvs[d][:, :half]
        vt[:, at : at + span] = jnp.transpose(kvs[d][:, half:].astype(F32)).astype(BF16)

    def q_block(qb, _):
        start = pl.multiple_of(qb * BLK, BLK)
        qs = pl.ds(start, BLK)
        qseg = qseg_ref[:, qs]
        for n in range(kv_heads):
            heads = [n * groups + g for g in range(groups)]
            sl = [slice(h * HEAD, (h + 1) * HEAD) for h in heads]
            q = [qt[r, qs] for r in sl]

            def tile(t, masked, carry, diag=False):
                ks = pl.ds(pl.multiple_of(t * BLK, BLK), BLK)
                k = kb[ks, n * HEAD : (n + 1) * HEAD]
                v = vt[n * HEAD : (n + 1) * HEAD, ks]
                ok = allowed_mask(t, start, diag, qseg, kseg) if masked else None
                out = []
                for g in range(groups):
                    m, l, acc = carry[g]
                    s = dg(k, q[g], 1, 0)
                    if masked:
                        s = jnp.where(ok, s, NEG)
                    m_new = jnp.maximum(m, jnp.max(s, axis=0, keepdims=True))
                    e = jnp.exp(s - m_new)
                    shrink = jnp.exp(m - m_new)
                    l = l * shrink + jnp.sum(e, axis=0, keepdims=True)
                    acc = acc * shrink + dg(v, e.astype(BF16), 1, 0)
                    out.append((m_new, l, acc))
                return tuple(out)

            if local:
                none = jnp.full((1, BLK), NEG, F32)
                init = (none, jnp.zeros((1, BLK), F32), jnp.zeros((HEAD, BLK), F32))
                state = tile(qb, True, (init,) * groups, True)
                state = tile_loop(meta_ref, qb, qb, tile, state)
                for g in range(groups):
                    h = heads[g]
                    m_ref[h : h + 1, qs], l_ref[h : h + 1, qs], acc_ref[sl[g], qs] = state[g]
            else:
                state = tuple(
                    (m_in[h : h + 1, qs], l_in[h : h + 1, qs], acc_in[r, qs])
                    for h, r in zip(heads, sl)
                )
                state = tile_loop(meta_ref, qb, np_ * (span // BLK), tile, state)
                for g in range(groups):
                    m, l, acc = state[g]
                    att[sl[g], qs] = acc / l
                    lse[heads[g] : heads[g] + 1, qs] = m + jnp.log(l)
        return 0

    lax.fori_loop(0, span // BLK, q_block, 0)
    if not local:
        low[...] = jnp.transpose(att[...]).astype(BF16)


def put_quarter(d, part, keep, other, send):
    if d % 2:
        send[d // 2] = part.astype(BF16)
    else:
        (other if d else keep)[...] = part.astype(BF16)


def project_kernel(own, idx_ref, low, wo, keep, other, send):
    rank = idx_ref[1]
    for d in range(4):
        rows = pl.ds(pl.multiple_of((rank ^ d) * own, 16), own)
        put_quarter(d, dg(low[rows, :], wo[...], 1, 1), keep, other, send)


def middle_kernel(x, gt, kept, got, last, middle, a2):
    mid = x[...].astype(F32) + three(kept, got, last)
    middle[...] = mid
    factor = lax.rsqrt(jnp.mean(mid * mid, axis=-1, keepdims=True) + NORM_EPS)
    a2[...] = (mid * factor * gt[1:2, :]).astype(BF16)


def select_tile(e, rows_ref, k=None):
    slot = e * SLOT + lax.broadcasted_iota(jnp.int32, (SLOT, rows_ref.shape[1]), 0)
    first, second = slot == rows_ref[0:1, :], slot == rows_ref[1:2, :]
    hit = (first | second) if k is None else (second if k else first)
    return jnp.where(hit, 1.0, 0.0).astype(BF16)


def dispatch_kernel(own, with_ids, idx_ref, rows_ref, *refs):
    xs, out = refs[:4], refs[4]
    xb, pick = refs[5:]
    rank = idx_ref[1]
    for d in range(4):
        xb[pl.ds(pl.multiple_of((rank ^ d) * own, 16), own), :] = xs[d][...]
    for e in range(E):
        pick[e * SLOT : (e + 1) * SLOT, :] = select_tile(e, rows_ref)
    width = 512
    for c in range(xb.shape[1] // width):
        lanes = slice(c * width, (c + 1) * width)
        y = dg(pick[...], xb[:, lanes], 1, 0)
        if not (with_ids and c == 0):
            out[:, lanes] = y.astype(BF16)
            continue
        ids = rows_ref[2:4, :].astype(F32).astype(BF16)
        for e in range(E):
            rows = slice(e * SLOT, (e + 1) * SLOT)
            row = dg(ids, select_tile(e, rows_ref, 0), 1, 1)[0:1]
            row = row + dg(ids, select_tile(e, rows_ref, 1), 1, 1)[1:2]
            row = jnp.concatenate([row, jnp.zeros((1, width - SLOT), F32)], axis=1)
            at = lax.broadcasted_iota(jnp.int32, (SLOT, width), 0)
            out[rows, lanes] = jnp.where(at == SLOT - 4, row, y[rows]).astype(BF16)


def eye():
    shape = (SLOT, SLOT)
    return lax.broadcasted_iota(jnp.int32, shape, 0) == lax.broadcasted_iota(jnp.int32, shape, 1)


def row_to_col(row):
    return jnp.sum(jnp.where(eye(), row, 0.0), axis=1, keepdims=True)


def col_to_row(col):
    return jnp.sum(jnp.where(eye(), col, 0.0), axis=0, keepdims=True)


def split_three(value):
    one = value.astype(BF16).astype(F32)
    two = (value - one).astype(BF16).astype(F32)
    return one, two, (value - one - two).astype(BF16).astype(F32)


def expert_kernel(ff, idx_ref, x_ref, gs, w0, w1, w2, w3, gt, so, ho, wo, dxo, dx):
    index = idx_ref[0] % E
    x = x_ref[...]
    logits = dg(x, gt[8:16, :].astype(BF16), 1, 1)
    lane = lax.broadcasted_iota(jnp.int32, (SLOT, E), 1)
    weights = []
    for d in range(E):
        rows = slice(d * SLOT, (d + 1) * SLOT)
        part = logits[rows]
        side = gs[(d + 1) * SLOT - 8 : (d + 1) * SLOT, 0:SLOT].astype(F32)
        other = row_to_col(side[4:5]).astype(jnp.int32)
        mine = jnp.sum(jnp.where(lane == index, part, 0.0), axis=1, keepdims=True)
        theirs = jnp.sum(jnp.where(lane == other, part, 0.0), axis=1, keepdims=True)
        weight = 1.0 / (1.0 + jnp.exp(theirs - mine))
        real = lax.broadcasted_iota(jnp.int32, (SLOT, 1), 0) < SLOT - 4
        weight = jnp.where(real, weight, 0.0)
        weights.append(weight)
        so[rows, :] = jnp.where(real, weight * gs[rows, :].astype(F32), 0.0).astype(BF16)
    wo[...] = jnp.concatenate(weights, axis=0)
    q = jnp.zeros((E * SLOT, 1), F32)
    for f, w in enumerate((w0, w1, w2, w3)):
        gate = dg(x, w[:, :ff], 1, 0)
        up = dg(x, w[:, ff : 2 * ff], 1, 0)
        hidden = dg(so[...], w[:, 2 * ff :], 1, 0)
        sig = 1.0 / (1.0 + jnp.exp(-gate))
        act = gate * sig * up
        q = q + jnp.sum(hidden * act, axis=1, keepdims=True)
        ho[f, :, :ff] = (hidden * up * sig * (1.0 + gate * (1.0 - sig))).astype(BF16)
        ho[f, :, ff : 2 * ff] = (hidden * gate * sig).astype(BF16)
        ho[f, :, 2 * ff :] = act.astype(BF16)
        part = dg(ho[f, :, : 2 * ff], w[:, : 2 * ff], 1, 1)
        dx[...] = part if f == 0 else dx[...] + part
    dxo[...] = dx[...].astype(BF16)
    for d in range(E):
        rows = slice(d * SLOT, (d + 1) * SLOT)
        head = dx[rows, 0:128]
        at = lax.broadcasted_iota(jnp.int32, head.shape, 0)
        row = jnp.concatenate([col_to_row(q[rows]), jnp.zeros((1, 128 - SLOT), F32)], axis=1)
        for k, term in enumerate(split_three(row)):
            head = jnp.where(at == SLOT - 4 + k, term, head)
        dxo[rows, 0:128] = head.astype(BF16)


def expert_grad_kernel(ff, cut, first, x, s, h, *outs):
    for f in range(4):
        out = outs[f]
        if first:
            out[...] = dg(x[...], h[f, :, :cut], 0, 0).astype(BF16)
        else:
            out[:, : 2 * ff - cut] = dg(x[...], h[f, :, cut : 2 * ff], 0, 0).astype(BF16)
            out[:, 2 * ff - cut :] = dg(s[...], h[f, :, 2 * ff :], 0, 0).astype(BF16)


def expert_out_kernel(ff, h, weight, w0, w1, w2, w3, out, acc):
    for f, w in enumerate((w0, w1, w2, w3)):
        part = dg(h[f, :, 2 * ff :], w[:, 2 * ff :], 1, 1)
        acc[...] = part if f == 0 else acc[...] + part
    out[...] = (acc[...] * weight[...]).astype(BF16)


def combine_kernel(own, with_q, idx_ref, cols, parts, keep, other, send, y):
    rank = idx_ref[1]
    width = parts.shape[1]
    y[:, :width] = parts[...]
    if with_q:
        for e in range(E):
            rows = slice(e * SLOT, (e + 1) * SLOT)
            tail = parts[(e + 1) * SLOT - 8 : (e + 1) * SLOT, 0:SLOT].astype(F32)
            lane = lax.broadcasted_iota(jnp.int32, (SLOT, EXTRA), 1)
            side = jnp.zeros((SLOT, EXTRA), F32)
            for k in range(3):
                side = jnp.where(lane == e + 8 * k, row_to_col(tail[4 + k : 5 + k]), side)
            y[rows, width:] = side.astype(BF16)
    slot = lax.broadcasted_iota(jnp.int32, (own, E * SLOT), 1)
    for d in range(4):
        at = pl.ds(pl.multiple_of((rank ^ d) * own, 16), own)
        hit = (cols[at, 0:1] == slot) | (cols[at, 1:2] == slot)
        part = dg(jnp.where(hit, 1.0, 0.0).astype(BF16), y[...], 1, 0)
        put_quarter(d, part, keep, other, send)


def middle_back_kernel(mid_ref, a2, g, ids, gt, kept, got, last, grad_mid, branch, small):
    width = mid_ref.shape[1]
    total = three(kept, got, last)
    h2, side = total[:, :width], total[:, width:]
    own = h2.shape[0]
    logits = dg(a2[...], gt[8:16, :].astype(BF16), 1, 1)
    lane = lax.broadcasted_iota(jnp.int32, (own, E), 1)
    q = side[:, 0:8] + side[:, 8:16] + side[:, 16:24]
    hit = [lane == ids[:, k : k + 1] for k in range(2)]
    logit = [jnp.sum(jnp.where(hit[k], logits, 0.0), axis=1, keepdims=True) for k in range(2)]
    terms = [jnp.sum(jnp.where(hit[k], q, 0.0), axis=1, keepdims=True) for k in range(2)]
    both = terms[0] + terms[1]
    logit_grad = jnp.zeros((own, E), F32)
    for k in range(2):
        weight = 1.0 / (1.0 + jnp.exp(logit[1 - k] - logit[k]))
        logit_grad = jnp.where(hit[k], terms[k] - weight * both, logit_grad)
    high = logit_grad.astype(BF16)
    rest = (logit_grad - high.astype(F32)).astype(BF16)
    router = gt[8:16, :].astype(BF16)
    h2 = h2 + dg(high, router, 1, 0) + dg(rest, router, 1, 0)
    mid = mid_ref[...]
    factor = lax.rsqrt(jnp.mean(mid * mid, axis=-1, keepdims=True) + NORM_EPS)
    normed = mid * factor
    u = h2 * gt[1:2, :]
    back = g[...].astype(F32) + factor * (
        u - normed * jnp.mean(u * normed, axis=-1, keepdims=True)
    )
    grad_mid[...] = back
    branch[...] = back.astype(BF16)
    small[...] = jnp.zeros_like(small)
    small[1:2, :] = jnp.sum(h2 * normed, axis=0, keepdims=True)
    small[8:16, :] = dg(high, a2[...], 0, 0) + dg(rest, a2[...], 0, 0)


def branch_kernel(own, rows, heads, idx_ref, *refs):
    bs = refs[:4]
    att, low, wo, small = refs[4:8]
    gt, delta, mine, theirs, full, grad = refs[8:]
    rank = idx_ref[1]
    qw = wo.shape[1]
    for d in range(4):
        full[pl.ds(pl.multiple_of((rank ^ d) * own, 16), own), :] = bs[d][...]
    gt[...] = dg(wo[...], full[...], 0, 1).astype(BF16)
    for h in range(heads):
        at = slice(h * HEAD, (h + 1) * HEAD)
        delta[h : h + 1, :] = jnp.sum(gt[at, :].astype(F32) * att[at, :], axis=0, keepdims=True)
    grad[:, :qw] = dg(full[...], low[...], 0, 0).astype(BF16)
    grad[:, qw:] = rows_as_columns(small)
    by_parity(rows, idx_ref[0] % 2, grad, mine, theirs)


def by_parity(rows, parity, grad, mine, theirs):
    for k in range(mine.shape[0] // rows):
        for out, p in ((mine, parity), (theirs, 1 - parity)):
            at = pl.ds(pl.multiple_of((2 * k + p) * rows, 8), rows)
            out[k * rows : (k + 1) * rows, :] = grad[at, :]


def rows_as_columns(small):
    pad = jnp.zeros((EXTRA - small.shape[0], small.shape[1]), F32)
    return jnp.transpose(jnp.concatenate([small[...], pad], axis=0)).astype(BF16)


def attend_back_kernel(np_, groups, local, meta_ref, *refs):
    qt, gt, lse, delta, qseg_ref, kseg = refs[:6]
    kvs = refs[6 : 6 + np_]
    refs = refs[6 + np_ :]
    if local:
        dq_in, dq, dkv, kb, vb, kt = refs
    else:
        dq = refs[0]
        dkvs = refs[1 : 1 + np_]
        kb, vb, kt, dkv = refs[1 + np_ :]
    span = qt.shape[1]
    half = kb.shape[1]
    kv_heads = half // HEAD
    for d in range(np_):
        at = (np_ - 1 - d) * span
        kb[at : at + span, :] = kvs[d][:, :half]
        vb[at : at + span, :] = kvs[d][:, half:]
        kt[:, at : at + span] = jnp.transpose(kvs[d][:, :half].astype(F32)).astype(BF16)
    dkv[...] = jnp.zeros_like(dkv)

    def q_block(qb, _):
        start = pl.multiple_of(qb * BLK, BLK)
        qs = pl.ds(start, BLK)
        qseg = qseg_ref[:, qs]
        for n in range(kv_heads):
            heads = [n * groups + g for g in range(groups)]
            sl = [slice(h * HEAD, (h + 1) * HEAD) for h in heads]
            q = [qt[r, qs] for r in sl]
            go = [gt[r, qs] for r in sl]
            ls = [lse[h : h + 1, qs] for h in heads]
            de = [delta[h : h + 1, qs] for h in heads]

            def tile(t, masked, carry, diag=False):
                ks = pl.ds(pl.multiple_of(t * BLK, BLK), BLK)
                lanes = slice(n * HEAD, (n + 1) * HEAD)
                k, v, k_t = kb[ks, lanes], vb[ks, lanes], kt[lanes, ks]
                ok = allowed_mask(t, start, diag, qseg, kseg) if masked else None
                out = []
                dk = dv = None
                for g in range(groups):
                    p = jnp.exp(dg(k, q[g], 1, 0) - ls[g])
                    if masked:
                        p = jnp.where(ok, p, 0.0)
                    ds = (p * (dg(v, go[g], 1, 0) - de[g])).astype(BF16)
                    one = dg(q[g], ds, 1, 1)
                    two = dg(go[g], p.astype(BF16), 1, 1)
                    dk = one if dk is None else dk + one
                    dv = two if dv is None else dv + two
                    out.append(carry[g] + dg(k_t, ds, 1, 0))
                dkv[n * HEAD : (n + 1) * HEAD, ks] += dk
                dkv[half + n * HEAD : half + (n + 1) * HEAD, ks] += dv
                return tuple(out)

            if local:
                state = tile(qb, True, tuple(dq_in[r, qs] for r in sl), True)
                state = tile_loop(meta_ref, qb, qb, tile, state)
                for g in range(groups):
                    dq[sl[g], qs] = (state[g] * (HEAD**-0.5)).astype(BF16)
            else:
                state = tuple(jnp.zeros((HEAD, BLK), F32) for _ in range(groups))
                state = tile_loop(meta_ref, qb, np_ * (span // BLK), tile, state)
                for g in range(groups):
                    dq[sl[g], qs] = state[g]
        return 0

    lax.fori_loop(0, span // BLK, q_block, 0)
    if not local:
        for d in range(np_):
            at = (np_ - 1 - d) * span
            dkvs[d][...] = dkv[:, at : at + span].astype(BF16)


def query_grad_kernel(rows, idx_ref, dq, a1, nat, mine, theirs, grad):
    nat[...] = jnp.transpose(dq[...].astype(F32)).astype(BF16)
    grad[...] = dg(a1[...], nat[...], 0, 0).astype(BF16)
    by_parity(rows, idx_ref[0] % 2, grad, mine, theirs)


def input_back_kernel(np_, own, idx_ref, *refs):
    nat_q, w, a1, gt = refs[:4]
    dkvs = refs[4 : 4 + np_]
    keep, other, send, nat, small = refs[4 + np_ :]
    rank = idx_ref[1]
    total = dkvs[0][...]
    for d in range(1, np_):
        total = total + dkvs[d][...].astype(F32)
    qw = nat_q.shape[1]
    nat[...] = jnp.transpose(total).astype(BF16)
    gain = jnp.zeros((1, w.shape[0]), F32)
    for d in range(4):
        rows = pl.ds(pl.multiple_of((rank ^ d) * own, 16), own)
        part = dg(nat_q[rows, :], w[:, :qw], 1, 1) + dg(nat[rows, :], w[:, qw:], 1, 1)
        gain = gain + jnp.sum(part * a1[rows, :].astype(F32), axis=0, keepdims=True)
        put_quarter(d, part, keep, other, send)
    small[...] = jnp.zeros_like(small)
    small[0:1, :] = gain / gt[0:1, :]


def keyval_grad_kernel(rows, idx_ref, a1, nat, small, mine, theirs, grad):
    width = nat.shape[1]
    grad[:, :width] = dg(a1[...], nat[...], 0, 0).astype(BF16)
    grad[:, width:] = rows_as_columns(small)
    by_parity(rows, idx_ref[0] % 2, grad, mine, theirs)


def input_grad_kernel(x, gt, grad_mid, kept, got, last, out):
    h1 = three(kept, got, last)
    v = x[...].astype(F32)
    factor = lax.rsqrt(jnp.mean(v * v, axis=-1, keepdims=True) + NORM_EPS)
    normed = v * factor
    u = h1 * gt[0:1, :]
    out[...] = grad_mid[...] + factor * (
        u - normed * jnp.mean(u * normed, axis=-1, keepdims=True)
    )


def expert_unpack_kernel(ff, cut, first, rest, gateup, down):
    for e in range(E):
        gateup[e, :, 0, :] = first[e].astype(F32)
        gateup[e, :, 1, :] = rest[e, :, :ff].astype(F32)
        down[e] = rest[e, :, 2 * ff - cut :].astype(F32)


def route_slots(expert_ids):
    listed = jnp.concatenate([expert_ids[:, 0], expert_ids[:, 1]])
    onehot = (listed[:, None] == jnp.arange(E, dtype=jnp.int32)[None, :]).astype(jnp.int32)
    earlier = jnp.cumsum(onehot, axis=0) - onehot
    return jnp.sum(earlier * onehot, axis=1).reshape(2, -1)


def per_device(
    hidden_in,
    attn_gain,
    query_proj,
    key_value_projection,
    output_proj,
    moe_gain,
    router_proj,
    gateup_proj,
    down_proj,
    segment_index_list,
    expert_ids,
    out_grad,
):
    n_dp, n_tensor = lax.axis_size("dp"), lax.axis_size("tensor")
    own, width = hidden_in.shape
    span = own * n_tensor
    rows = query_proj.shape[0]
    qw = query_proj.shape[1]
    kvw = 2 * key_value_projection.shape[2]
    groups = 2 * qw // kvw
    ff = gateup_proj.shape[3]
    n_groups = n_dp // E
    dp_groups = None
    if n_groups > 1:
        dp_groups = [list(range(g * E, (g + 1) * E)) for g in range(n_groups)]
    dp, rank = lax.axis_index("dp"), lax.axis_index("tensor")
    idx = jnp.stack([dp, rank]).astype(jnp.int32)

    cols = qw + kvw
    early = jnp.concatenate(
        [query_proj, key_value_projection.reshape(rows, kvw), output_proj.T], axis=1
    )
    side = [attn_gain[None, :], moe_gain[None, :], jnp.zeros((6, rows), BF16), router_proj.T]
    side = jnp.pad(jnp.concatenate(side, axis=0), ((0, 0), (0, cols + qw - rows)))
    early = jnp.concatenate([early, side], axis=0)
    x_parts = [hidden_in, swap(hidden_in, "tensor", 1)]

    def slots_of(ids):
        position = route_slots(ids)
        per_rank = CAP // n_tensor
        local = position - rank * per_rank
        ids_t = ids.T
        slots = jnp.where(
            (local >= 0) & (local < per_rank) & (position < CAP), ids_t * SLOT + local, -1
        ).astype(jnp.int32)
        pad = jnp.zeros((4, span), jnp.int32)
        slot_rows = jnp.concatenate([slots, ids_t[::-1], pad], axis=0)
        return slot_rows, slots.T, lax.dynamic_slice_in_dim(ids, rank * own, own, 0)

    longest = segment_index_list.shape[0] // 4
    reach = min(SEQ_SPANS - 1, -(-(longest - 1) // span))
    n_pieces = reach + 1
    tiles = span // BLK

    def keys_of(segments):
        padded = jnp.concatenate([jnp.full((reach * span,), -1, jnp.int32), segments])
        window = lax.dynamic_slice_in_dim(padded, dp * span, n_pieces * span, 0)
        seg_mine = window[reach * span :]
        valid = jnp.minimum(dp % SEQ_SPANS, reach)
        first_seg, last_seg = seg_mine[::BLK], seg_mine[BLK - 1 :: BLK]
        low_tile = jnp.sum(window[None, :] < first_seg[:, None], axis=1) // BLK
        low_tile = jnp.maximum(low_tile, (reach - valid) * tiles)
        full_tile = -(-jnp.sum(window[None, :] < last_seg[:, None], axis=1) // BLK)
        meta = jnp.stack([low_tile, full_tile]).astype(jnp.int32)
        meta_own, meta = jnp.maximum(meta - reach * tiles, 0), jnp.minimum(meta, reach * tiles)
        return meta, meta_own, seg_mine[None, :], seg_mine[:, None], window[: reach * span, None]

    def packed_of(gateup, down):
        return jnp.concatenate(
            [gateup[:, :, 0], gateup[:, :, 1], jnp.transpose(down, (0, 2, 1))], axis=2
        )

    made = {}

    def meanwhile(step, piece):
        if step == 1:
            made["slots"] = slots_of(expert_ids)
            return made["slots"]
        if step == 2:
            made["packed"] = packed_of(after(gateup_proj, piece), down_proj)
            return (made["packed"],)
        if step == 3:
            two = after(x_parts.pop(), piece)
            x_parts.extend([two, swap(two, "tensor", 1)])
            made["keys"] = keys_of(after(segment_index_list, piece))
            return made["keys"]
        return ()

    x_parts.append(swap(hidden_in, "tensor", 2))
    pieces, source = ring_gather(early, "dp", meanwhile)
    slot_rows, slot_cols, ids_own = made["slots"]
    meta, meta_own, qseg, kseg_own, kseg = made["keys"]
    packed = made["packed"]
    w_early, wo, gt, a1, qt, kv = kcall(
        "qkv",
        functools.partial(qkv_kernel, len(pieces), own, rows, qw, cols),
        [
            sds((width, cols), BF16),
            sds((width, qw), BF16),
            sds((16, width), F32),
            sds((span, width), BF16),
            sds((qw, span), BF16),
            sds((span, kvw), BF16),
        ],
        [source, idx],
        pieces + x_parts,
        [
            pltpu.VMEM((span, width), BF16),
            pltpu.VMEM((span, qw), F32),
            pltpu.VMEM((n_dp, 16, rows), F32),
        ],
    )

    def dispatch(parts, with_ids):
        (tiles_,) = kcall(
            "dispatch",
            functools.partial(dispatch_kernel, own, with_ids),
            [sds((E * SLOT, width), BF16)],
            [idx],
            [slot_rows] + parts,
            [pltpu.VMEM((span, width), BF16), pltpu.VMEM((E * SLOT, span), BF16)],
        )
        return tiles_

    half = kvw // 2
    far = [shifted(kv, "dp", d) for d in range(1, n_pieces)]
    acc, top, total = kcall(
        "attend_own",
        functools.partial(attend_kernel, 1, groups, True),
        [sds((qw, span), F32), sds((8, span), F32), sds((8, span), F32)],
        [meta_own],
        [qt, qseg, kseg_own, kv],
        [pltpu.VMEM((span, half), BF16), pltpu.VMEM((half, span), BF16)],
    )

    g_in = after(out_grad, qt)
    g_core, g_across = swap(g_in, "tensor", 1), swap(g_in, "tensor", 2)
    far[-1] = after(far[-1], acc, g_across)
    near = exchange(after(packed, qt), dp_groups)
    w_expert = near.reshape(E * rows, 3 * ff)
    if n_groups > 1:
        shape = (n_groups, E * rows, 3 * ff)
        whole = jnp.zeros(shape, BF16)
        for h in range(n_groups):
            part = w_expert if h == 0 else swap(near.reshape(E * rows, 3 * ff), "dp", h * E)
            whole = lax.dynamic_update_index_in_dim(whole, part, (dp // E) ^ h, 0)
        w_expert = whole.reshape(width, 3 * ff)
    w_core = swap(w_expert, "tensor", 1)

    att, lse, low = kcall(
        "attend_far",
        functools.partial(attend_kernel, reach, groups, False),
        [sds((qw, span), F32), sds((8, span), F32), sds((span, qw), BF16)],
        [meta],
        [qt, qseg, kseg] + far + [acc, top, total],
        [pltpu.VMEM((reach * span, half), BF16), pltpu.VMEM((half, reach * span), BF16)],
    )
    def quarters(wide):
        return [sds((own, wide), BF16), sds((own, wide), BF16), sds((2, own, wide), BF16)]

    keep, other, send = kcall(
        "project",
        functools.partial(project_kernel, own),
        quarters(width),
        [idx],
        [low, wo],
    )
    mid_terms, across = scatter_tensor(keep, other, send)
    middle, a2 = kcall(
        "middle",
        middle_kernel,
        [sds((own, width), F32), sds((own, width), BF16)],
        [],
        [hidden_in, gt] + mid_terms,
    )

    g_parts = [out_grad, g_core, g_across, after(swap(g_across, "tensor", 1), across)]
    g_slots = exchange(after(dispatch(g_parts, True), w_expert), dp_groups)
    a2_parts = gather_tensor(a2)
    w_across = swap(after(w_expert, a2_parts[2]), "tensor", 2)
    w_parts = [w_expert, w_core, w_across, swap(w_across, "tensor", 1)]
    x_slots = exchange(after(dispatch(a2_parts, False), g_slots), dp_groups)
    n_slots = E * SLOT
    s_slots, hid, slot_weight, dx = kcall(
        "expert",
        functools.partial(expert_kernel, ff),
        [
            sds((n_slots, width), BF16),
            sds((4, n_slots, 3 * ff), BF16),
            sds((n_slots, 1), F32),
            sds((n_slots, width), BF16),
        ],
        [idx],
        [x_slots, g_slots] + w_parts + [gt],
        [pltpu.VMEM((n_slots, width), F32)],
    )
    cut = ff

    def expert_grad(first):
        return kcall(
            "expert_grad",
            functools.partial(expert_grad_kernel, ff, cut, first),
            [sds((width, cut if first else 3 * ff - cut), BF16)] * 4,
            [],
            [x_slots, s_slots, hid],
        )

    dx_back = exchange(dx, dp_groups)
    keep_a, near_a, other_a, far_a = expert_grad(True)
    keep_b, near_b, other_b, far_b = expert_grad(False)
    (out_slots,) = kcall(
        "expert_out",
        functools.partial(expert_out_kernel, ff),
        [sds((n_slots, width), BF16)],
        [],
        [hid, slot_weight] + w_parts,
        [pltpu.VMEM((n_slots, width), F32)],
    )
    second_a = (other_a.astype(F32) + swap(far_a, "tensor", 1).astype(F32)).astype(BF16)
    second_b = (other_b.astype(F32) + swap(far_b, "tensor", 1).astype(F32)).astype(BF16)
    got_a, got_b = swap(near_a, "tensor", 1), swap(near_b, "tensor", 1)
    last_a = swap(second_a, "tensor", 2)
    dx_back = after(dx_back, keep_a, keep_b, out_slots)

    def combine(parts_, with_q, *others):
        wide = width + (EXTRA if with_q else 0)
        keep, other, send = kcall(
            "combine" if with_q else "combine_out",
            functools.partial(combine_kernel, own, with_q),
            quarters(wide),
            [idx],
            [slot_cols, parts_],
            [pltpu.VMEM((E * SLOT, wide), BF16)],
        )
        return scatter_tensor(keep, other, after(send, *others) if others else send)

    def expert_total(kept, got, last):
        total = (kept.astype(F32) + got.astype(F32) + last.astype(F32)).astype(BF16)
        if n_groups > 1:
            group = dp // E
            blocks = total.reshape(n_groups, E * rows, -1)
            total = lax.dynamic_index_in_dim(blocks, group, 0, keepdims=False).astype(F32)
            for h in range(1, n_groups):
                there = lax.dynamic_index_in_dim(blocks, group ^ h, 0, keepdims=False)
                total = total + swap(there, "dp", h * E).astype(F32)
            total = total.astype(BF16)
        return total.reshape(E, rows, -1)

    back_terms, across = combine(dx_back, True, last_a)
    total_a = expert_total(keep_a, got_a, last_a)
    back_terms[0] = after(back_terms[0], second_b, total_a)
    out_back = exchange(after(out_slots, across), dp_groups)
    grad_middle, branch, small_two = kcall(
        "middle_back",
        middle_back_kernel,
        [sds((own, width), F32), sds((own, width), BF16), sds((16, width), F32)],
        [],
        [middle, a2, out_grad, ids_own, gt] + back_terms,
    )
    branch_parts = gather_tensor(branch)
    last_b = swap(after(second_b, branch_parts[2]), "tensor", 2)

    heads = qw // HEAD
    g_heads, delta, mine, theirs = kcall(
        "branch",
        functools.partial(branch_kernel, own, rows, heads),
        [
            sds((qw, span), BF16),
            sds((8, span), F32),
            sds((width // 2, qw + EXTRA), BF16),
            sds((width // 2, qw + EXTRA), BF16),
        ],
        [idx],
        branch_parts + [att, low, wo, small_two],
        [pltpu.VMEM((span, width), BF16), pltpu.VMEM((width, qw + EXTRA), BF16)],
    )
    own_a = exchange(after(total_a, out_back, g_heads), dp_groups)
    pairs = [list(range(p, n_dp, 2)) for p in range(2)]

    def pair_sum(mine, theirs, *others):
        got = swap(theirs, "dp", 1)
        got = after(got, *others) if others else got
        return (mine.astype(F32) + got.astype(F32)).astype(BF16)

    def owner_sum(value, *others, late=()):
        parts = after(exchange(after(value, *others), pairs), *late)
        return jnp.sum(parts.reshape(n_dp // 2, rows, -1).astype(F32), axis=0)

    out_pair = pair_sum(mine, theirs)
    outs = kcall(
        "attend_back_far",
        functools.partial(attend_back_kernel, reach, groups, False),
        [sds((qw, span), F32)] + [sds((kvw, span), BF16)] * reach,
        [meta],
        [qt, g_heads, lse, delta, qseg, kseg] + far,
        [
            pltpu.VMEM((reach * span, half), BF16),
            pltpu.VMEM((reach * span, half), BF16),
            pltpu.VMEM((half, reach * span), BF16),
            pltpu.VMEM((kvw, reach * span), F32),
        ],
    )
    dkv_far = [shifted(outs[d], "dp", -d) for d in range(1, n_pieces)]
    dq, dkv_own = kcall(
        "attend_back_own",
        functools.partial(attend_back_kernel, 1, groups, True),
        [sds((qw, span), BF16), sds((kvw, span), F32)],
        [meta_own],
        [qt, g_heads, lse, delta, qseg, kseg_own, kv, after(outs[0], own_a)],
        [
            pltpu.VMEM((span, half), BF16),
            pltpu.VMEM((span, half), BF16),
            pltpu.VMEM((half, span), BF16),
        ],
    )
    out_sum = owner_sum(out_pair, own_a)
    total_b = expert_total(keep_b, got_b, after(last_b, dq))
    own_b = exchange(after(total_b, out_sum, *dkv_far), dp_groups)

    nat_q, mine, theirs = kcall(
        "query_grad",
        functools.partial(query_grad_kernel, rows),
        [
            sds((span, qw), BF16),
            sds((width // 2, qw), BF16),
            sds((width // 2, qw), BF16),
        ],
        [idx],
        [after(dq, out_sum, *dkv_far), a1],
        [pltpu.VMEM((width, qw), BF16)],
    )
    q_sum = owner_sum(pair_sum(mine, theirs), own_b)
    keep_h, other_h, send_h, nat_kv, small_one = kcall(
        "input_back",
        functools.partial(input_back_kernel, n_pieces, own),
        quarters(width) + [sds((span, kvw), BF16), sds((16, width), F32)],
        [idx],
        [nat_q, w_early, a1, gt, dkv_own] + dkv_far,
    )
    in_terms, _ = scatter_tensor(keep_h, other_h, send_h)
    gain_sum = small_one + swap(small_one, "tensor", 1)
    gain_sum = gain_sum + swap(gain_sum, "tensor", 2)
    mine, theirs = kcall(
        "keyval_grad",
        functools.partial(keyval_grad_kernel, rows),
        [
            sds((width // 2, kvw + EXTRA), BF16),
            sds((width // 2, kvw + EXTRA), BF16),
        ],
        [idx],
        [a1, nat_kv, gain_sum],
        [pltpu.VMEM((width, kvw + EXTRA), BF16)],
    )
    (input_grad,) = kcall(
        "input_grad",
        input_grad_kernel,
        [sds((own, width), F32)],
        [],
        [hidden_in, gt, grad_middle] + in_terms,
    )

    out_terms, _ = combine(after(out_back, theirs), False)
    hidden_out = (
        middle + out_terms[0].astype(F32) + out_terms[1][0].astype(F32) + out_terms[2].astype(F32)
    ).astype(BF16)
    gateup_grad, down_grad = kcall(
        "expert_unpack",
        functools.partial(expert_unpack_kernel, ff, cut),
        [sds((E, rows, 2, ff), F32), sds((E, rows, ff), F32)],
        [],
        [own_a, own_b],
    )
    o_sum = out_sum[:, :qw].T
    side = out_sum[:, qw : qw + 16]
    side = side + swap(side, "tensor", 1)
    side = side + swap(side, "tensor", 2)
    ready = (input_grad, hidden_out, gateup_grad, down_grad, q_sum, o_sum, side)
    kv_sum = owner_sum(pair_sum(mine, theirs, q_sum), late=ready)
    return (
        hidden_out,
        input_grad,
        kv_sum[:, kvw],
        q_sum,
        kv_sum[:, :kvw].reshape(rows, 2, kvw // 2),
        o_sum,
        side[:, 1],
        side[:, 8:16],
        gateup_grad,
        jnp.transpose(down_grad, (0, 2, 1)),
    )


def solution(mesh):
    return jax.shard_map(
        per_device,
        mesh=mesh,
        in_specs=(
            P(("dp", "tensor"), None),
            P("dp"),
            P("dp", "tensor"),
            P("dp", None, "tensor"),
            P("tensor", "dp"),
            P("dp"),
            P("dp", None),
            P(None, "dp", None, "tensor"),
            P(None, "tensor", "dp"),
            P(),
            P("dp", None),
            P(("dp", "tensor"), None),
        ),
        out_specs=(
            P(("dp", "tensor"), None),
            P(("dp", "tensor"), None),
            P("dp"),
            P("dp", "tensor"),
            P("dp", None, "tensor"),
            P("tensor", "dp"),
            P("dp"),
            P("dp", None),
            P(None, "dp", None, "tensor"),
            P(None, "tensor", "dp"),
        ),
        check_vma=False,
    )
```

```python
import functools

import jax
import jax.numpy as jnp
from jax import lax
from jax.experimental import pallas as pl
from jax.experimental.pallas import tpu as pltpu
from jax.sharding import PartitionSpec as P

HEAD = 64
E = 8
SEQ_SPANS = 8
CAP = 240
SLOT = 64
BLK = 384
FAR_Q, FAR_K = 384, 768
EXTRA = 128

NORM_EPS = 1e-05
NEG = -1e30

F32 = jnp.float32
BF16 = jnp.bfloat16


def dg(a, b, ca, cb):
    return lax.dot_general(a, b, (((ca,), (cb,)), ((), ())), preferred_element_type=F32)


def sds(shape, dtype):
    return jax.ShapeDtypeStruct(shape, dtype)


TIMES = {
    "qkv": 7,
    "attend_own": 14,
    "attend_far": 20,
    "project": 4,
    "middle": 3,
    "dispatch": 4,
    "expert": 17,
    "expert_grad": 3,
    "expert_out": 3,
    "combine": 12,
    "combine_out": 1,
    "middle_back": 5,
    "branch": 6,
    "attend_back_far": 20,
    "attend_back_own": 14,
    "query_grad": 1,
    "input_back": 1,
    "keyval_grad": 1,
    "input_grad": 1,
    "expert_unpack": 1,
}


def kcall(name, body, outs, smem, vmem, scratch=(), hbm=(), limit=60):
    return pl.pallas_call(
        body,
        name=name,
        out_shape=list(outs),
        in_specs=[pl.BlockSpec(memory_space=pltpu.SMEM)] * len(smem)
        + [pl.BlockSpec(memory_space=pltpu.VMEM)] * len(vmem)
        + [pl.BlockSpec(memory_space=pl.ANY)] * len(hbm),
        out_specs=[pl.BlockSpec(memory_space=pltpu.VMEM)] * len(outs),
        scratch_shapes=list(scratch),
        compiler_params=pltpu.CompilerParams(vmem_limit_bytes=limit << 20),
        cost_estimate=pl.CostEstimate(
            flops=TIMES[name] * 10**9, bytes_accessed=10**6, transcendentals=0
        ),
    )(*smem, *vmem, *hbm)


def swap(value, axis, by):
    size = lax.axis_size(axis)
    return lax.ppermute(value, axis, [(i, i ^ by) for i in range(size)])


def shifted(value, axis, by):
    size = lax.axis_size(axis)
    return lax.ppermute(value, axis, [(i, i + by) for i in range(size) if 0 <= i + by < size])


def gather_tensor(value):
    one = swap(value, "tensor", 1)
    two = swap(value, "tensor", 2)
    return [value, one, two, swap(two, "tensor", 1)]


def scatter_tensor(keep, other, send):
    got = swap(send, "tensor", 1)
    second = (other.astype(F32) + got[1].astype(F32)).astype(BF16)
    return [keep, got, swap(second, "tensor", 2)], second


def three(kept, got, last):
    return kept[...].astype(F32) + got[0].astype(F32) + last[...].astype(F32)


def ring_pos(index, size):
    return jnp.where(index % 2 == 0, index // 2, size - 1 - (index - 1) // 2)


def ring_dev(pos, size):
    pos = pos % size
    return jnp.where(pos < size // 2, 2 * pos, 2 * (size - 1 - pos) + 1)


def ring_gather(value, axis, meanwhile):
    size = lax.axis_size(axis)
    order = list(range(0, size, 2)) + list(range(size - 1, 0, -2))
    ahead = [(order[k], order[(k + 1) % size]) for k in range(size)]
    back = [(b, a) for a, b in ahead]
    half = value.shape[0] // 16 * 8
    index = lax.axis_index(axis)
    pos = ring_pos(index, size)
    pieces, source = [value], [index]
    one = two = value
    for step in range(1, size // 2 + 1):
        last = step == size // 2
        got_one = lax.ppermute(one[:half] if last else one, axis, ahead)
        got_two = lax.ppermute(two[half:] if last else two, axis, back)
        done = meanwhile(step, one)
        one, two = (after(got_one, *done), got_two) if done else (got_one, got_two)
        pieces += [one, two]
        source += [ring_dev(pos - step, size), ring_dev(pos + step, size)]
    return pieces, jnp.stack(source).astype(jnp.int32)


def exchange(value, groups=None):
    return lax.all_to_all(
        value, "dp", split_axis=0, concat_axis=0, axis_index_groups=groups, tiled=True
    )


def after(value, *others):
    return lax.optimization_barrier((value,) + others)[0]


def qkv_kernel(n, own, rows, qw, cols, src_ref, idx_ref, *refs):
    pieces = refs[:n]
    xs = refs[n : n + 4]
    w, wo, gt, a1, qt, kv, xb, qn, gs = refs[n + 4 :]
    rank = idx_ref[1]
    for k in range(n):
        piece = pieces[k]
        first = pieces[n - 2].shape[0] if k == n - 1 else 0
        last = min(first + piece.shape[0], rows)
        at = pl.ds(pl.multiple_of(src_ref[k] * rows + first, 8), last - first)
        w[at, :] = piece[: last - first, :cols]
        wo[at, :] = piece[: last - first, cols:]
        if first + piece.shape[0] > rows:
            gs[pl.ds(src_ref[k], 1)] = piece[last - first :, :rows].astype(F32)[None]
    for d in range(4):
        xb[pl.ds(pl.multiple_of((rank ^ d) * own, 16), own), :] = xs[d][...]
    gt[...] = jnp.concatenate([gs[j] for j in range(gs.shape[0])], axis=1)

    def block(j, _):
        at = pl.ds(pl.multiple_of(j * own, 16), own)
        x = xb[at, :].astype(F32)
        factor = lax.rsqrt(jnp.mean(x * x, axis=-1, keepdims=True) + NORM_EPS)
        a = (x * factor * gt[0:1, :]).astype(BF16)
        a1[at, :] = a
        y = dg(a, w[...], 1, 0)
        qn[at, :] = y[:, :qw] * (HEAD**-0.5)
        kv[at, :] = y[:, qw:].astype(BF16)
        return 0

    lax.fori_loop(0, 4, block, 0)
    qt[...] = jnp.transpose(qn[...]).astype(BF16)


def tile_loop(meta_ref, qb, end, body, carry):
    low, full = meta_ref[0, qb], meta_ref[1, qb]
    carry = lax.fori_loop(low, jnp.minimum(full, end), lambda t, c: body(t, True, c), carry)
    return lax.fori_loop(jnp.maximum(full, low), end, lambda t, c: body(t, False, c), carry)


def allowed_mask(ks, diag, qseg, kseg):
    ok = kseg[ks, :] == qseg
    if diag:
        keys = lax.broadcasted_iota(jnp.int32, (BLK, BLK), 0)
        ok = ok & (keys <= lax.broadcasted_iota(jnp.int32, (BLK, BLK), 1))
    return ok


def attend_kernel(np_, groups, local, meta_ref, *refs):
    qt, qseg_ref, kseg = refs[:3]
    kvs = refs[3 : 3 + np_]
    if local:
        acc_ref, m_ref, l_ref, kb, vt = refs[3 + np_ :]
    else:
        acc_in, m_in, l_in, att, lse, low, kb, vt = refs[3 + np_ :]
    span = qt.shape[1]
    n_q, n_k = (BLK, BLK) if local else (FAR_Q, FAR_K)
    half = kb.shape[1]
    kv_heads = half // HEAD
    for d in range(np_):
        at = (np_ - 1 - d) * span
        kb[at : at + span, :] = kvs[d][:, :half]
        vt[:, at : at + span] = jnp.transpose(kvs[d][:, half:].astype(F32)).astype(BF16)

    def q_block(qb, _):
        qs = pl.ds(pl.multiple_of(qb * n_q, n_q), n_q)
        qseg = qseg_ref[:, qs]
        for n in range(kv_heads):
            heads = [n * groups + g for g in range(groups)]
            sl = [slice(h * HEAD, (h + 1) * HEAD) for h in heads]
            q = [qt[r, qs] for r in sl]

            def tile(t, masked, carry, diag=False):
                ks = pl.ds(pl.multiple_of(t * n_k, n_k), n_k)
                k = kb[ks, n * HEAD : (n + 1) * HEAD]
                v = vt[n * HEAD : (n + 1) * HEAD, ks]
                ok = allowed_mask(ks, diag, qseg, kseg) if masked else None
                out = []
                for g in range(groups):
                    m, l, acc = carry[g]
                    s = dg(k, q[g], 1, 0)
                    if masked:
                        s = jnp.where(ok, s, NEG)
                    m_new = jnp.maximum(m, jnp.max(s, axis=0, keepdims=True))
                    e = jnp.exp(s - m_new)
                    shrink = jnp.exp(m - m_new)
                    l = l * shrink + jnp.sum(e, axis=0, keepdims=True)
                    acc = acc * shrink + dg(v, e.astype(BF16), 1, 0)
                    out.append((m_new, l, acc))
                return tuple(out)

            if local:
                none = jnp.full((1, BLK), NEG, F32)
                init = (none, jnp.zeros((1, BLK), F32), jnp.zeros((HEAD, BLK), F32))
                state = tile(qb, True, (init,) * groups, True)
                state = tile_loop(meta_ref, qb, qb, tile, state)
                for g in range(groups):
                    h = heads[g]
                    m_ref[h : h + 1, qs], l_ref[h : h + 1, qs], acc_ref[sl[g], qs] = state[g]
            else:
                state = tuple(
                    (m_in[h : h + 1, qs], l_in[h : h + 1, qs], acc_in[r, qs])
                    for h, r in zip(heads, sl)
                )
                state = tile_loop(meta_ref, qb, np_ * (span // n_k), tile, state)
                for g in range(groups):
                    m, l, acc = state[g]
                    att[sl[g], qs] = acc / l
                    lse[heads[g] : heads[g] + 1, qs] = m + jnp.log(l)
        return 0

    lax.fori_loop(0, span // n_q, q_block, 0)
    if not local:
        low[...] = jnp.transpose(att[...]).astype(BF16)


def put_quarter(d, part, keep, other, send):
    if d % 2:
        send[d // 2] = part.astype(BF16)
    else:
        (other if d else keep)[...] = part.astype(BF16)


def project_kernel(own, idx_ref, low, wo, keep, other, send):
    rank = idx_ref[1]
    for d in range(4):
        rows = pl.ds(pl.multiple_of((rank ^ d) * own, 16), own)
        put_quarter(d, dg(low[rows, :], wo[...], 1, 1), keep, other, send)


def middle_kernel(x, gt, kept, got, last, middle, a2):
    mid = x[...].astype(F32) + three(kept, got, last)
    middle[...] = mid
    factor = lax.rsqrt(jnp.mean(mid * mid, axis=-1, keepdims=True) + NORM_EPS)
    a2[...] = (mid * factor * gt[1:2, :]).astype(BF16)


def select_tile(e, rows_ref, k=None):
    slot = e * SLOT + lax.broadcasted_iota(jnp.int32, (SLOT, rows_ref.shape[1]), 0)
    first, second = slot == rows_ref[0:1, :], slot == rows_ref[1:2, :]
    hit = (first | second) if k is None else (second if k else first)
    return jnp.where(hit, 1.0, 0.0).astype(BF16)


def dispatch_kernel(own, with_ids, idx_ref, rows_ref, *refs):
    xs, out = refs[:4], refs[4]
    xb, pick = refs[5:]
    rank = idx_ref[1]
    for d in range(4):
        xb[pl.ds(pl.multiple_of((rank ^ d) * own, 16), own), :] = xs[d][...]
    for e in range(E):
        pick[e * SLOT : (e + 1) * SLOT, :] = select_tile(e, rows_ref)
    width = 512
    for c in range(xb.shape[1] // width):
        lanes = slice(c * width, (c + 1) * width)
        y = dg(pick[...], xb[:, lanes], 1, 0)
        if not (with_ids and c == 0):
            out[:, lanes] = y.astype(BF16)
            continue
        ids = rows_ref[2:4, :].astype(F32).astype(BF16)
        for e in range(E):
            rows = slice(e * SLOT, (e + 1) * SLOT)
            row = dg(ids, select_tile(e, rows_ref, 0), 1, 1)[0:1]
            row = row + dg(ids, select_tile(e, rows_ref, 1), 1, 1)[1:2]
            row = jnp.concatenate([row, jnp.zeros((1, width - SLOT), F32)], axis=1)
            at = lax.broadcasted_iota(jnp.int32, (SLOT, width), 0)
            out[rows, lanes] = jnp.where(at == SLOT - 4, row, y[rows]).astype(BF16)


def eye():
    shape = (SLOT, SLOT)
    return lax.broadcasted_iota(jnp.int32, shape, 0) == lax.broadcasted_iota(jnp.int32, shape, 1)


def row_to_col(row):
    return jnp.sum(jnp.where(eye(), row, 0.0), axis=1, keepdims=True)


def col_to_row(col):
    return jnp.sum(jnp.where(eye(), col, 0.0), axis=0, keepdims=True)


def split_three(value):
    one = value.astype(BF16).astype(F32)
    two = (value - one).astype(BF16).astype(F32)
    return one, two, (value - one - two).astype(BF16).astype(F32)


def expert_kernel(ff, idx_ref, x_ref, gs, gt, w0, w1, w2, w3, so, ho, wo, dxo, dx, qs, wb, sems):
    index = idx_ref[0] % E
    ws = (w0, w1, w2, w3)
    for f in range(4):
        pltpu.make_async_copy(ws[f], wb.at[f], sems.at[f]).start()
    x = x_ref[...]
    logits = dg(x, gt[8:16, :].astype(BF16), 1, 1)
    lane = lax.broadcasted_iota(jnp.int32, (SLOT, E), 1)
    weights = []
    for d in range(E):
        rows = slice(d * SLOT, (d + 1) * SLOT)
        part = logits[rows]
        side = gs[(d + 1) * SLOT - 8 : (d + 1) * SLOT, 0:SLOT].astype(F32)
        other = row_to_col(side[4:5]).astype(jnp.int32)
        mine = jnp.sum(jnp.where(lane == index, part, 0.0), axis=1, keepdims=True)
        theirs = jnp.sum(jnp.where(lane == other, part, 0.0), axis=1, keepdims=True)
        weight = 1.0 / (1.0 + jnp.exp(theirs - mine))
        real = lax.broadcasted_iota(jnp.int32, (SLOT, 1), 0) < SLOT - 4
        weight = jnp.where(real, weight, 0.0)
        weights.append(weight)
        so[rows, :] = jnp.where(real, weight * gs[rows, :].astype(F32), 0.0).astype(BF16)
    wo[...] = jnp.concatenate(weights, axis=0)
    qs[...] = jnp.zeros_like(qs)
    dx[...] = jnp.zeros_like(dx)

    def hidden_slice(f, _):
        pltpu.make_async_copy(w0, wb.at[f], sems.at[f]).wait()
        gate = dg(x_ref[...], wb[f, :, :ff], 1, 0)
        up = dg(x_ref[...], wb[f, :, ff : 2 * ff], 1, 0)
        hidden = dg(so[...], wb[f, :, 2 * ff :], 1, 0)
        sig = 1.0 / (1.0 + jnp.exp(-gate))
        act = gate * sig * up
        qs[...] += jnp.sum(hidden * act, axis=1, keepdims=True)
        ho[f, :, :ff] = (hidden * up * sig * (1.0 + gate * (1.0 - sig))).astype(BF16)
        ho[f, :, ff : 2 * ff] = (hidden * gate * sig).astype(BF16)
        ho[f, :, 2 * ff :] = act.astype(BF16)
        dx[...] += dg(ho[f, :, : 2 * ff], wb[f, :, : 2 * ff], 1, 1)
        return 0

    lax.fori_loop(0, 4, hidden_slice, 0)
    q = qs[...]
    dxo[...] = dx[...].astype(BF16)
    for d in range(E):
        rows = slice(d * SLOT, (d + 1) * SLOT)
        head = dx[rows, 0:128]
        at = lax.broadcasted_iota(jnp.int32, head.shape, 0)
        row = jnp.concatenate([col_to_row(q[rows]), jnp.zeros((1, 128 - SLOT), F32)], axis=1)
        for k, term in enumerate(split_three(row)):
            head = jnp.where(at == SLOT - 4 + k, term, head)
        dxo[rows, 0:128] = head.astype(BF16)


def expert_grad_kernel(ff, cut, first, x, s, h, *outs):
    for f in range(4):
        out = outs[f]
        if first:
            out[...] = dg(x[...], h[f, :, :cut], 0, 0).astype(BF16)
        else:
            out[:, : 2 * ff - cut] = dg(x[...], h[f, :, cut : 2 * ff], 0, 0).astype(BF16)
            out[:, 2 * ff - cut :] = dg(s[...], h[f, :, 2 * ff :], 0, 0).astype(BF16)


def expert_out_kernel(ff, h, weight, w0, w1, w2, w3, out, acc):
    for f, w in enumerate((w0, w1, w2, w3)):
        part = dg(h[f, :, 2 * ff :], w[:, 2 * ff :], 1, 1)
        acc[...] = part if f == 0 else acc[...] + part
    out[...] = (acc[...] * weight[...]).astype(BF16)


def combine_kernel(own, with_q, idx_ref, cols, parts, keep, other, send, y):
    rank = idx_ref[1]
    width = parts.shape[1]
    y[:, :width] = parts[...]
    if with_q:
        for e in range(E):
            rows = slice(e * SLOT, (e + 1) * SLOT)
            tail = parts[(e + 1) * SLOT - 8 : (e + 1) * SLOT, 0:SLOT].astype(F32)
            lane = lax.broadcasted_iota(jnp.int32, (SLOT, EXTRA), 1)
            side = jnp.zeros((SLOT, EXTRA), F32)
            for k in range(3):
                side = jnp.where(lane == e + 8 * k, row_to_col(tail[4 + k : 5 + k]), side)
            y[rows, width:] = side.astype(BF16)
    slot = lax.broadcasted_iota(jnp.int32, (own, E * SLOT), 1)
    for d in range(4):
        at = pl.ds(pl.multiple_of((rank ^ d) * own, 16), own)
        hit = (cols[at, 0:1] == slot) | (cols[at, 1:2] == slot)
        part = dg(jnp.where(hit, 1.0, 0.0).astype(BF16), y[...], 1, 0)
        put_quarter(d, part, keep, other, send)


def middle_back_kernel(mid_ref, a2, g, ids, gt, kept, got, last, grad_mid, branch, small):
    width = mid_ref.shape[1]
    total = three(kept, got, last)
    h2, side = total[:, :width], total[:, width:]
    own = h2.shape[0]
    logits = dg(a2[...], gt[8:16, :].astype(BF16), 1, 1)
    lane = lax.broadcasted_iota(jnp.int32, (own, E), 1)
    q = side[:, 0:8] + side[:, 8:16] + side[:, 16:24]
    hit = [lane == ids[:, k : k + 1] for k in range(2)]
    logit = [jnp.sum(jnp.where(hit[k], logits, 0.0), axis=1, keepdims=True) for k in range(2)]
    terms = [jnp.sum(jnp.where(hit[k], q, 0.0), axis=1, keepdims=True) for k in range(2)]
    both = terms[0] + terms[1]
    logit_grad = jnp.zeros((own, E), F32)
    for k in range(2):
        weight = 1.0 / (1.0 + jnp.exp(logit[1 - k] - logit[k]))
        logit_grad = jnp.where(hit[k], terms[k] - weight * both, logit_grad)
    high = logit_grad.astype(BF16)
    rest = (logit_grad - high.astype(F32)).astype(BF16)
    router = gt[8:16, :].astype(BF16)
    h2 = h2 + dg(high, router, 1, 0) + dg(rest, router, 1, 0)
    mid = mid_ref[...]
    factor = lax.rsqrt(jnp.mean(mid * mid, axis=-1, keepdims=True) + NORM_EPS)
    normed = mid * factor
    u = h2 * gt[1:2, :]
    back = g[...].astype(F32) + factor * (
        u - normed * jnp.mean(u * normed, axis=-1, keepdims=True)
    )
    grad_mid[...] = back
    branch[...] = back.astype(BF16)
    small[...] = jnp.zeros_like(small)
    small[1:2, :] = jnp.sum(h2 * normed, axis=0, keepdims=True)
    small[8:16, :] = dg(high, a2[...], 0, 0) + dg(rest, a2[...], 0, 0)


def branch_kernel(own, rows, heads, idx_ref, *refs):
    bs = refs[:4]
    att, low, wo, small = refs[4:8]
    gt, delta, mine, theirs, full, grad = refs[8:]
    rank = idx_ref[1]
    qw = wo.shape[1]
    for d in range(4):
        full[pl.ds(pl.multiple_of((rank ^ d) * own, 16), own), :] = bs[d][...]
    gt[...] = dg(wo[...], full[...], 0, 1).astype(BF16)
    for h in range(heads):
        at = slice(h * HEAD, (h + 1) * HEAD)
        delta[h : h + 1, :] = jnp.sum(gt[at, :].astype(F32) * att[at, :], axis=0, keepdims=True)
    grad[...] = dg(full[...], low[...], 0, 0).astype(BF16)
    by_parity(rows, idx_ref[0] % 2, grad, mine, theirs, small)


def by_parity(rows, parity, grad, mine, theirs, side=None):
    n = grad.shape[0] // rows
    block = mine.shape[0] * 2 // n
    for k in range(n // 2):
        for out, p in ((mine, parity), (theirs, 1 - parity)):
            at = pl.ds(pl.multiple_of((2 * k + p) * rows, 8), rows)
            out[k * block : k * block + rows, :] = grad[at, :]
        if side is not None:
            tail = slice(k * block + rows, (k + 1) * block)
            pad = jnp.zeros((block - rows, grad.shape[1] - rows), F32)
            even, odd = [
                jnp.concatenate([side[: block - rows, j * rows : (j + 1) * rows], pad], axis=1)
                for j in (2 * k, 2 * k + 1)
            ]
            mine[tail, :] = jnp.where(parity == 0, even, odd).astype(BF16)
            theirs[tail, :] = jnp.where(parity == 0, odd, even).astype(BF16)


def attend_back_kernel(np_, groups, local, meta_ref, *refs):
    qt, gt, lse, delta, qseg_ref, kseg = refs[:6]
    kvs = refs[6 : 6 + np_]
    refs = refs[6 + np_ :]
    if local:
        dq_in, dq, dkv, kb, vb, kt = refs
    else:
        dq = refs[0]
        dkvs = refs[1 : 1 + np_]
        kb, vb, kt, dkv = refs[1 + np_ :]
    span = qt.shape[1]
    n_q, n_k = (BLK, BLK) if local else (FAR_Q, FAR_K)
    half = kb.shape[1]
    kv_heads = half // HEAD
    for d in range(np_):
        at = (np_ - 1 - d) * span
        kb[at : at + span, :] = kvs[d][:, :half]
        vb[at : at + span, :] = kvs[d][:, half:]
        kt[:, at : at + span] = jnp.transpose(kvs[d][:, :half].astype(F32)).astype(BF16)
    dkv[...] = jnp.zeros_like(dkv)

    def q_block(qb, _):
        qs = pl.ds(pl.multiple_of(qb * n_q, n_q), n_q)
        qseg = qseg_ref[:, qs]
        for n in range(kv_heads):
            heads = [n * groups + g for g in range(groups)]
            sl = [slice(h * HEAD, (h + 1) * HEAD) for h in heads]
            q = [qt[r, qs] for r in sl]
            go = [gt[r, qs] for r in sl]
            ls = [lse[h : h + 1, qs] for h in heads]
            de = [delta[h : h + 1, qs] for h in heads]

            def tile(t, masked, carry, diag=False):
                ks = pl.ds(pl.multiple_of(t * n_k, n_k), n_k)
                lanes = slice(n * HEAD, (n + 1) * HEAD)
                k, v, k_t = kb[ks, lanes], vb[ks, lanes], kt[lanes, ks]
                ok = allowed_mask(ks, diag, qseg, kseg) if masked else None
                out = []
                dk = dv = None
                for g in range(groups):
                    p = jnp.exp(dg(k, q[g], 1, 0) - ls[g])
                    if masked:
                        p = jnp.where(ok, p, 0.0)
                    ds = (p * (dg(v, go[g], 1, 0) - de[g])).astype(BF16)
                    one = dg(q[g], ds, 1, 1)
                    two = dg(go[g], p.astype(BF16), 1, 1)
                    dk = one if dk is None else dk + one
                    dv = two if dv is None else dv + two
                    out.append(carry[g] + dg(k_t, ds, 1, 0))
                dkv[n * HEAD : (n + 1) * HEAD, ks] += dk
                dkv[half + n * HEAD : half + (n + 1) * HEAD, ks] += dv
                return tuple(out)

            if local:
                state = tile(qb, True, tuple(dq_in[r, qs] for r in sl), True)
                state = tile_loop(meta_ref, qb, qb, tile, state)
                for g in range(groups):
                    dq[sl[g], qs] = (state[g] * (HEAD**-0.5)).astype(BF16)
            else:
                state = tuple(jnp.zeros((HEAD, n_q), F32) for _ in range(groups))
                state = tile_loop(meta_ref, qb, np_ * (span // n_k), tile, state)
                for g in range(groups):
                    dq[sl[g], qs] = state[g]
        return 0

    lax.fori_loop(0, span // n_q, q_block, 0)
    if not local:
        for d in range(np_):
            at = (np_ - 1 - d) * span
            dkvs[d][...] = dkv[:, at : at + span].astype(BF16)


def query_grad_kernel(rows, idx_ref, dq, a1, nat, mine, theirs, grad):
    nat[...] = jnp.transpose(dq[...].astype(F32)).astype(BF16)
    grad[...] = dg(a1[...], nat[...], 0, 0).astype(BF16)
    by_parity(rows, idx_ref[0] % 2, grad, mine, theirs)


def input_back_kernel(np_, own, idx_ref, *refs):
    nat_q, w, a1, gt = refs[:4]
    dkvs = refs[4 : 4 + np_]
    keep, other, send, nat, small = refs[4 + np_ :]
    rank = idx_ref[1]
    total = dkvs[0][...]
    for d in range(1, np_):
        total = total + dkvs[d][...].astype(F32)
    qw = nat_q.shape[1]
    nat[...] = jnp.transpose(total).astype(BF16)
    gain = jnp.zeros((1, w.shape[0]), F32)
    for d in range(4):
        rows = pl.ds(pl.multiple_of((rank ^ d) * own, 16), own)
        part = dg(nat_q[rows, :], w[:, :qw], 1, 1) + dg(nat[rows, :], w[:, qw:], 1, 1)
        gain = gain + jnp.sum(part * a1[rows, :].astype(F32), axis=0, keepdims=True)
        put_quarter(d, part, keep, other, send)
    small[...] = jnp.zeros_like(small)
    small[0:1, :] = gain / gt[0:1, :]


def keyval_grad_kernel(rows, idx_ref, a1, nat, small, mine, theirs, grad):
    grad[...] = dg(a1[...], nat[...], 0, 0).astype(BF16)
    by_parity(rows, idx_ref[0] % 2, grad, mine, theirs, small)


def input_grad_kernel(x, gt, grad_mid, kept, got, last, out):
    h1 = three(kept, got, last)
    v = x[...].astype(F32)
    factor = lax.rsqrt(jnp.mean(v * v, axis=-1, keepdims=True) + NORM_EPS)
    normed = v * factor
    u = h1 * gt[0:1, :]
    out[...] = grad_mid[...] + factor * (
        u - normed * jnp.mean(u * normed, axis=-1, keepdims=True)
    )


def expert_unpack_kernel(ff, cut, first, rest, gateup, down):
    for e in range(E):
        gateup[e, :, 0, :] = first[e].astype(F32)
        gateup[e, :, 1, :] = rest[e, :, :ff].astype(F32)
        down[e] = rest[e, :, 2 * ff - cut :].astype(F32)


def route_slots(expert_ids):
    listed = jnp.concatenate([expert_ids[:, 0], expert_ids[:, 1]])
    onehot = (listed[:, None] == jnp.arange(E, dtype=jnp.int32)[None, :]).astype(jnp.int32)
    earlier = jnp.cumsum(onehot, axis=0) - onehot
    return jnp.sum(earlier * onehot, axis=1).reshape(2, -1)


def per_device(
    hidden_in,
    attn_gain,
    query_proj,
    key_value_projection,
    output_proj,
    moe_gain,
    router_proj,
    gateup_proj,
    down_proj,
    segment_index_list,
    expert_ids,
    out_grad,
):
    n_dp, n_tensor = lax.axis_size("dp"), lax.axis_size("tensor")
    own, width = hidden_in.shape
    span = own * n_tensor
    rows = query_proj.shape[0]
    qw = query_proj.shape[1]
    kvw = 2 * key_value_projection.shape[2]
    groups = 2 * qw // kvw
    ff = gateup_proj.shape[3]
    n_groups = n_dp // E
    dp_groups = None
    if n_groups > 1:
        dp_groups = [list(range(g * E, (g + 1) * E)) for g in range(n_groups)]
    dp, rank = lax.axis_index("dp"), lax.axis_index("tensor")
    idx = jnp.stack([dp, rank]).astype(jnp.int32)

    cols = qw + kvw
    early = jnp.concatenate(
        [query_proj, key_value_projection.reshape(rows, kvw), output_proj.T], axis=1
    )
    side = [attn_gain[None, :], moe_gain[None, :], jnp.zeros((6, rows), BF16), router_proj.T]
    side = jnp.pad(jnp.concatenate(side, axis=0), ((0, 0), (0, cols + qw - rows)))
    early = jnp.concatenate([early, side], axis=0)
    x_parts = [hidden_in, swap(hidden_in, "tensor", 1)]

    def slots_of(ids):
        position = route_slots(ids)
        per_rank = CAP // n_tensor
        local = position - rank * per_rank
        ids_t = ids.T
        slots = jnp.where(
            (local >= 0) & (local < per_rank) & (position < CAP), ids_t * SLOT + local, -1
        ).astype(jnp.int32)
        pad = jnp.zeros((4, span), jnp.int32)
        slot_rows = jnp.concatenate([slots, ids_t[::-1], pad], axis=0)
        return slot_rows, slots.T, lax.dynamic_slice_in_dim(ids, rank * own, own, 0)

    longest = segment_index_list.shape[0] // 4
    reach = min(SEQ_SPANS - 1, -(-(longest - 1) // span))
    n_pieces = reach + 1

    def keys_of(segments):
        padded = jnp.concatenate([jnp.full((reach * span,), -1, jnp.int32), segments])
        window = lax.dynamic_slice_in_dim(padded, dp * span, n_pieces * span, 0)
        seg_mine = window[reach * span :]
        valid = jnp.minimum(dp % SEQ_SPANS, reach)

        def bounds(keys, n_q, n_k, start):
            first_seg, last_seg = seg_mine[::n_q], seg_mine[n_q - 1 :: n_q]
            low = jnp.sum(keys[None, :] < first_seg[:, None], axis=1) // n_k
            full = -(-jnp.sum(keys[None, :] < last_seg[:, None], axis=1) // n_k)
            return jnp.stack([jnp.maximum(low, start), full]).astype(jnp.int32)

        earlier = window[: reach * span]
        meta = bounds(earlier, FAR_Q, FAR_K, (reach - valid) * (span // FAR_K))
        meta_own = bounds(seg_mine, BLK, BLK, 0)
        return meta, meta_own, seg_mine[None, :], seg_mine[:, None], earlier[:, None]

    def packed_of(gateup, down):
        return jnp.concatenate(
            [gateup[:, :, 0], gateup[:, :, 1], jnp.transpose(down, (0, 2, 1))], axis=2
        )

    made = {}

    def meanwhile(step, piece):
        if step == 1:
            made["slots"] = slots_of(expert_ids)
            return made["slots"]
        if step == 2:
            made["packed"] = packed_of(after(gateup_proj, piece), down_proj)
            return (made["packed"],)
        if step == 3:
            two = after(x_parts.pop(), piece)
            x_parts.extend([two, swap(two, "tensor", 1)])
            made["keys"] = keys_of(after(segment_index_list, piece))
            return made["keys"]
        return ()

    x_parts.append(swap(hidden_in, "tensor", 2))
    pieces, source = ring_gather(early, "dp", meanwhile)
    slot_rows, slot_cols, ids_own = made["slots"]
    meta, meta_own, qseg, kseg_own, kseg = made["keys"]
    packed = made["packed"]
    w_early, wo, gt, a1, qt, kv = kcall(
        "qkv",
        functools.partial(qkv_kernel, len(pieces), own, rows, qw, cols),
        [
            sds((width, cols), BF16),
            sds((width, qw), BF16),
            sds((16, width), F32),
            sds((span, width), BF16),
            sds((qw, span), BF16),
            sds((span, kvw), BF16),
        ],
        [source, idx],
        pieces + x_parts,
        [
            pltpu.VMEM((span, width), BF16),
            pltpu.VMEM((span, qw), F32),
            pltpu.VMEM((n_dp, 16, rows), F32),
        ],
    )

    def dispatch(parts, with_ids):
        (tiles_,) = kcall(
            "dispatch",
            functools.partial(dispatch_kernel, own, with_ids),
            [sds((E * SLOT, width), BF16)],
            [idx],
            [slot_rows] + parts,
            [pltpu.VMEM((span, width), BF16), pltpu.VMEM((E * SLOT, span), BF16)],
        )
        return tiles_

    half = kvw // 2
    far = [shifted(kv, "dp", d) for d in range(1, n_pieces)]
    acc, top, total = kcall(
        "attend_own",
        functools.partial(attend_kernel, 1, groups, True),
        [sds((qw, span), F32), sds((8, span), F32), sds((8, span), F32)],
        [meta_own],
        [qt, qseg, kseg_own, kv],
        [pltpu.VMEM((span, half), BF16), pltpu.VMEM((half, span), BF16)],
    )

    g_in = after(out_grad, qt)
    g_core, g_across = swap(g_in, "tensor", 1), swap(g_in, "tensor", 2)
    far[-1] = after(far[-1], acc, g_across)
    near = exchange(after(packed, qt), dp_groups)
    w_expert = near.reshape(E * rows, 3 * ff)
    if n_groups > 1:
        shape = (n_groups, E * rows, 3 * ff)
        whole = jnp.zeros(shape, BF16)
        for h in range(n_groups):
            part = w_expert if h == 0 else swap(near.reshape(E * rows, 3 * ff), "dp", h * E)
            whole = lax.dynamic_update_index_in_dim(whole, part, (dp // E) ^ h, 0)
        w_expert = whole.reshape(width, 3 * ff)
    w_core = swap(w_expert, "tensor", 1)

    att, lse, low = kcall(
        "attend_far",
        functools.partial(attend_kernel, reach, groups, False),
        [sds((qw, span), F32), sds((8, span), F32), sds((span, qw), BF16)],
        [meta],
        [qt, qseg, kseg] + far + [acc, top, total],
        [pltpu.VMEM((reach * span, half), BF16), pltpu.VMEM((half, reach * span), BF16)],
    )
    def quarters(wide):
        return [sds((own, wide), BF16), sds((own, wide), BF16), sds((2, own, wide), BF16)]

    keep, other, send = kcall(
        "project",
        functools.partial(project_kernel, own),
        quarters(width),
        [idx],
        [low, wo],
    )
    mid_terms, across = scatter_tensor(keep, other, send)
    middle, a2 = kcall(
        "middle",
        middle_kernel,
        [sds((own, width), F32), sds((own, width), BF16)],
        [],
        [hidden_in, gt] + mid_terms,
    )

    g_parts = [out_grad, g_core, g_across, after(swap(g_across, "tensor", 1), across)]
    g_slots = exchange(after(dispatch(g_parts, True), w_expert), dp_groups)
    a2_parts = gather_tensor(a2)
    w_across = swap(after(w_expert, a2_parts[2]), "tensor", 2)
    w_parts = [w_expert, w_core, w_across, swap(w_across, "tensor", 1)]
    x_slots = exchange(after(dispatch(a2_parts, False), g_slots), dp_groups)
    n_slots = E * SLOT
    s_slots, hid, slot_weight, dx = kcall(
        "expert",
        functools.partial(expert_kernel, ff),
        [
            sds((n_slots, width), BF16),
            sds((4, n_slots, 3 * ff), BF16),
            sds((n_slots, 1), F32),
            sds((n_slots, width), BF16),
        ],
        [idx],
        [x_slots, g_slots, gt],
        [
            pltpu.VMEM((n_slots, width), F32),
            pltpu.VMEM((n_slots, 1), F32),
            pltpu.VMEM((4, width, 3 * ff), BF16),
            pltpu.SemaphoreType.DMA((4,)),
        ],
        hbm=w_parts,
    )
    cut = ff

    def expert_grad(first):
        return kcall(
            "expert_grad",
            functools.partial(expert_grad_kernel, ff, cut, first),
            [sds((width, cut if first else 3 * ff - cut), BF16)] * 4,
            [],
            [x_slots, s_slots, hid],
        )

    dx_back = exchange(dx, dp_groups)
    keep_a, near_a, other_a, far_a = expert_grad(True)
    keep_b, near_b, other_b, far_b = expert_grad(False)
    (out_slots,) = kcall(
        "expert_out",
        functools.partial(expert_out_kernel, ff),
        [sds((n_slots, width), BF16)],
        [],
        [hid, slot_weight] + w_parts,
        [pltpu.VMEM((n_slots, width), F32)],
    )
    second_a = (other_a.astype(F32) + swap(far_a, "tensor", 1).astype(F32)).astype(BF16)
    second_b = (other_b.astype(F32) + swap(far_b, "tensor", 1).astype(F32)).astype(BF16)
    got_a, got_b = swap(near_a, "tensor", 1), swap(near_b, "tensor", 1)
    last_a = swap(second_a, "tensor", 2)
    dx_back = after(dx_back, keep_a, keep_b, out_slots)

    def combine(parts_, with_q, *others):
        wide = width + (EXTRA if with_q else 0)
        keep, other, send = kcall(
            "combine" if with_q else "combine_out",
            functools.partial(combine_kernel, own, with_q),
            quarters(wide),
            [idx],
            [slot_cols, parts_],
            [pltpu.VMEM((E * SLOT, wide), BF16)],
        )
        return scatter_tensor(keep, other, after(send, *others) if others else send)

    def expert_total(kept, got, last):
        total = (kept.astype(F32) + got.astype(F32) + last.astype(F32)).astype(BF16)
        if n_groups > 1:
            group = dp // E
            blocks = total.reshape(n_groups, E * rows, -1)
            total = lax.dynamic_index_in_dim(blocks, group, 0, keepdims=False).astype(F32)
            for h in range(1, n_groups):
                there = lax.dynamic_index_in_dim(blocks, group ^ h, 0, keepdims=False)
                total = total + swap(there, "dp", h * E).astype(F32)
            total = total.astype(BF16)
        return total.reshape(E, rows, -1)

    back_terms, across = combine(dx_back, True, last_a)
    total_a = expert_total(keep_a, got_a, last_a)
    back_terms[0] = after(back_terms[0], second_b, total_a)
    out_back = exchange(after(out_slots, across), dp_groups)
    grad_middle, branch, small_two = kcall(
        "middle_back",
        middle_back_kernel,
        [sds((own, width), F32), sds((own, width), BF16), sds((16, width), F32)],
        [],
        [middle, a2, out_grad, ids_own, gt] + back_terms,
    )
    branch_parts = gather_tensor(branch)
    last_b = swap(after(second_b, branch_parts[2]), "tensor", 2)

    heads = qw // HEAD
    g_heads, delta, mine, theirs = kcall(
        "branch",
        functools.partial(branch_kernel, own, rows, heads),
        [
            sds((qw, span), BF16),
            sds((8, span), F32),
            sds((n_dp // 2 * (rows + 16), qw), BF16),
            sds((n_dp // 2 * (rows + 16), qw), BF16),
        ],
        [idx],
        branch_parts + [att, low, wo, small_two],
        [pltpu.VMEM((span, width), BF16), pltpu.VMEM((width, qw), BF16)],
    )
    own_a = exchange(after(total_a, out_back, g_heads), dp_groups)
    pairs = [list(range(p, n_dp, 2)) for p in range(2)]

    def pair_sum(mine, theirs, *others):
        got = swap(theirs, "dp", 1)
        got = after(got, *others) if others else got
        return (mine.astype(F32) + got.astype(F32)).astype(BF16)

    def owner_sum(value, *others, late=()):
        parts = after(exchange(after(value, *others), pairs), *late)
        return jnp.sum(parts.reshape(n_dp // 2, -1, parts.shape[1]).astype(F32), axis=0)

    out_pair = pair_sum(mine, theirs)
    outs = kcall(
        "attend_back_far",
        functools.partial(attend_back_kernel, reach, groups, False),
        [sds((qw, span), F32)] + [sds((kvw, span), BF16)] * reach,
        [meta],
        [qt, g_heads, lse, delta, qseg, kseg] + far,
        [
            pltpu.VMEM((reach * span, half), BF16),
            pltpu.VMEM((reach * span, half), BF16),
            pltpu.VMEM((half, reach * span), BF16),
            pltpu.VMEM((kvw, reach * span), F32),
        ],
    )
    dkv_far = [shifted(outs[d], "dp", -d) for d in range(1, n_pieces)]
    dq, dkv_own = kcall(
        "attend_back_own",
        functools.partial(attend_back_kernel, 1, groups, True),
        [sds((qw, span), BF16), sds((kvw, span), F32)],
        [meta_own],
        [qt, g_heads, lse, delta, qseg, kseg_own, kv, after(outs[0], own_a)],
        [
            pltpu.VMEM((span, half), BF16),
            pltpu.VMEM((span, half), BF16),
            pltpu.VMEM((half, span), BF16),
        ],
    )
    out_sum = owner_sum(out_pair, own_a)
    total_b = expert_total(keep_b, got_b, after(last_b, dq))
    own_b = exchange(after(total_b, out_sum, *dkv_far), dp_groups)

    nat_q, mine, theirs = kcall(
        "query_grad",
        functools.partial(query_grad_kernel, rows),
        [
            sds((span, qw), BF16),
            sds((width // 2, qw), BF16),
            sds((width // 2, qw), BF16),
        ],
        [idx],
        [after(dq, out_sum, *dkv_far), a1],
        [pltpu.VMEM((width, qw), BF16)],
    )
    q_sum = owner_sum(pair_sum(mine, theirs), own_b)
    keep_h, other_h, send_h, nat_kv, small_one = kcall(
        "input_back",
        functools.partial(input_back_kernel, n_pieces, own),
        quarters(width) + [sds((span, kvw), BF16), sds((16, width), F32)],
        [idx],
        [nat_q, w_early, a1, gt, dkv_own] + dkv_far,
    )
    in_terms, _ = scatter_tensor(keep_h, other_h, send_h)
    gain_sum = small_one + swap(small_one, "tensor", 1)
    gain_sum = gain_sum + swap(gain_sum, "tensor", 2)
    mine, theirs = kcall(
        "keyval_grad",
        functools.partial(keyval_grad_kernel, rows),
        [
            sds((n_dp // 2 * (rows + 8), kvw), BF16),
            sds((n_dp // 2 * (rows + 8), kvw), BF16),
        ],
        [idx],
        [a1, nat_kv, gain_sum],
        [pltpu.VMEM((width, kvw), BF16)],
    )
    (input_grad,) = kcall(
        "input_grad",
        input_grad_kernel,
        [sds((own, width), F32)],
        [],
        [hidden_in, gt, grad_middle] + in_terms,
    )

    out_terms, _ = combine(after(out_back, theirs), False)
    hidden_out = (
        middle + out_terms[0].astype(F32) + out_terms[1][0].astype(F32) + out_terms[2].astype(F32)
    ).astype(BF16)
    gateup_grad, down_grad = kcall(
        "expert_unpack",
        functools.partial(expert_unpack_kernel, ff, cut),
        [sds((E, rows, 2, ff), F32), sds((E, rows, ff), F32)],
        [],
        [own_a, own_b],
    )
    o_sum = out_sum[:rows].T
    side = out_sum[rows:, :rows]
    side = side + swap(side, "tensor", 1)
    side = side + swap(side, "tensor", 2)
    ready = (input_grad, hidden_out, gateup_grad, down_grad, q_sum, o_sum, side)
    kv_sum = owner_sum(pair_sum(mine, theirs, q_sum, gateup_grad), late=ready)
    return (
        hidden_out,
        input_grad,
        kv_sum[rows, :rows],
        q_sum,
        kv_sum[:rows].reshape(rows, 2, kvw // 2),
        o_sum,
        side[1],
        side[8:16].T,
        gateup_grad,
        jnp.transpose(down_grad, (0, 2, 1)),
    )


def solution(mesh):
    return jax.shard_map(
        per_device,
        mesh=mesh,
        in_specs=(
            P(("dp", "tensor"), None),
            P("dp"),
            P("dp", "tensor"),
            P("dp", None, "tensor"),
            P("tensor", "dp"),
            P("dp"),
            P("dp", None),
            P(None, "dp", None, "tensor"),
            P(None, "tensor", "dp"),
            P(),
            P("dp", None),
            P(("dp", "tensor"), None),
        ),
        out_specs=(
            P(("dp", "tensor"), None),
            P(("dp", "tensor"), None),
            P("dp"),
            P("dp", "tensor"),
            P("dp", None, "tensor"),
            P("tensor", "dp"),
            P("dp"),
            P("dp", None),
            P(None, "dp", None, "tensor"),
            P(None, "tensor", "dp"),
        ),
        check_vma=False,
    )
```

```python
import functools

import jax
import jax.numpy as jnp
from jax import lax
from jax.experimental import pallas as pl
from jax.experimental.pallas import tpu as pltpu
from jax.sharding import PartitionSpec as P

HEAD = 64
E = 8
SEQ_SPANS = 8
CAP = 240
SLOT = 64
BLK = 384
FAR_Q, FAR_K = 384, 384
EXTRA = 128

NORM_EPS = 1e-05
NEG = -1e30

F32 = jnp.float32
BF16 = jnp.bfloat16


def dg(a, b, ca, cb):
    return lax.dot_general(a, b, (((ca,), (cb,)), ((), ())), preferred_element_type=F32)


def sds(shape, dtype):
    return jax.ShapeDtypeStruct(shape, dtype)


TIMES = {
    "qkv": 7,
    "attend_own": 14,
    "attend_far": 20,
    "project": 4,
    "middle": 3,
    "dispatch": 4,
    "expert": 17,
    "expert_grad": 3,
    "expert_out": 3,
    "combine": 12,
    "combine_out": 1,
    "middle_back": 5,
    "branch": 6,
    "attend_back_far": 20,
    "attend_back_own": 14,
    "query_grad": 1,
    "input_back": 1,
    "keyval_grad": 1,
    "input_grad": 1,
    "expert_unpack": 1,
}


def kcall(name, body, outs, smem, vmem, scratch=(), hbm=(), limit=60):
    return pl.pallas_call(
        body,
        name=name,
        out_shape=list(outs),
        in_specs=[pl.BlockSpec(memory_space=pltpu.SMEM)] * len(smem)
        + [pl.BlockSpec(memory_space=pltpu.VMEM)] * len(vmem)
        + [pl.BlockSpec(memory_space=pl.ANY)] * len(hbm),
        out_specs=[pl.BlockSpec(memory_space=pltpu.VMEM)] * len(outs),
        scratch_shapes=list(scratch),
        compiler_params=pltpu.CompilerParams(vmem_limit_bytes=limit << 20),
        cost_estimate=pl.CostEstimate(
            flops=TIMES[name] * 10**9, bytes_accessed=10**6, transcendentals=0
        ),
    )(*smem, *vmem, *hbm)


def swap(value, axis, by):
    size = lax.axis_size(axis)
    return lax.ppermute(value, axis, [(i, i ^ by) for i in range(size)])


def shifted(value, axis, by):
    size = lax.axis_size(axis)
    return lax.ppermute(value, axis, [(i, i + by) for i in range(size) if 0 <= i + by < size])


def gather_tensor(value):
    one = swap(value, "tensor", 1)
    two = swap(value, "tensor", 2)
    return [value, one, two, swap(two, "tensor", 1)]


def scatter_tensor(keep, other, send):
    got = swap(send, "tensor", 1)
    second = (other.astype(F32) + got[1].astype(F32)).astype(BF16)
    return [keep, got, swap(second, "tensor", 2)], second


def three(kept, got, last):
    return kept[...].astype(F32) + got[0].astype(F32) + last[...].astype(F32)


def ring_pos(index, size):
    return jnp.where(index % 2 == 0, index // 2, size - 1 - (index - 1) // 2)


def ring_dev(pos, size):
    pos = pos % size
    return jnp.where(pos < size // 2, 2 * pos, 2 * (size - 1 - pos) + 1)


def ring_gather(value, axis, meanwhile):
    size = lax.axis_size(axis)
    order = list(range(0, size, 2)) + list(range(size - 1, 0, -2))
    ahead = [(order[k], order[(k + 1) % size]) for k in range(size)]
    back = [(b, a) for a, b in ahead]
    half = value.shape[0] // 16 * 8
    index = lax.axis_index(axis)
    pos = ring_pos(index, size)
    pieces, source = [value], [index]
    one = two = value
    for step in range(1, size // 2 + 1):
        last = step == size // 2
        got_one = lax.ppermute(one[:half] if last else one, axis, ahead)
        got_two = lax.ppermute(two[half:] if last else two, axis, back)
        done = meanwhile(step, one)
        one, two = (after(got_one, *done), got_two) if done else (got_one, got_two)
        pieces += [one, two]
        source += [ring_dev(pos - step, size), ring_dev(pos + step, size)]
    return pieces, jnp.stack(source).astype(jnp.int32)


def exchange(value, groups=None):
    return lax.all_to_all(
        value, "dp", split_axis=0, concat_axis=0, axis_index_groups=groups, tiled=True
    )


def after(value, *others):
    return lax.optimization_barrier((value,) + others)[0]


def qkv_kernel(n, own, rows, qw, cols, src_ref, idx_ref, *refs):
    pieces = refs[:n]
    xs = refs[n : n + 4]
    w, wo, gt, a1, qt, kv, xb, qn, gs = refs[n + 4 :]
    rank = idx_ref[1]
    for k in range(n):
        piece = pieces[k]
        first = pieces[n - 2].shape[0] if k == n - 1 else 0
        last = min(first + piece.shape[0], rows)
        at = pl.ds(pl.multiple_of(src_ref[k] * rows + first, 8), last - first)
        w[at, :] = piece[: last - first, :cols]
        wo[at, :] = piece[: last - first, cols:]
        if first + piece.shape[0] > rows:
            gs[pl.ds(src_ref[k], 1)] = piece[last - first :, :rows].astype(F32)[None]
    for d in range(4):
        xb[pl.ds(pl.multiple_of((rank ^ d) * own, 16), own), :] = xs[d][...]
    gt[...] = jnp.concatenate([gs[j] for j in range(gs.shape[0])], axis=1)

    def block(j, _):
        at = pl.ds(pl.multiple_of(j * own, 16), own)
        x = xb[at, :].astype(F32)
        factor = lax.rsqrt(jnp.mean(x * x, axis=-1, keepdims=True) + NORM_EPS)
        a = (x * factor * gt[0:1, :]).astype(BF16)
        a1[at, :] = a
        y = dg(a, w[...], 1, 0)
        qn[at, :] = y[:, :qw] * (HEAD**-0.5)
        kv[at, :] = y[:, qw:].astype(BF16)
        return 0

    lax.fori_loop(0, 4, block, 0)
    qt[...] = jnp.transpose(qn[...]).astype(BF16)


def tile_loop(meta_ref, qb, end, body, carry):
    low, full = meta_ref[0, qb], meta_ref[1, qb]
    carry = lax.fori_loop(low, jnp.minimum(full, end), lambda t, c: body(t, True, c), carry)
    return lax.fori_loop(jnp.maximum(full, low), end, lambda t, c: body(t, False, c), carry)


def allowed_mask(ks, diag, qseg, kseg):
    ok = kseg[ks, :] == qseg
    if diag:
        keys = lax.broadcasted_iota(jnp.int32, (BLK, BLK), 0)
        ok = ok & (keys <= lax.broadcasted_iota(jnp.int32, (BLK, BLK), 1))
    return ok


def attend_kernel(np_, groups, local, meta_ref, *refs):
    qt, qseg_ref, kseg = refs[:3]
    kvs = refs[3 : 3 + np_]
    if local:
        acc_ref, m_ref, l_ref, kb, vt = refs[3 + np_ :]
    else:
        acc_in, m_in, l_in, att, lse, low, kb, vt = refs[3 + np_ :]
    span = qt.shape[1]
    n_q, n_k = (BLK, BLK) if local else (FAR_Q, FAR_K)
    half = kb.shape[1]
    kv_heads = half // HEAD
    for d in range(np_):
        at = (np_ - 1 - d) * span
        kb[at : at + span, :] = kvs[d][:, :half]
        vt[:, at : at + span] = jnp.transpose(kvs[d][:, half:].astype(F32)).astype(BF16)

    def q_block(qb, _):
        qs = pl.ds(pl.multiple_of(qb * n_q, n_q), n_q)
        qseg = qseg_ref[:, qs]
        for n in range(kv_heads):
            heads = [n * groups + g for g in range(groups)]
            sl = [slice(h * HEAD, (h + 1) * HEAD) for h in heads]
            q = [qt[r, qs] for r in sl]

            def tile(t, masked, carry, diag=False):
                ks = pl.ds(pl.multiple_of(t * n_k, n_k), n_k)
                k = kb[ks, n * HEAD : (n + 1) * HEAD]
                v = vt[n * HEAD : (n + 1) * HEAD, ks]
                ok = allowed_mask(ks, diag, qseg, kseg) if masked else None
                out = []
                for g in range(groups):
                    m, l, acc = carry[g]
                    s = dg(k, q[g], 1, 0)
                    if masked:
                        s = jnp.where(ok, s, NEG)
                    m_new = jnp.maximum(m, jnp.max(s, axis=0, keepdims=True))
                    e = jnp.exp(s - m_new)
                    shrink = jnp.exp(m - m_new)
                    l = l * shrink + jnp.sum(e, axis=0, keepdims=True)
                    acc = acc * shrink + dg(v, e.astype(BF16), 1, 0)
                    out.append((m_new, l, acc))
                return tuple(out)

            if local:
                none = jnp.full((1, BLK), NEG, F32)
                init = (none, jnp.zeros((1, BLK), F32), jnp.zeros((HEAD, BLK), F32))
                state = tile(qb, True, (init,) * groups, True)
                state = tile_loop(meta_ref, qb, qb, tile, state)
                for g in range(groups):
                    h = heads[g]
                    m_ref[h : h + 1, qs], l_ref[h : h + 1, qs], acc_ref[sl[g], qs] = state[g]
            else:
                state = tuple(
                    (m_in[h : h + 1, qs], l_in[h : h + 1, qs], acc_in[r, qs])
                    for h, r in zip(heads, sl)
                )
                state = tile_loop(meta_ref, qb, np_ * (span // n_k), tile, state)
                for g in range(groups):
                    m, l, acc = state[g]
                    att[sl[g], qs] = acc / l
                    lse[heads[g] : heads[g] + 1, qs] = m + jnp.log(l)
        return 0

    lax.fori_loop(0, span // n_q, q_block, 0)
    if not local:
        low[...] = jnp.transpose(att[...]).astype(BF16)


def put_quarter(d, part, keep, other, send):
    if d % 2:
        send[d // 2] = part.astype(BF16)
    else:
        (other if d else keep)[...] = part.astype(BF16)


def project_kernel(own, idx_ref, low, wo, keep, other, send):
    rank = idx_ref[1]
    for d in range(4):
        rows = pl.ds(pl.multiple_of((rank ^ d) * own, 16), own)
        put_quarter(d, dg(low[rows, :], wo[...], 1, 1), keep, other, send)


def middle_kernel(x, gt, kept, got, last, middle, a2):
    mid = x[...].astype(F32) + three(kept, got, last)
    middle[...] = mid
    factor = lax.rsqrt(jnp.mean(mid * mid, axis=-1, keepdims=True) + NORM_EPS)
    a2[...] = (mid * factor * gt[1:2, :]).astype(BF16)


def select_tile(e, rows_ref, k=None):
    slot = e * SLOT + lax.broadcasted_iota(jnp.int32, (SLOT, rows_ref.shape[1]), 0)
    first, second = slot == rows_ref[0:1, :], slot == rows_ref[1:2, :]
    hit = (first | second) if k is None else (second if k else first)
    return jnp.where(hit, 1.0, 0.0).astype(BF16)


def dispatch_kernel(own, with_ids, idx_ref, rows_ref, *refs):
    xs, out = refs[:4], refs[4]
    xb, pick = refs[5:]
    rank = idx_ref[1]
    for d in range(4):
        xb[pl.ds(pl.multiple_of((rank ^ d) * own, 16), own), :] = xs[d][...]
    for e in range(E):
        pick[e * SLOT : (e + 1) * SLOT, :] = select_tile(e, rows_ref)
    width = 512
    for c in range(xb.shape[1] // width):
        lanes = slice(c * width, (c + 1) * width)
        y = dg(pick[...], xb[:, lanes], 1, 0)
        if not (with_ids and c == 0):
            out[:, lanes] = y.astype(BF16)
            continue
        ids = rows_ref[2:4, :].astype(F32).astype(BF16)
        for e in range(E):
            rows = slice(e * SLOT, (e + 1) * SLOT)
            row = dg(ids, select_tile(e, rows_ref, 0), 1, 1)[0:1]
            row = row + dg(ids, select_tile(e, rows_ref, 1), 1, 1)[1:2]
            row = jnp.concatenate([row, jnp.zeros((1, width - SLOT), F32)], axis=1)
            at = lax.broadcasted_iota(jnp.int32, (SLOT, width), 0)
            out[rows, lanes] = jnp.where(at == SLOT - 4, row, y[rows]).astype(BF16)


def eye():
    shape = (SLOT, SLOT)
    return lax.broadcasted_iota(jnp.int32, shape, 0) == lax.broadcasted_iota(jnp.int32, shape, 1)


def row_to_col(row):
    return jnp.sum(jnp.where(eye(), row, 0.0), axis=1, keepdims=True)


def col_to_row(col):
    return jnp.sum(jnp.where(eye(), col, 0.0), axis=0, keepdims=True)


def split_three(value):
    one = value.astype(BF16).astype(F32)
    two = (value - one).astype(BF16).astype(F32)
    return one, two, (value - one - two).astype(BF16).astype(F32)


def expert_kernel(ff, idx_ref, x_ref, gs, gt, w0, w1, w2, w3, so, ho, wo, dxo, dx, qs, wb, sems):
    index = idx_ref[0] % E
    ws = (w0, w1, w2, w3)
    for f in range(4):
        pltpu.make_async_copy(ws[f], wb.at[f], sems.at[f]).start()
    x = x_ref[...]
    logits = dg(x, gt[8:16, :].astype(BF16), 1, 1)
    lane = lax.broadcasted_iota(jnp.int32, (SLOT, E), 1)
    weights = []
    for d in range(E):
        rows = slice(d * SLOT, (d + 1) * SLOT)
        part = logits[rows]
        side = gs[(d + 1) * SLOT - 8 : (d + 1) * SLOT, 0:SLOT].astype(F32)
        other = row_to_col(side[4:5]).astype(jnp.int32)
        mine = jnp.sum(jnp.where(lane == index, part, 0.0), axis=1, keepdims=True)
        theirs = jnp.sum(jnp.where(lane == other, part, 0.0), axis=1, keepdims=True)
        weight = 1.0 / (1.0 + jnp.exp(theirs - mine))
        real = lax.broadcasted_iota(jnp.int32, (SLOT, 1), 0) < SLOT - 4
        weight = jnp.where(real, weight, 0.0)
        weights.append(weight)
        so[rows, :] = jnp.where(real, weight * gs[rows, :].astype(F32), 0.0).astype(BF16)
    wo[...] = jnp.concatenate(weights, axis=0)
    qs[...] = jnp.zeros_like(qs)
    dx[...] = jnp.zeros_like(dx)

    def hidden_slice(f, _):
        pltpu.make_async_copy(w0, wb.at[f], sems.at[f]).wait()
        gate = dg(x_ref[...], wb[f, :, :ff], 1, 0)
        up = dg(x_ref[...], wb[f, :, ff : 2 * ff], 1, 0)
        hidden = dg(so[...], wb[f, :, 2 * ff :], 1, 0)
        sig = 1.0 / (1.0 + jnp.exp(-gate))
        act = gate * sig * up
        qs[...] += jnp.sum(hidden * act, axis=1, keepdims=True)
        ho[f, :, :ff] = (hidden * up * sig * (1.0 + gate * (1.0 - sig))).astype(BF16)
        ho[f, :, ff : 2 * ff] = (hidden * gate * sig).astype(BF16)
        ho[f, :, 2 * ff :] = act.astype(BF16)
        dx[...] += dg(ho[f, :, : 2 * ff], wb[f, :, : 2 * ff], 1, 1)
        return 0

    lax.fori_loop(0, 4, hidden_slice, 0)
    q = qs[...]
    dxo[...] = dx[...].astype(BF16)
    for d in range(E):
        rows = slice(d * SLOT, (d + 1) * SLOT)
        head = dx[rows, 0:128]
        at = lax.broadcasted_iota(jnp.int32, head.shape, 0)
        row = jnp.concatenate([col_to_row(q[rows]), jnp.zeros((1, 128 - SLOT), F32)], axis=1)
        for k, term in enumerate(split_three(row)):
            head = jnp.where(at == SLOT - 4 + k, term, head)
        dxo[rows, 0:128] = head.astype(BF16)


def expert_grad_kernel(ff, cut, first, x, s, h, *outs):
    for f in range(4):
        out = outs[f]
        if first:
            out[...] = dg(x[...], h[f, :, :cut], 0, 0).astype(BF16)
        else:
            out[:, : 2 * ff - cut] = dg(x[...], h[f, :, cut : 2 * ff], 0, 0).astype(BF16)
            out[:, 2 * ff - cut :] = dg(s[...], h[f, :, 2 * ff :], 0, 0).astype(BF16)


def expert_out_kernel(ff, h, weight, w0, w1, w2, w3, out, acc):
    for f, w in enumerate((w0, w1, w2, w3)):
        part = dg(h[f, :, 2 * ff :], w[:, 2 * ff :], 1, 1)
        acc[...] = part if f == 0 else acc[...] + part
    out[...] = (acc[...] * weight[...]).astype(BF16)


def combine_kernel(own, with_q, idx_ref, cols, parts, keep, other, send, y):
    rank = idx_ref[1]
    width = parts.shape[1]
    y[:, :width] = parts[...]
    if with_q:
        for e in range(E):
            rows = slice(e * SLOT, (e + 1) * SLOT)
            tail = parts[(e + 1) * SLOT - 8 : (e + 1) * SLOT, 0:SLOT].astype(F32)
            lane = lax.broadcasted_iota(jnp.int32, (SLOT, EXTRA), 1)
            side = jnp.zeros((SLOT, EXTRA), F32)
            for k in range(3):
                side = jnp.where(lane == e + 8 * k, row_to_col(tail[4 + k : 5 + k]), side)
            y[rows, width:] = side.astype(BF16)
    slot = lax.broadcasted_iota(jnp.int32, (own, E * SLOT), 1)
    for d in range(4):
        at = pl.ds(pl.multiple_of((rank ^ d) * own, 16), own)
        hit = (cols[at, 0:1] == slot) | (cols[at, 1:2] == slot)
        part = dg(jnp.where(hit, 1.0, 0.0).astype(BF16), y[...], 1, 0)
        put_quarter(d, part, keep, other, send)


def middle_back_kernel(mid_ref, a2, g, ids, gt, kept, got, last, grad_mid, branch, small):
    width = mid_ref.shape[1]
    total = three(kept, got, last)
    h2, side = total[:, :width], total[:, width:]
    own = h2.shape[0]
    logits = dg(a2[...], gt[8:16, :].astype(BF16), 1, 1)
    lane = lax.broadcasted_iota(jnp.int32, (own, E), 1)
    q = side[:, 0:8] + side[:, 8:16] + side[:, 16:24]
    hit = [lane == ids[:, k : k + 1] for k in range(2)]
    logit = [jnp.sum(jnp.where(hit[k], logits, 0.0), axis=1, keepdims=True) for k in range(2)]
    terms = [jnp.sum(jnp.where(hit[k], q, 0.0), axis=1, keepdims=True) for k in range(2)]
    both = terms[0] + terms[1]
    logit_grad = jnp.zeros((own, E), F32)
    for k in range(2):
        weight = 1.0 / (1.0 + jnp.exp(logit[1 - k] - logit[k]))
        logit_grad = jnp.where(hit[k], terms[k] - weight * both, logit_grad)
    high = logit_grad.astype(BF16)
    rest = (logit_grad - high.astype(F32)).astype(BF16)
    router = gt[8:16, :].astype(BF16)
    h2 = h2 + dg(high, router, 1, 0) + dg(rest, router, 1, 0)
    mid = mid_ref[...]
    factor = lax.rsqrt(jnp.mean(mid * mid, axis=-1, keepdims=True) + NORM_EPS)
    normed = mid * factor
    u = h2 * gt[1:2, :]
    back = g[...].astype(F32) + factor * (
        u - normed * jnp.mean(u * normed, axis=-1, keepdims=True)
    )
    grad_mid[...] = back
    branch[...] = back.astype(BF16)
    small[...] = jnp.zeros_like(small)
    small[1:2, :] = jnp.sum(h2 * normed, axis=0, keepdims=True)
    small[8:16, :] = dg(high, a2[...], 0, 0) + dg(rest, a2[...], 0, 0)


def branch_kernel(own, rows, heads, idx_ref, *refs):
    bs = refs[:4]
    att, low, wo, small = refs[4:8]
    gt, delta, mine, theirs, full, grad = refs[8:]
    rank = idx_ref[1]
    qw = wo.shape[1]
    for d in range(4):
        full[pl.ds(pl.multiple_of((rank ^ d) * own, 16), own), :] = bs[d][...]
    gt[...] = dg(wo[...], full[...], 0, 1).astype(BF16)
    for h in range(heads):
        at = slice(h * HEAD, (h + 1) * HEAD)
        delta[h : h + 1, :] = jnp.sum(gt[at, :].astype(F32) * att[at, :], axis=0, keepdims=True)
    grad[...] = dg(full[...], low[...], 0, 0).astype(BF16)
    by_parity(rows, idx_ref[0] % 2, grad, mine, theirs, small)


def by_parity(rows, parity, grad, mine, theirs, side=None):
    n = grad.shape[0] // rows
    block = mine.shape[0] * 2 // n
    for k in range(n // 2):
        for out, p in ((mine, parity), (theirs, 1 - parity)):
            at = pl.ds(pl.multiple_of((2 * k + p) * rows, 8), rows)
            out[k * block : k * block + rows, :] = grad[at, :]
        if side is not None:
            tail = slice(k * block + rows, (k + 1) * block)
            pad = jnp.zeros((block - rows, grad.shape[1] - rows), F32)
            even, odd = [
                jnp.concatenate([side[: block - rows, j * rows : (j + 1) * rows], pad], axis=1)
                for j in (2 * k, 2 * k + 1)
            ]
            mine[tail, :] = jnp.where(parity == 0, even, odd).astype(BF16)
            theirs[tail, :] = jnp.where(parity == 0, odd, even).astype(BF16)


def attend_back_kernel(np_, groups, local, meta_ref, *refs):
    qt, gt, lse, delta, qseg_ref, kseg = refs[:6]
    kvs = refs[6 : 6 + np_]
    refs = refs[6 + np_ :]
    if local:
        dq_in, dq, dkv, kb, vb, kt = refs
    else:
        dq = refs[0]
        dkvs = refs[1 : 1 + np_]
        kb, vb, kt, dkv = refs[1 + np_ :]
    span = qt.shape[1]
    n_q, n_k = (BLK, BLK) if local else (FAR_Q, FAR_K)
    half = kb.shape[1]
    kv_heads = half // HEAD
    for d in range(np_):
        at = (np_ - 1 - d) * span
        kb[at : at + span, :] = kvs[d][:, :half]
        vb[at : at + span, :] = kvs[d][:, half:]
        kt[:, at : at + span] = jnp.transpose(kvs[d][:, :half].astype(F32)).astype(BF16)
    dkv[...] = jnp.zeros_like(dkv)

    def q_block(qb, _):
        qs = pl.ds(pl.multiple_of(qb * n_q, n_q), n_q)
        qseg = qseg_ref[:, qs]
        for n in range(kv_heads):
            heads = [n * groups + g for g in range(groups)]
            sl = [slice(h * HEAD, (h + 1) * HEAD) for h in heads]
            q = [qt[r, qs] for r in sl]
            go = [gt[r, qs] for r in sl]
            ls = [lse[h : h + 1, qs] for h in heads]
            de = [delta[h : h + 1, qs] for h in heads]

            def tile(t, masked, carry, diag=False):
                ks = pl.ds(pl.multiple_of(t * n_k, n_k), n_k)
                lanes = slice(n * HEAD, (n + 1) * HEAD)
                k, v, k_t = kb[ks, lanes], vb[ks, lanes], kt[lanes, ks]
                ok = allowed_mask(ks, diag, qseg, kseg) if masked else None
                out = []
                dk = dv = None
                for g in range(groups):
                    p = jnp.exp(dg(k, q[g], 1, 0) - ls[g])
                    if masked:
                        p = jnp.where(ok, p, 0.0)
                    ds = (p * (dg(v, go[g], 1, 0) - de[g])).astype(BF16)
                    one = dg(q[g], ds, 1, 1)
                    two = dg(go[g], p.astype(BF16), 1, 1)
                    dk = one if dk is None else dk + one
                    dv = two if dv is None else dv + two
                    out.append(carry[g] + dg(k_t, ds, 1, 0))
                dkv[n * HEAD : (n + 1) * HEAD, ks] += dk
                dkv[half + n * HEAD : half + (n + 1) * HEAD, ks] += dv
                return tuple(out)

            if local:
                state = tile(qb, True, tuple(dq_in[r, qs] for r in sl), True)
                state = tile_loop(meta_ref, qb, qb, tile, state)
                for g in range(groups):
                    dq[sl[g], qs] = (state[g] * (HEAD**-0.5)).astype(BF16)
            else:
                state = tuple(jnp.zeros((HEAD, n_q), F32) for _ in range(groups))
                state = tile_loop(meta_ref, qb, np_ * (span // n_k), tile, state)
                for g in range(groups):
                    dq[sl[g], qs] = state[g]
        return 0

    lax.fori_loop(0, span // n_q, q_block, 0)
    if not local:
        for d in range(np_):
            at = (np_ - 1 - d) * span
            dkvs[d][...] = dkv[:, at : at + span].astype(BF16)


def query_grad_kernel(rows, idx_ref, dq, a1, nat, mine, theirs, grad):
    nat[...] = jnp.transpose(dq[...].astype(F32)).astype(BF16)
    grad[...] = dg(a1[...], nat[...], 0, 0).astype(BF16)
    by_parity(rows, idx_ref[0] % 2, grad, mine, theirs)


def input_back_kernel(np_, own, idx_ref, *refs):
    nat_q, w, a1, gt = refs[:4]
    dkvs = refs[4 : 4 + np_]
    keep, other, send, nat, small = refs[4 + np_ :]
    rank = idx_ref[1]
    total = dkvs[0][...]
    for d in range(1, np_):
        total = total + dkvs[d][...].astype(F32)
    qw = nat_q.shape[1]
    nat[...] = jnp.transpose(total).astype(BF16)
    gain = jnp.zeros((1, w.shape[0]), F32)
    for d in range(4):
        rows = pl.ds(pl.multiple_of((rank ^ d) * own, 16), own)
        part = dg(nat_q[rows, :], w[:, :qw], 1, 1) + dg(nat[rows, :], w[:, qw:], 1, 1)
        gain = gain + jnp.sum(part * a1[rows, :].astype(F32), axis=0, keepdims=True)
        put_quarter(d, part, keep, other, send)
    small[...] = jnp.zeros_like(small)
    small[0:1, :] = gain / gt[0:1, :]


def keyval_grad_kernel(rows, idx_ref, a1, nat, small, mine, theirs, grad):
    grad[...] = dg(a1[...], nat[...], 0, 0).astype(BF16)
    by_parity(rows, idx_ref[0] % 2, grad, mine, theirs, small)


def input_grad_kernel(x, gt, grad_mid, kept, got, last, out):
    h1 = three(kept, got, last)
    v = x[...].astype(F32)
    factor = lax.rsqrt(jnp.mean(v * v, axis=-1, keepdims=True) + NORM_EPS)
    normed = v * factor
    u = h1 * gt[0:1, :]
    out[...] = grad_mid[...] + factor * (
        u - normed * jnp.mean(u * normed, axis=-1, keepdims=True)
    )


def expert_unpack_kernel(ff, cut, first, rest, gateup, down):
    for e in range(E):
        gateup[e, :, 0, :] = first[e].astype(F32)
        gateup[e, :, 1, :] = rest[e, :, :ff].astype(F32)
        down[e] = rest[e, :, 2 * ff - cut :].astype(F32)


def route_slots(expert_ids):
    listed = jnp.concatenate([expert_ids[:, 0], expert_ids[:, 1]])
    onehot = (listed[:, None] == jnp.arange(E, dtype=jnp.int32)[None, :]).astype(jnp.int32)
    earlier = jnp.cumsum(onehot, axis=0) - onehot
    return jnp.sum(earlier * onehot, axis=1).reshape(2, -1)


def per_device(
    hidden_in,
    attn_gain,
    query_proj,
    key_value_projection,
    output_proj,
    moe_gain,
    router_proj,
    gateup_proj,
    down_proj,
    segment_index_list,
    expert_ids,
    out_grad,
):
    n_dp, n_tensor = lax.axis_size("dp"), lax.axis_size("tensor")
    own, width = hidden_in.shape
    span = own * n_tensor
    rows = query_proj.shape[0]
    qw = query_proj.shape[1]
    kvw = 2 * key_value_projection.shape[2]
    groups = 2 * qw // kvw
    ff = gateup_proj.shape[3]
    n_groups = n_dp // E
    dp_groups = None
    if n_groups > 1:
        dp_groups = [list(range(g * E, (g + 1) * E)) for g in range(n_groups)]
    dp, rank = lax.axis_index("dp"), lax.axis_index("tensor")
    idx = jnp.stack([dp, rank]).astype(jnp.int32)

    cols = qw + kvw
    early = jnp.concatenate(
        [query_proj, key_value_projection.reshape(rows, kvw), output_proj.T], axis=1
    )
    side = [attn_gain[None, :], moe_gain[None, :], jnp.zeros((6, rows), BF16), router_proj.T]
    side = jnp.pad(jnp.concatenate(side, axis=0), ((0, 0), (0, cols + qw - rows)))
    early = jnp.concatenate([early, side], axis=0)
    x_parts = [hidden_in, swap(hidden_in, "tensor", 1)]

    def slots_of(ids):
        position = route_slots(ids)
        per_rank = CAP // n_tensor
        local = position - rank * per_rank
        ids_t = ids.T
        slots = jnp.where(
            (local >= 0) & (local < per_rank) & (position < CAP), ids_t * SLOT + local, -1
        ).astype(jnp.int32)
        pad = jnp.zeros((4, span), jnp.int32)
        slot_rows = jnp.concatenate([slots, ids_t[::-1], pad], axis=0)
        return slot_rows, slots.T, lax.dynamic_slice_in_dim(ids, rank * own, own, 0)

    longest = segment_index_list.shape[0] // 4
    reach = min(SEQ_SPANS - 1, -(-(longest - 1) // span))
    n_pieces = reach + 1

    def keys_of(segments):
        padded = jnp.concatenate([jnp.full((reach * span,), -1, jnp.int32), segments])
        window = lax.dynamic_slice_in_dim(padded, dp * span, n_pieces * span, 0)
        seg_mine = window[reach * span :]
        valid = jnp.minimum(dp % SEQ_SPANS, reach)

        def bounds(keys, n_q, n_k, start):
            first_seg, last_seg = seg_mine[::n_q], seg_mine[n_q - 1 :: n_q]
            low = jnp.sum(keys[None, :] < first_seg[:, None], axis=1) // n_k
            full = -(-jnp.sum(keys[None, :] < last_seg[:, None], axis=1) // n_k)
            return jnp.stack([jnp.maximum(low, start), full]).astype(jnp.int32)

        earlier = window[: reach * span]
        meta = bounds(earlier, FAR_Q, FAR_K, (reach - valid) * (span // FAR_K))
        meta_own = bounds(seg_mine, BLK, BLK, 0)
        return meta, meta_own, seg_mine[None, :], seg_mine[:, None], earlier[:, None]

    def packed_of(gateup, down):
        return jnp.concatenate(
            [gateup[:, :, 0], gateup[:, :, 1], jnp.transpose(down, (0, 2, 1))], axis=2
        )

    made = {}

    def meanwhile(step, piece):
        if step == 1:
            made["slots"] = slots_of(expert_ids)
            return made["slots"]
        if step == 2:
            made["packed"] = packed_of(after(gateup_proj, piece), down_proj)
            return (made["packed"],)
        if step == 3:
            two = after(x_parts.pop(), piece)
            x_parts.extend([two, swap(two, "tensor", 1)])
            made["keys"] = keys_of(after(segment_index_list, piece))
            return made["keys"]
        return ()

    x_parts.append(swap(hidden_in, "tensor", 2))
    pieces, source = ring_gather(early, "dp", meanwhile)
    slot_rows, slot_cols, ids_own = made["slots"]
    meta, meta_own, qseg, kseg_own, kseg = made["keys"]
    packed = made["packed"]
    w_early, wo, gt, a1, qt, kv = kcall(
        "qkv",
        functools.partial(qkv_kernel, len(pieces), own, rows, qw, cols),
        [
            sds((width, cols), BF16),
            sds((width, qw), BF16),
            sds((16, width), F32),
            sds((span, width), BF16),
            sds((qw, span), BF16),
            sds((span, kvw), BF16),
        ],
        [source, idx],
        pieces + x_parts,
        [
            pltpu.VMEM((span, width), BF16),
            pltpu.VMEM((span, qw), F32),
            pltpu.VMEM((n_dp, 16, rows), F32),
        ],
    )

    def dispatch(parts, with_ids):
        (tiles_,) = kcall(
            "dispatch",
            functools.partial(dispatch_kernel, own, with_ids),
            [sds((E * SLOT, width), BF16)],
            [idx],
            [slot_rows] + parts,
            [pltpu.VMEM((span, width), BF16), pltpu.VMEM((E * SLOT, span), BF16)],
        )
        return tiles_

    half = kvw // 2
    far = [shifted(kv, "dp", d) for d in range(1, n_pieces)]
    acc, top, total = kcall(
        "attend_own",
        functools.partial(attend_kernel, 1, groups, True),
        [sds((qw, span), F32), sds((8, span), F32), sds((8, span), F32)],
        [meta_own],
        [qt, qseg, kseg_own, kv],
        [pltpu.VMEM((span, half), BF16), pltpu.VMEM((half, span), BF16)],
    )

    g_in = after(out_grad, qt)
    g_core, g_across = swap(g_in, "tensor", 1), swap(g_in, "tensor", 2)
    far[-1] = after(far[-1], acc, g_across)
    near = exchange(after(packed, qt), dp_groups)
    w_expert = near.reshape(E * rows, 3 * ff)
    if n_groups > 1:
        shape = (n_groups, E * rows, 3 * ff)
        whole = jnp.zeros(shape, BF16)
        for h in range(n_groups):
            part = w_expert if h == 0 else swap(near.reshape(E * rows, 3 * ff), "dp", h * E)
            whole = lax.dynamic_update_index_in_dim(whole, part, (dp // E) ^ h, 0)
        w_expert = whole.reshape(width, 3 * ff)
    w_core = swap(w_expert, "tensor", 1)

    att, lse, low = kcall(
        "attend_far",
        functools.partial(attend_kernel, reach, groups, False),
        [sds((qw, span), F32), sds((8, span), F32), sds((span, qw), BF16)],
        [meta],
        [qt, qseg, kseg] + far + [acc, top, total],
        [pltpu.VMEM((reach * span, half), BF16), pltpu.VMEM((half, reach * span), BF16)],
    )
    def quarters(wide):
        return [sds((own, wide), BF16), sds((own, wide), BF16), sds((2, own, wide), BF16)]

    keep, other, send = kcall(
        "project",
        functools.partial(project_kernel, own),
        quarters(width),
        [idx],
        [low, wo],
    )
    mid_terms, across = scatter_tensor(keep, other, send)
    middle, a2 = kcall(
        "middle",
        middle_kernel,
        [sds((own, width), F32), sds((own, width), BF16)],
        [],
        [hidden_in, gt] + mid_terms,
    )

    g_parts = [out_grad, g_core, g_across, after(swap(g_across, "tensor", 1), across)]
    g_slots = exchange(after(dispatch(g_parts, True), w_expert), dp_groups)
    a2_parts = gather_tensor(a2)
    w_across = swap(after(w_expert, a2_parts[2]), "tensor", 2)
    w_parts = [w_expert, w_core, w_across, swap(w_across, "tensor", 1)]
    x_slots = exchange(after(dispatch(a2_parts, False), g_slots), dp_groups)
    n_slots = E * SLOT
    s_slots, hid, slot_weight, dx = kcall(
        "expert",
        functools.partial(expert_kernel, ff),
        [
            sds((n_slots, width), BF16),
            sds((4, n_slots, 3 * ff), BF16),
            sds((n_slots, 1), F32),
            sds((n_slots, width), BF16),
        ],
        [idx],
        [x_slots, g_slots, gt],
        [
            pltpu.VMEM((n_slots, width), F32),
            pltpu.VMEM((n_slots, 1), F32),
            pltpu.VMEM((4, width, 3 * ff), BF16),
            pltpu.SemaphoreType.DMA((4,)),
        ],
        hbm=w_parts,
    )
    cut = ff

    def expert_grad(first):
        return kcall(
            "expert_grad",
            functools.partial(expert_grad_kernel, ff, cut, first),
            [sds((width, cut if first else 3 * ff - cut), BF16)] * 4,
            [],
            [x_slots, s_slots, hid],
        )

    dx_back = exchange(dx, dp_groups)
    keep_a, near_a, other_a, far_a = expert_grad(True)
    keep_b, near_b, other_b, far_b = expert_grad(False)
    (out_slots,) = kcall(
        "expert_out",
        functools.partial(expert_out_kernel, ff),
        [sds((n_slots, width), BF16)],
        [],
        [hid, slot_weight] + w_parts,
        [pltpu.VMEM((n_slots, width), F32)],
    )
    second_a = (other_a.astype(F32) + swap(far_a, "tensor", 1).astype(F32)).astype(BF16)
    second_b = (other_b.astype(F32) + swap(far_b, "tensor", 1).astype(F32)).astype(BF16)
    got_a, got_b = swap(near_a, "tensor", 1), swap(near_b, "tensor", 1)
    last_a = swap(second_a, "tensor", 2)
    dx_back = after(dx_back, keep_a, keep_b, out_slots)

    def combine(parts_, with_q, *others):
        wide = width + (EXTRA if with_q else 0)
        keep, other, send = kcall(
            "combine" if with_q else "combine_out",
            functools.partial(combine_kernel, own, with_q),
            quarters(wide),
            [idx],
            [slot_cols, parts_],
            [pltpu.VMEM((E * SLOT, wide), BF16)],
        )
        return scatter_tensor(keep, other, after(send, *others) if others else send)

    def expert_total(kept, got, last):
        total = (kept.astype(F32) + got.astype(F32) + last.astype(F32)).astype(BF16)
        if n_groups > 1:
            group = dp // E
            blocks = total.reshape(n_groups, E * rows, -1)
            total = lax.dynamic_index_in_dim(blocks, group, 0, keepdims=False).astype(F32)
            for h in range(1, n_groups):
                there = lax.dynamic_index_in_dim(blocks, group ^ h, 0, keepdims=False)
                total = total + swap(there, "dp", h * E).astype(F32)
            total = total.astype(BF16)
        return total.reshape(E, rows, -1)

    back_terms, across = combine(dx_back, True, last_a)
    total_a = expert_total(keep_a, got_a, last_a)
    back_terms[0] = after(back_terms[0], second_b, total_a)
    out_back = exchange(after(out_slots, across), dp_groups)
    grad_middle, branch, small_two = kcall(
        "middle_back",
        middle_back_kernel,
        [sds((own, width), F32), sds((own, width), BF16), sds((16, width), F32)],
        [],
        [middle, a2, out_grad, ids_own, gt] + back_terms,
    )
    branch_parts = gather_tensor(branch)
    last_b = swap(after(second_b, branch_parts[2]), "tensor", 2)

    heads = qw // HEAD
    g_heads, delta, mine, theirs = kcall(
        "branch",
        functools.partial(branch_kernel, own, rows, heads),
        [
            sds((qw, span), BF16),
            sds((8, span), F32),
            sds((n_dp // 2 * (rows + 16), qw), BF16),
            sds((n_dp // 2 * (rows + 16), qw), BF16),
        ],
        [idx],
        branch_parts + [att, low, wo, small_two],
        [pltpu.VMEM((span, width), BF16), pltpu.VMEM((width, qw), BF16)],
    )
    own_a = exchange(after(total_a, out_back, g_heads), dp_groups)
    pairs = [list(range(p, n_dp, 2)) for p in range(2)]

    def pair_sum(mine, theirs, *others):
        got = swap(theirs, "dp", 1)
        got = after(got, *others) if others else got
        return (mine.astype(F32) + got.astype(F32)).astype(BF16)

    def owner_sum(value, *others, late=()):
        parts = after(exchange(after(value, *others), pairs), *late)
        return jnp.sum(parts.reshape(n_dp // 2, -1, parts.shape[1]).astype(F32), axis=0)

    out_pair = pair_sum(mine, theirs)
    outs = kcall(
        "attend_back_far",
        functools.partial(attend_back_kernel, reach, groups, False),
        [sds((qw, span), F32)] + [sds((kvw, span), BF16)] * reach,
        [meta],
        [qt, g_heads, lse, delta, qseg, kseg] + far,
        [
            pltpu.VMEM((reach * span, half), BF16),
            pltpu.VMEM((reach * span, half), BF16),
            pltpu.VMEM((half, reach * span), BF16),
            pltpu.VMEM((kvw, reach * span), F32),
        ],
    )
    dkv_far = [shifted(outs[d], "dp", -d) for d in range(1, n_pieces)]
    dq, dkv_own = kcall(
        "attend_back_own",
        functools.partial(attend_back_kernel, 1, groups, True),
        [sds((qw, span), BF16), sds((kvw, span), F32)],
        [meta_own],
        [qt, g_heads, lse, delta, qseg, kseg_own, kv, after(outs[0], own_a)],
        [
            pltpu.VMEM((span, half), BF16),
            pltpu.VMEM((span, half), BF16),
            pltpu.VMEM((half, span), BF16),
        ],
    )
    out_sum = owner_sum(out_pair, own_a)
    total_b = expert_total(keep_b, got_b, after(last_b, dq))
    own_b = exchange(after(total_b, out_sum, *dkv_far), dp_groups)

    nat_q, mine, theirs = kcall(
        "query_grad",
        functools.partial(query_grad_kernel, rows),
        [
            sds((span, qw), BF16),
            sds((width // 2, qw), BF16),
            sds((width // 2, qw), BF16),
        ],
        [idx],
        [after(dq, out_sum, *dkv_far), a1],
        [pltpu.VMEM((width, qw), BF16)],
    )
    q_sum = owner_sum(pair_sum(mine, theirs), own_b)
    keep_h, other_h, send_h, nat_kv, small_one = kcall(
        "input_back",
        functools.partial(input_back_kernel, n_pieces, own),
        quarters(width) + [sds((span, kvw), BF16), sds((16, width), F32)],
        [idx],
        [nat_q, w_early, a1, gt, dkv_own] + dkv_far,
    )
    in_terms, _ = scatter_tensor(keep_h, other_h, send_h)
    gain_sum = small_one + swap(small_one, "tensor", 1)
    gain_sum = gain_sum + swap(gain_sum, "tensor", 2)
    mine, theirs = kcall(
        "keyval_grad",
        functools.partial(keyval_grad_kernel, rows),
        [
            sds((n_dp // 2 * (rows + 8), kvw), BF16),
            sds((n_dp // 2 * (rows + 8), kvw), BF16),
        ],
        [idx],
        [a1, nat_kv, gain_sum],
        [pltpu.VMEM((width, kvw), BF16)],
    )
    (input_grad,) = kcall(
        "input_grad",
        input_grad_kernel,
        [sds((own, width), F32)],
        [],
        [hidden_in, gt, grad_middle] + in_terms,
    )

    out_terms, _ = combine(after(out_back, theirs), False)
    hidden_out = (
        middle + out_terms[0].astype(F32) + out_terms[1][0].astype(F32) + out_terms[2].astype(F32)
    ).astype(BF16)
    gateup_grad, down_grad = kcall(
        "expert_unpack",
        functools.partial(expert_unpack_kernel, ff, cut),
        [sds((E, rows, 2, ff), F32), sds((E, rows, ff), F32)],
        [],
        [own_a, own_b],
    )
    o_sum = out_sum[:rows].T
    side = out_sum[rows:, :rows]
    side = side + swap(side, "tensor", 1)
    side = side + swap(side, "tensor", 2)
    ready = (input_grad, hidden_out, gateup_grad, down_grad, q_sum, o_sum, side)
    kv_sum = owner_sum(pair_sum(mine, theirs, q_sum, gateup_grad), late=ready)
    return (
        hidden_out,
        input_grad,
        kv_sum[rows, :rows],
        q_sum,
        kv_sum[:rows].reshape(rows, 2, kvw // 2),
        o_sum,
        side[1],
        side[8:16].T,
        gateup_grad,
        jnp.transpose(down_grad, (0, 2, 1)),
    )


def solution(mesh):
    return jax.shard_map(
        per_device,
        mesh=mesh,
        in_specs=(
            P(("dp", "tensor"), None),
            P("dp"),
            P("dp", "tensor"),
            P("dp", None, "tensor"),
            P("tensor", "dp"),
            P("dp"),
            P("dp", None),
            P(None, "dp", None, "tensor"),
            P(None, "tensor", "dp"),
            P(),
            P("dp", None),
            P(("dp", "tensor"), None),
        ),
        out_specs=(
            P(("dp", "tensor"), None),
            P(("dp", "tensor"), None),
            P("dp"),
            P("dp", "tensor"),
            P("dp", None, "tensor"),
            P("tensor", "dp"),
            P("dp"),
            P("dp", None),
            P(None, "dp", None, "tensor"),
            P(None, "tensor", "dp"),
        ),
        check_vma=False,
    )
```
